32 devices in a mesh: groups: 2 (over y), ctx: 4 (over z), head: 2 (over x), rows: 2 (over core).
Axes of the slice: x: 2, y: 2, z: 4, core: 2. Of those that a mesh axis runs over, the one named last changes fastest.
Arguments:
- keys: bfloat16 [65536, 1024], P(('groups', 'ctx'), 'head'), parts along dimension 0, may hold values from -18 to 18
- values: bfloat16 [65536, 1024], P(('groups', 'ctx'), 'head'), parts along dimension 0, may hold values from -6 to 6
- window_q: bfloat16 [64, 8192], P(('groups', 'ctx'), 'head'), parts along dimension 0, may hold values from -6 to 6
- keep_stretches: int32 [16, 20], P(('groups', 'head')), parts along dimension 0, may hold values from 0 to 62, as said below
- dec_q: bfloat16 [128, 4, 8192], P('groups', None, 'head'), parts along dimension 0, may hold values from -6 to 6
- dec_k: bfloat16 [128, 4, 1024], P('groups', None, 'head'), parts along dimension 0, may hold values from -8 to 8
- dec_v: bfloat16 [128, 4, 1024], P('groups', None, 'head'), parts along dimension 0, may hold values from -6 to 6
- row_order: int32 [128], P('groups'), parts along dimension 0, may hold values from 0 to 63, each once
Outputs:
- stretch_scores: float32 [16, 64], P(('groups', 'head', 'rows'), 'ctx'), parts along dimension 0
- decoded: bfloat16 [128, 4, 8192], P(('groups', 'ctx', 'rows'), None, 'head'), parts along dimension 0
The draws below stay inside these ranges and needn't reach their ends.
There are 2 independent parts, one for each index of `groups`. The reference program is written for one: setup_inputs(seed, part) draws one part's arguments, and reference() takes and returns one part's arrays. A program takes and returns all parts, laid end to end along the dimension named above; each array names one. Nothing has to cross between parts.
Inputs may be any that keep to these rules, and one draw needn't show every extreme that they name: keep_stretches[k] lists 20 distinct stretch numbers of key-value head k in ascending order and never the last stretch; for every head some context shard has all 16 of its stretches listed.
All inputs are finite; a program needn't handle non-finite values.
Results may differ from the reference program's by a relative error of at most 0.0045.
Values may be sent and summed in bfloat16 or wider, within the bound.
No kernel may reach another device: no remote copies, remote signals or barrier semaphores. Data moves between devices by JAX's collectives and lax.ppermute only.
A program may use at most 128 MiB of HBM per device.

```python
import jax
import jax.numpy as jnp
from jax import lax

QH = 64
KVH = 8
HD = 128
STRETCH = 512
W = 32
ROWS = 64
STEPS = 4
CTX = 32768
CPD = 16
NCHUNK = 64
KEEP = 20
N_CTX = 4


def own_affinity():
    return (jnp.log(jnp.float32(KEEP * STRETCH + W)) + 4.0) / HD ** 0.5


def draw_keys(key, part):
    sample = 3.0 * jnp.clip(jax.random.normal(jax.random.fold_in(key, 1), (CTX, KVH * HD)), -6.0, 6.0)
    return sample.astype(jnp.bfloat16)


def draw_window_q(key, part):
    sample = jnp.clip(jax.random.normal(jax.random.fold_in(key, 21), (W, QH * HD)), -6.0, 6.0)
    return sample.astype(jnp.bfloat16)


def decode_common(key):
    shape = (ROWS, STEPS, KVH, HD)
    common = jnp.clip(jax.random.normal(jax.random.fold_in(key, 31), shape), -3.0, 3.0)
    return common


def draw_dec_q(key, part):
    common = decode_common(key)
    shape = (ROWS, STEPS, KVH, QH // KVH, HD)
    jitter = jax.random.normal(jax.random.fold_in(key, 35), shape)
    sample = jnp.clip(common[:, :, :, None, :] + 0.6 * jitter, -6.0, 6.0).reshape(ROWS, STEPS, QH * HD)
    return sample.astype(jnp.bfloat16)


def draw_dec_k(key, part):
    common = decode_common(key)
    shape = (ROWS, STEPS, KVH, HD)
    jitter = jax.random.normal(jax.random.fold_in(key, 36), shape)
    sample = jnp.clip(own_affinity() * common + 0.5 * jitter, -8.0, 8.0).reshape(ROWS, STEPS, KVH * HD)
    return sample.astype(jnp.bfloat16)


def draw_keep_stretches(key, part):
    full_shard = jax.random.randint(jax.random.fold_in(key, 301), (KVH,), 0, N_CTX - 1)
    levels = jax.random.randint(jax.random.fold_in(key, 302), (KVH, N_CTX), 0, 4)
    jitter = jax.random.randint(jax.random.fold_in(key, 303), (KVH, NCHUNK), 0, 1024)
    stretch_ids = jnp.arange(NCHUNK, dtype=jnp.int32)
    shard_ids = stretch_ids // CPD
    ranking = jitter + 1024 * levels[:, shard_ids]
    ranking = jnp.where(shard_ids[None, :] == full_shard[:, None], 1 << 20, ranking)
    ranking = jnp.where(stretch_ids[None, :] == NCHUNK - 1, -1, ranking)
    ranking = ranking * NCHUNK + stretch_ids[None, :]
    unused, chosen = lax.top_k(ranking, KEEP)
    return jnp.sort(chosen.astype(jnp.int32), axis=1)


def steps_of(key, extent, shards, low, largest):
    loudness, own = 1.0, jax.random.fold_in(key, 6)
    for axis_at, parts in shards:
        draws = jnp.exp(jax.random.uniform(jax.random.fold_in(own, axis_at), (parts,), jnp.float32, low / len(shards), largest / len(shards)))
        loudness = loudness * jnp.repeat(draws, extent[axis_at] // parts).reshape([-1 if axis == axis_at else 1 for axis in range(len(extent))])
    return loudness


def noise(rng, shape, scale, bound, shards=(), kind=jnp.bfloat16):
    level = steps_of(rng, shape, shards, -0.22, 0.18) if shards else 1.0
    drawn = jax.random.normal(rng, shape, jnp.float32) * scale * level
    return jnp.minimum(jnp.maximum(drawn, -bound), bound).astype(kind)


def setup_inputs(seed: int = 0, part: int = 0) -> dict:
    key_list = jax.random.split(jax.random.key(seed), 9)
    part_splits = jax.random.split(jax.random.fold_in(key_list[8], part), 9)
    keys = draw_keys(jax.random.fold_in(jax.random.fold_in(key_list[8], part), 71), part)
    values = noise(part_splits[1], (CTX, KVH * HD), 1.0, 6.0, ((0, 4), (1, 2)))
    window_q = draw_window_q(jax.random.fold_in(jax.random.fold_in(key_list[8], part), 71), part)
    keep_stretches = draw_keep_stretches(jax.random.fold_in(jax.random.fold_in(key_list[8], part), 71), part)
    dec_q = draw_dec_q(jax.random.fold_in(jax.random.fold_in(key_list[8], part), 71), part)
    dec_k = draw_dec_k(jax.random.fold_in(jax.random.fold_in(key_list[8], part), 71), part)
    dec_v = noise(part_splits[6], (ROWS, STEPS, KVH * HD), 1.0, 6.0, ((2, 2),))
    row_order = jax.random.permutation(part_splits[7], ROWS).astype(jnp.int32)
    return {"keys": keys, "values": values, "window_q": window_q, "keep_stretches": keep_stretches, "dec_q": dec_q, "dec_k": dec_k, "dec_v": dec_v, "row_order": row_order}


MASK_FILL = -1.0e30


def score_head(inputs):
    window_query, head_keys = inputs
    scores = jnp.einsum("whd,td->wht", window_query.astype(jnp.float32), head_keys.astype(jnp.float32)) * (HD ** -0.5)
    positions = jnp.arange(CTX, dtype=jnp.int32)
    reaches = CTX - W + jnp.arange(W, dtype=jnp.int32)
    allowed = (positions[None, :] <= reaches[:, None])[:, None, :]
    masked = jnp.where(allowed, scores, MASK_FILL)
    maxima = jnp.max(masked, axis=2, keepdims=True)
    weights = jnp.where(allowed, jnp.exp(masked - maxima), 0.0)
    probability = weights / jnp.sum(weights, axis=2, keepdims=True)
    return jnp.sum(probability, axis=(0, 1)).reshape(NCHUNK, STRETCH).sum(axis=1)


def decode_head(inputs):
    head_query, head_keys, head_values, keep_list, own_keys, own_values = inputs
    positions = (keep_list[:, None] * STRETCH + jnp.arange(STRETCH, dtype=jnp.int32)[None, :]).reshape(-1)
    positions = jnp.concatenate([positions.astype(jnp.int32), jnp.arange(CTX - W, CTX, dtype=jnp.int32)])
    kept_keys = head_keys[positions]
    kept_values = head_values[positions]
    causal = (jnp.arange(STEPS, dtype=jnp.int32)[None, :] <= jnp.arange(STEPS, dtype=jnp.int32)[:, None])[None, :, None, :]

    def one_block(block_data):
        queries, self_keys, self_values = block_data
        rows_block = queries.shape[0]
        group_size = queries.shape[2]
        flat_query = queries.reshape(-1, HD)
        ctx_scores = jnp.dot(flat_query, kept_keys.T, preferred_element_type=jnp.float32) * (HD ** -0.5)
        own_scores = jnp.einsum("rshd,rtd->rsht", queries.astype(jnp.float32), self_keys.astype(jnp.float32)) * (HD ** -0.5)
        own_masked = jnp.where(causal, own_scores, MASK_FILL)
        maxima = jnp.maximum(jnp.max(ctx_scores, axis=1), jnp.max(own_masked.reshape(-1, STEPS), axis=1))
        ctx_weights = jnp.exp(ctx_scores - maxima[:, None])
        own_weights = jnp.where(causal, jnp.exp(own_masked - maxima.reshape(rows_block, STEPS, group_size, 1)), 0.0)
        totals = jnp.sum(ctx_weights, axis=1) + jnp.sum(own_weights.reshape(-1, STEPS), axis=1)
        own_rounded = lax.optimization_barrier(own_weights.astype(jnp.bfloat16)).astype(jnp.float32)
        weighted = jnp.dot(ctx_weights.astype(jnp.bfloat16), kept_values, preferred_element_type=jnp.float32)
        weighted = weighted + jnp.einsum("rsht,rtd->rshd", own_rounded, self_values.astype(jnp.float32)).reshape(-1, HD)
        return (weighted / totals[:, None]).reshape(rows_block, STEPS, group_size, HD)

    group_size = head_query.shape[2]
    outputs = lax.map(one_block, (head_query.reshape(ROWS // 8, 8, STEPS, group_size, HD), own_keys.reshape(ROWS // 8, 8, STEPS, HD), own_values.reshape(ROWS // 8, 8, STEPS, HD)))
    return outputs.reshape(ROWS, STEPS, group_size, HD)


def reference(keys, values, window_q, keep_stretches, dec_q, dec_k, dec_v, row_order):
    group_size = QH // KVH
    key_heads = keys.reshape(CTX, KVH, HD).transpose(1, 0, 2)
    value_heads = values.reshape(CTX, KVH, HD).transpose(1, 0, 2)
    query_heads = window_q.reshape(W, KVH, group_size, HD).transpose(1, 0, 2, 3)
    stretch_scores = lax.map(score_head, (query_heads, key_heads))
    decode_query = dec_q.reshape(ROWS, STEPS, KVH, group_size, HD).transpose(2, 0, 1, 3, 4)
    own_keys = dec_k.reshape(ROWS, STEPS, KVH, HD).transpose(2, 0, 1, 3)
    own_values = dec_v.reshape(ROWS, STEPS, KVH, HD).transpose(2, 0, 1, 3)
    outputs = lax.map(decode_head, (decode_query, key_heads, value_heads, keep_stretches, own_keys, own_values))
    outputs = outputs.transpose(1, 2, 0, 3, 4).reshape(ROWS, STEPS, QH * HD)
    decoded = outputs[row_order.astype(jnp.int32)].astype(jnp.bfloat16)
    return stretch_scores, decoded
```

```python
import functools
import math

import jax
import jax.numpy as jnp
from jax import lax
from jax.experimental import pallas as pl
from jax.experimental.pallas import tpu as pltpu
from jax.sharding import PartitionSpec as P

QH = 64
KVH = 8
HD = 128
STRETCH = 512
W = 32
GROUP = QH // KVH

FILL = -1.0e30
SCALE2 = HD ** (-0.5) * math.log2(math.e)
NT = (((1,), (1,)), ((), ()))


def lanes_of(column):
    rows = []
    step = min(128, column.shape[0])
    for at in range(0, column.shape[0], step):
        block = column[at : at + step]
        eye = lax.broadcasted_iota(jnp.int32, block.shape, 0) == lax.broadcasted_iota(
            jnp.int32, block.shape, 1
        )
        rows.append(jnp.sum(jnp.where(eye, block, 0.0), axis=0, keepdims=True))
    return rows


def decode_kernel(
    heads,
    ctx_count,
    row_count,
    keep_ref,
    order_ref,
    place_ref,
    q_hbm,
    k_hbm,
    v_hbm,
    own_k_hbm,
    own_v_hbm,
    *rest,
):
    outs = rest[:ctx_count]
    (q_buf, k_buf, v_buf, kx_buf, vx_buf, m_ref, l_ref, acc_ref, q_sem, k_sem, v_sem, x_sem) = rest[
        ctx_count:
    ]
    keep_count = keep_ref.shape[1]
    here = k_hbm.shape[0] // STRETCH
    own_index = place_ref[0]
    row_index = place_ref[1]
    is_last = own_index == ctx_count - 1
    base = own_index * here
    rows_total = q_hbm.shape[0]
    rows_each = rows_total // (ctx_count * row_count)
    per_row = q_hbm.shape[2]
    local_rows = rows_each * ctx_count
    queries = local_rows * per_row
    chunk = min(256, queries)
    steps = own_k_hbm.shape[1] // rows_total
    own_keys = own_k_hbm.shape[1]

    def row_at(j):
        k = j // rows_each
        i = lax.rem(j, rows_each)
        dest = lax.rem(own_index + k, ctx_count)
        return order_ref[dest * (row_count * rows_each) + row_index * rows_each + i]

    def q_copy(j, row):
        return pltpu.make_async_copy(
            q_hbm.at[row, pl.ds(heads[0], len(heads))], q_buf.at[:, j], q_sem.at[j]
        )

    for j in range(local_rows):
        q_copy(j, row_at(j)).start()

    starts, counts = [], []
    for h in heads:
        start = jnp.int32(0)
        count = jnp.int32(0)
        for i in range(keep_count):
            local = keep_ref[h, i] - base
            start = start + (local < 0).astype(jnp.int32)
            count = count + ((local >= 0) & (local < here)).astype(jnp.int32)
        starts.append(start)
        counts.append(count)

    def unit_copies(at, u, h):
        local = keep_ref[h, starts[at] + u] - base
        rows = pl.ds(pl.multiple_of(local * STRETCH, STRETCH), STRETCH)
        cols = pl.ds(h * HD, HD)
        slot = at * here + u
        return (
            pltpu.make_async_copy(k_hbm.at[rows, cols], k_buf.at[slot], k_sem.at[slot]),
            pltpu.make_async_copy(v_hbm.at[rows, cols], v_buf.at[slot], v_sem.at[slot]),
        )

    def extra_copies(at, h):
        tail = pl.ds(k_hbm.shape[0] - W, W)
        cols = pl.ds(h * HD, HD)
        return (
            pltpu.make_async_copy(own_k_hbm.at[h], kx_buf.at[at, pl.ds(0, own_keys)], x_sem.at[at, 0]),
            pltpu.make_async_copy(own_v_hbm.at[h], vx_buf.at[at, pl.ds(0, own_keys)], x_sem.at[at, 1]),
            pltpu.make_async_copy(k_hbm.at[tail, cols], kx_buf.at[at, pl.ds(own_keys, W)], x_sem.at[at, 2]),
            pltpu.make_async_copy(v_hbm.at[tail, cols], vx_buf.at[at, pl.ds(own_keys, W)], x_sem.at[at, 3]),
        )

    for at, h in enumerate(heads):

        @pl.loop(0, counts[at])
        def _(u):
            for copy in unit_copies(at, u, h):
                copy.start()

    @pl.when(is_last)
    def _():
        rest_rows = kx_buf.shape[1] - own_keys - W
        for at, h in enumerate(heads):
            kx_buf[at, pl.ds(own_keys + W, rest_rows)] = jnp.zeros((rest_rows, HD), jnp.bfloat16)
            vx_buf[at, pl.ds(own_keys + W, rest_rows)] = jnp.zeros((rest_rows, HD), jnp.bfloat16)
            for copy in extra_copies(at, h):
                copy.start()

    for j in range(local_rows):
        q_copy(j, 0).wait()

    def fold(at, first, keys, values, mask):
        sl = pl.ds(first, chunk)
        j0 = first // per_row
        q = q_buf[at, j0 : j0 + chunk // per_row].reshape(chunk, HD)
        s = lax.dot_general(q, keys, NT, preferred_element_type=jnp.float32) * SCALE2
        if mask is not None:
            s = jnp.where(mask, s, FILL)
        m_old = m_ref[sl]
        m_new = jnp.maximum(m_old, jnp.max(s, axis=1, keepdims=True))
        alpha = jnp.exp2(m_old - m_new)
        total = None
        parts = []
        for c in range(0, s.shape[1], HD):
            p = jnp.exp2(s[:, c : c + HD] - m_new)
            if mask is not None:
                p = jnp.where(mask[:, c : c + HD], p, 0.0)
            total = p if total is None else total + p
            parts.append(p.astype(jnp.bfloat16))
        p = jnp.concatenate(parts, axis=1)
        l_ref[sl] = l_ref[sl] * alpha + total
        acc_ref[sl] = acc_ref[sl] * alpha + jnp.dot(p, values, preferred_element_type=jnp.float32)
        m_ref[sl] = m_new

    for at, h in enumerate(heads):
        m_ref[...] = jnp.full(m_ref.shape, FILL, jnp.float32)
        l_ref[...] = jnp.zeros(l_ref.shape, jnp.float32)
        acc_ref[...] = jnp.zeros(acc_ref.shape, jnp.float32)

        @pl.loop(0, counts[at])
        def _(u):
            slot = at * here + u
            for copy in unit_copies(at, u, h):
                copy.wait()
            for first in range(0, queries, chunk):
                fold(at, first, k_buf[slot], v_buf[slot], None)

        @pl.when(is_last)
        def _():
            for copy in extra_copies(at, h):
                copy.wait()
            width = kx_buf.shape[1]
            lane = lax.broadcasted_iota(jnp.int32, (per_row, width), 1)
            q_step = lax.rem(lax.broadcasted_iota(jnp.int32, (per_row, width), 0), steps)
            causal = (lax.rem(lane, steps) <= q_step) & (lane < own_keys)
            window = (lane >= own_keys) & (lane < own_keys + W)
            key_row = lane // steps
            for first in range(0, queries, chunk):
                masks = []
                for j in range(first // per_row, (first + chunk) // per_row):
                    masks.append(jnp.where((causal & (key_row == row_at(j))) | window, 1.0, 0.0))
                mask = jnp.concatenate(masks, axis=0) > 0.5
                fold(at, first, kx_buf[at], vx_buf[at], mask)

        per_dest = queries // ctx_count
        for k in range(ctx_count):
            sl = pl.ds(k * per_dest, per_dest)
            total = jnp.sum(l_ref[sl], axis=1, keepdims=True)
            some = total > 0.0
            out = acc_ref[sl] / jnp.where(some, total, 1.0)
            lse = jnp.where(some, m_ref[sl] + jnp.log2(jnp.where(some, total, 1.0)), FILL)
            outs[k][at, pl.ds(0, per_dest)] = out.astype(jnp.bfloat16)
            lines = lanes_of(lse)
            n = len(lines)
            high = [x.astype(jnp.bfloat16).astype(jnp.float32) for x in lines]
            mid = [(x - y).astype(jnp.bfloat16).astype(jnp.float32) for x, y in zip(lines, high)]
            low = [x - y - z for x, y, z in zip(lines, high, mid)]
            block = jnp.concatenate(
                high + mid + low + [jnp.zeros((16 - 3 * n, HD), jnp.float32)], axis=0
            )
            outs[k][at, pl.ds(per_dest, 16)] = block.astype(jnp.bfloat16)


def decode(heads, ctx_count, row_count, keep, order, place, q, keys, values, own_k, own_v):
    rows_total, _, per_row, _ = q.shape
    local_rows = rows_total // row_count
    queries = local_rows * per_row
    per_dest = queries // ctx_count
    here = keys.shape[0] // STRETCH
    width = pl.cdiv(own_k.shape[1] + W, HD) * HD
    n = len(heads)
    slots = n * here
    any_space = pl.BlockSpec(memory_space=pl.ANY)
    return pl.pallas_call(
        functools.partial(decode_kernel, heads, ctx_count, row_count),
        out_shape=[jax.ShapeDtypeStruct((n, per_dest + 16, HD), jnp.bfloat16)] * ctx_count,
        grid_spec=pltpu.PrefetchScalarGridSpec(
            num_scalar_prefetch=3,
            grid=(),
            in_specs=[any_space] * 5,
            out_specs=[pl.BlockSpec(memory_space=pltpu.VMEM)] * ctx_count,
            scratch_shapes=[
                pltpu.VMEM((n, local_rows, per_row, HD), jnp.bfloat16),
                pltpu.VMEM((slots, STRETCH, HD), jnp.bfloat16),
                pltpu.VMEM((slots, STRETCH, HD), jnp.bfloat16),
                pltpu.VMEM((n, width, HD), jnp.bfloat16),
                pltpu.VMEM((n, width, HD), jnp.bfloat16),
                pltpu.VMEM((queries, HD), jnp.float32),
                pltpu.VMEM((queries, HD), jnp.float32),
                pltpu.VMEM((queries, HD), jnp.float32),
                pltpu.SemaphoreType.DMA((local_rows,)),
                pltpu.SemaphoreType.DMA((slots,)),
                pltpu.SemaphoreType.DMA((slots,)),
                pltpu.SemaphoreType.DMA((n, 4)),
            ],
        ),
        cost_estimate=pl.CostEstimate(
            flops=n * 8 * queries * STRETCH * HD * 4,
            bytes_accessed=n * 8 * STRETCH * HD * 4,
            transcendentals=n * 8 * queries * STRETCH,
        ),
        name="decode",
    )(keep, order, place, q, keys, values, own_k, own_v)


def window_kernel(ctx_count, place_ref, q_ref, k_ref, max_ref, sum_ref):
    block = pl.program_id(1)
    own_index = place_ref[0]
    q = q_ref[...].reshape(-1, HD)
    per_piece = q.shape[0] // ctx_count
    w_each = W // ctx_count
    count = k_ref.shape[0] // STRETCH
    last_block = (own_index == ctx_count - 1) & (block == pl.num_programs(1) - 1)
    row = lax.broadcasted_iota(jnp.int32, (W, q.shape[0]), 0)
    col = lax.broadcasted_iota(jnp.int32, (W, q.shape[0]), 1)
    w = (ctx_count - 1 - col // per_piece) * w_each + lax.rem(col, w_each)
    allowed = (row <= w) | jnp.logical_not(last_block)
    for c in range(count):
        keys = k_ref[pl.ds(c * STRETCH, STRETCH)]
        s = lax.dot_general(keys, q, NT, preferred_element_type=jnp.float32) * SCALE2
        if c == count - 1:
            s = jnp.concatenate([s[: STRETCH - W], jnp.where(allowed, s[STRETCH - W :], FILL)], axis=0)
        peak = jnp.max(s, axis=0, keepdims=True)
        max_ref[0, pl.ds(c, 1)] = peak
        sum_ref[0, pl.ds(c, 1)] = jnp.sum(jnp.exp2(s - peak), axis=0, keepdims=True)


def window(ctx_count, score_heads, place, pieces, keys):
    here = keys.shape[0] // STRETCH
    per_block = math.gcd(here, 8)
    queries = W * GROUP
    stats = jax.ShapeDtypeStruct((score_heads, here, queries), jnp.float32)
    return pl.pallas_call(
        functools.partial(window_kernel, ctx_count),
        out_shape=[stats, stats],
        grid_spec=pltpu.PrefetchScalarGridSpec(
            num_scalar_prefetch=1,
            grid=(score_heads, here // per_block),
            in_specs=[
                pl.BlockSpec(
                    (ctx_count, 1, queries // ctx_count, HD), lambda g, b, place: (0, g, 0, 0)
                ),
                pl.BlockSpec(
                    (per_block * STRETCH, HD), lambda g, b, place: (b, place[1] * score_heads + g)
                ),
            ],
            out_specs=[
                pl.BlockSpec((1, per_block, queries), lambda g, b, place: (g, b, 0)),
                pl.BlockSpec((1, per_block, queries), lambda g, b, place: (g, b, 0)),
            ],
        ),
        cost_estimate=pl.CostEstimate(
            flops=score_heads * queries * keys.shape[0] * HD * 2,
            bytes_accessed=score_heads * keys.shape[0] * HD * 2,
            transcendentals=score_heads * queries * keys.shape[0],
        ),
        name="window",
    )(place, pieces, keys)


def combine_kernel(ctx_count, groups, *refs):
    out_ref = refs[-1]
    for at_group, heads in enumerate(groups):
        parts = refs[at_group * ctx_count : (at_group + 1) * ctx_count]
        per_dest = parts[0].shape[1] - 16
        step = min(128, per_dest)
        n = per_dest // step
        for at, h in enumerate(heads):
            for b in range(n):
                lses = []
                for part in parts:
                    tail = part[at, pl.ds(per_dest, 16)].astype(jnp.float32)
                    line = tail[b : b + 1] + tail[n + b : n + b + 1] + tail[2 * n + b : 2 * n + b + 1]
                    lses.append(line)
                top = functools.reduce(jnp.maximum, lses)
                weights = [jnp.exp2(x - top) for x in lses]
                whole = functools.reduce(jnp.add, weights)
                total = None
                for part, weight in zip(parts, weights):
                    share = jnp.broadcast_to(weight / whole, (128, HD)).T[:step]
                    term = part[at, pl.ds(b * step, step)].astype(jnp.float32) * share
                    total = term if total is None else total + term
                per_row = GROUP * 4
                lines = step // per_row
                out_ref[pl.ds(b * lines, lines), h] = total.reshape(lines, per_row, HD).astype(
                    jnp.bfloat16
                )


def local(keys, values, window_q, keep_stretches, dec_q, dec_k, dec_v, row_order):
    ctx_count = lax.axis_size("ctx")
    row_count = lax.axis_size("rows")
    own_index = lax.axis_index("ctx")
    row_index = lax.axis_index("rows")
    place = jnp.stack([own_index, row_index]).astype(jnp.int32)
    heads = keys.shape[1] // HD
    rows_total, steps = dec_q.shape[:2]
    score_heads = heads // row_count
    shifts = range(1, ctx_count)

    def shifted(x, k):
        return lax.ppermute(x, "ctx", [(i, (i + k) % ctx_count) for i in range(ctx_count)])

    w_each = window_q.shape[0]
    window_tiles = window_q.reshape(w_each, heads * GROUP, HD).transpose(1, 0, 2)
    window_tiles = window_tiles.reshape(heads, GROUP * w_each, HD)
    mine = lax.dynamic_slice_in_dim(window_tiles, row_index * score_heads, score_heads, 0)
    pieces = jnp.stack([mine] + [shifted(mine, k) for k in shifts])

    q = dec_q.reshape(rows_total, steps, heads * GROUP, HD).transpose(0, 2, 1, 3)
    q = q.reshape(rows_total, heads, GROUP * steps, HD)
    own_k = dec_k.reshape(rows_total, steps, heads, HD).transpose(2, 0, 1, 3)
    own_k = own_k.reshape(heads, rows_total * steps, HD)
    own_v = dec_v.reshape(rows_total, steps, heads, HD).transpose(2, 0, 1, 3)
    own_v = own_v.reshape(heads, rows_total * steps, HD)

    groups = [tuple([h]) for h in range(heads)]
    operands = []
    for group in groups:
        parts = decode(
            group, ctx_count, row_count, keep_stretches, row_order, place, q, keys, values, own_k, own_v
        )
        operands += [parts[0]] + [shifted(parts[k], k) for k in shifts]

    peaks, sums = window(ctx_count, score_heads, place, pieces, keys)
    top = jnp.max(peaks, axis=1)
    total = jnp.sum(sums * jnp.exp2(peaks - top[:, None]), axis=1)
    stat = jnp.stack([top, total]).reshape(2, score_heads, ctx_count, -1)
    stats = [stat] + [jnp.roll(shifted(stat, k), k, axis=2) for k in shifts]
    tops = jnp.stack([x[0] for x in stats])
    peak = jnp.max(tops, axis=0)
    whole = sum(x[1] * jnp.exp2(x[0] - peak) for x in stats)
    peak, whole = peak.reshape(score_heads, -1), whole.reshape(score_heads, -1)
    stretch_scores = jnp.sum(sums * (jnp.exp2(peaks - peak[:, None]) / whole[:, None]), axis=2)

    rows_each = rows_total // (ctx_count * row_count)
    decoded = pl.pallas_call(
        functools.partial(combine_kernel, ctx_count, groups),
        out_shape=jax.ShapeDtypeStruct((rows_each, heads, GROUP * steps, HD), jnp.bfloat16),
        in_specs=[pl.BlockSpec(memory_space=pltpu.VMEM)] * len(operands),
        out_specs=pl.BlockSpec(memory_space=pltpu.VMEM),
        name="combine",
    )(*operands)
    decoded = decoded.reshape(rows_each, heads * GROUP, steps, HD).transpose(0, 2, 1, 3)
    return (stretch_scores, decoded.reshape(rows_each, steps, heads * GROUP * HD))


def solution(mesh):
    placed = (
        P(("groups", "ctx"), "head"),
        P(("groups", "ctx"), "head"),
        P(("groups", "ctx"), "head"),
        P(("groups", "head"), None),
        P("groups", None, "head"),
        P("groups", None, "head"),
        P("groups", None, "head"),
        P("groups"),
    )
    return jax.shard_map(
        local,
        mesh=mesh,
        in_specs=placed,
        out_specs=(
            P(("groups", "head", "rows"), "ctx"),
            P(("groups", "ctx", "rows"), None, "head"),
        ),
        check_vma=False,
    )
```

```python
import functools
import math

import jax
import jax.numpy as jnp
from jax import lax
from jax.experimental import pallas as pl
from jax.experimental.pallas import tpu as pltpu
from jax.sharding import PartitionSpec as P

QH = 64
KVH = 8
HD = 128
STRETCH = 512
W = 32
GROUP = QH // KVH

FILL = -1.0e30
LIMIT = 1.0e30
SCALE2 = HD ** (-0.5) * math.log2(math.e)
NT = (((1,), (1,)), ((), ()))
TAIL = 16
ONES = 16


def head_order(keep_ref, here):
    heads, keep_count = keep_ref.shape
    if heads != 4:
        return [jnp.int32(h) for h in range(heads)]
    full = [keep_ref[h, keep_count // 2] // here for h in range(heads)]

    def clash(a, b, c, d):
        return (full[a] == full[b]).astype(jnp.int32) + (full[c] == full[d]).astype(jnp.int32)

    c1, c2, c3 = clash(0, 1, 2, 3), clash(0, 2, 1, 3), clash(0, 3, 1, 2)
    mate = jnp.where((c1 <= c2) & (c1 <= c3), 1, jnp.where(c2 <= c3, 2, 3))
    return [jnp.int32(0), mate, jnp.where(mate == 1, 2, 1), jnp.where(mate == 3, 2, 3)]


def pick(options, at):
    value = options[-1]
    for i in range(len(options) - 2, -1, -1):
        value = jnp.where(at == i, options[i], value)
    return value


def decode_kernel(
    group,
    group_count,
    ctx_count,
    row_count,
    keep_ref,
    order_ref,
    q_hbm,
    k_hbm,
    v_hbm,
    own_k_hbm,
    own_v_hbm,
    after_ref,
    *rest,
):
    outs = rest[:ctx_count]
    (q_buf, k_buf, v_buf, kx_buf, vx_buf, m_ref, l_ref, acc_ref, s_buf, note, q_sem, k_sem, v_sem, x_sem) = rest[
        ctx_count:
    ]
    keep_count = keep_ref.shape[1]
    here = k_hbm.shape[0] // STRETCH
    own_index = lax.axis_index("ctx")
    row_index = lax.axis_index("rows")
    is_last = own_index == ctx_count - 1
    base = own_index * here
    rows_total, heads, per_row, _ = q_hbm.shape
    rows_each = rows_total // (ctx_count * row_count)
    local_rows = rows_each * ctx_count
    queries = local_rows * per_row
    chunk = min(256, queries)
    firsts = list(range(0, queries, chunk))
    own_keys = own_k_hbm.shape[0]
    steps = own_keys // (rows_total * heads)
    extra = kx_buf.shape[0]
    count_here = heads // group_count
    order = head_order(keep_ref, here)[group * count_here : (group + 1) * count_here]

    def row_at(j):
        k = j // rows_each
        i = lax.rem(j, rows_each)
        dest = lax.rem(own_index + k, ctx_count)
        return order_ref[dest * (row_count * rows_each) + row_index * rows_each + i]

    @pl.loop(0, local_rows)
    def _(j):
        row = row_at(j)
        for at in range(count_here):
            pltpu.make_async_copy(q_hbm.at[row, order[at]], q_buf.at[at, j], q_sem.at[at]).start()

    for at in range(count_here):
        start = jnp.int32(0)
        count = jnp.int32(0)
        for i in range(keep_count):
            local = keep_ref[order[at], i] - base
            start = start + (local < 0).astype(jnp.int32)
            count = count + ((local >= 0) & (local < here)).astype(jnp.int32)
        note[at, 0] = start
        note[at, 1] = count

    def unit_copies(at, h, u):
        local = keep_ref[h, note[at, 0] + u] - base
        rows = pl.ds(pl.multiple_of(local * STRETCH, STRETCH), STRETCH)
        cols = pl.ds(pl.multiple_of(h * HD, HD), HD)
        slot = at * here + u
        return (
            pltpu.make_async_copy(k_hbm.at[rows, cols], k_buf.at[slot], k_sem.at[slot]),
            pltpu.make_async_copy(v_hbm.at[rows, cols], v_buf.at[slot], v_sem.at[slot]),
        )

    def wait_slot(buf, sem, slot):
        pltpu.make_async_copy(buf.at[slot], buf.at[slot], sem.at[slot]).wait()

    for at in range(count_here):

        @pl.loop(0, note[at, 1])
        def _(u):
            for copy in unit_copies(at, order[at], u):
                copy.start()

    def own_copies():
        return (
            pltpu.make_async_copy(own_k_hbm, kx_buf.at[pl.ds(0, own_keys)], x_sem.at[0]),
            pltpu.make_async_copy(own_v_hbm, vx_buf.at[pl.ds(0, own_keys)], x_sem.at[1]),
        )

    def tail_copies(h):
        tail = pl.ds(k_hbm.shape[0] - W, W)
        cols = pl.ds(pl.multiple_of(h * HD, HD), HD)
        return (
            pltpu.make_async_copy(k_hbm.at[tail, cols], kx_buf.at[pl.ds(own_keys, W)], x_sem.at[2]),
            pltpu.make_async_copy(v_hbm.at[tail, cols], vx_buf.at[pl.ds(own_keys, W)], x_sem.at[3]),
        )

    @pl.when(is_last)
    def _():
        spare = extra - own_keys - W
        kx_buf[pl.ds(own_keys + W, spare)] = jnp.zeros((spare, HD), jnp.bfloat16)
        vx_buf[pl.ds(own_keys + W, spare)] = jnp.zeros((spare, HD), jnp.bfloat16)
        for copy in own_copies():
            copy.start()
        for copy in own_copies():
            copy.wait()

    def turned(v):
        return jnp.concatenate([v.T, jnp.ones((ONES, v.shape[0]), jnp.bfloat16)], axis=0)

    def fold(sl, vt, s):
        old = m_ref[:, sl]
        new = jnp.maximum(old, jnp.max(s, axis=0, keepdims=True))
        alpha = jnp.exp2(old - new)
        t = jnp.dot(vt, jnp.exp2(s - new).astype(jnp.bfloat16), preferred_element_type=jnp.float32)
        l_ref[:, sl] = l_ref[:, sl] * alpha + t[HD : HD + 8]
        acc_ref[:, sl] = acc_ref[:, sl] * alpha + t[:HD]
        m_ref[:, sl] = new

    @pl.loop(0, count_here)
    def _(at):
        h = pick(order, at)
        count = note[at, 1]
        pairs = count // 2
        slot0 = at * here

        @pl.when(is_last)
        def _():
            for copy in tail_copies(h):
                copy.start()

        pltpu.make_async_copy(q_buf.at[at], q_buf.at[at], q_sem.at[at]).wait()

        def q_of(first):
            j0 = first // per_row
            return q_buf[at, pl.ds(j0, chunk // per_row)].reshape(chunk, HD)

        def scores(keys, first):
            return lax.dot_general(keys, q_of(first), NT, preferred_element_type=jnp.float32)

        def pair(buf, b):
            return buf[pl.ds(slot0 + 2 * b, 2)].reshape(2 * STRETCH, HD)

        def fast(sl, vt, s):
            p = jnp.exp2(s * SCALE2 - m_ref[:, sl]).astype(jnp.bfloat16)
            t = jnp.dot(vt, p, preferred_element_type=jnp.float32)
            l_ref[:, sl] += t[HD : HD + 8]
            acc_ref[:, sl] += t[:HD]

        l_ref[...] = jnp.zeros(l_ref.shape, jnp.float32)
        acc_ref[...] = jnp.zeros(acc_ref.shape, jnp.float32)

        @pl.when(count == 0)
        def _():
            m_ref[...] = jnp.full(m_ref.shape, FILL, jnp.float32)

        @pl.when(count > 0)
        def _():
            wait_slot(k_buf, k_sem, slot0)
            for first in firsts:
                s = scores(k_buf[slot0, pl.ds(0, 128)], first)
                m_ref[:, pl.ds(first, chunk)] = jnp.max(s, axis=0, keepdims=True) * SCALE2

        @pl.when(pairs > 0)
        def _():
            wait_slot(k_buf, k_sem, slot0 + 1)
            s_buf[0] = scores(pair(k_buf, 0), firsts[0])

            @pl.loop(0, pairs)
            def _(b):
                more = b + 1 < pairs
                wait_slot(v_buf, v_sem, slot0 + 2 * b)
                wait_slot(v_buf, v_sem, slot0 + 2 * b + 1)

                @pl.when(more)
                def _():
                    wait_slot(k_buf, k_sem, slot0 + 2 * b + 2)
                    wait_slot(k_buf, k_sem, slot0 + 2 * b + 3)

                following = jnp.where(more, b + 1, b)
                vt = turned(pair(v_buf, b))
                for i, first in enumerate(firsts):
                    if i + 1 < len(firsts):
                        s_buf[(i + 1) % 2] = scores(pair(k_buf, b), firsts[i + 1])
                    else:
                        s_buf[(i + 1) % 2] = scores(pair(k_buf, following), firsts[0])
                    fast(pl.ds(first, chunk), vt, s_buf[i % 2])

        @pl.when(count > 2 * pairs)
        def _():
            slot = slot0 + 2 * pairs

            @pl.when(pairs > 0)
            def _():
                wait_slot(k_buf, k_sem, slot)

            wait_slot(v_buf, v_sem, slot)
            vt = turned(v_buf[slot])
            s = scores(k_buf[slot], firsts[0])
            for i, first in enumerate(firsts):
                ahead = scores(k_buf[slot], firsts[i + 1]) if i + 1 < len(firsts) else None
                fast(pl.ds(first, chunk), vt, s)
                s = ahead

        bad = jnp.max(jnp.where(l_ref[...] < LIMIT, 0.0, 1.0))

        @pl.when(bad > 0.0)
        def _():
            l_ref[...] = jnp.zeros(l_ref.shape, jnp.float32)
            acc_ref[...] = jnp.zeros(acc_ref.shape, jnp.float32)
            m_ref[...] = jnp.full(m_ref.shape, FILL, jnp.float32)

            @pl.loop(0, count)
            def _(u):
                vt = turned(v_buf[slot0 + u])
                for first in firsts:
                    fold(pl.ds(first, chunk), vt, scores(k_buf[slot0 + u], first) * SCALE2)

        @pl.when(is_last)
        def _():
            for copy in tail_copies(h):
                copy.wait()
            vt = turned(vx_buf[...])
            key = lax.broadcasted_iota(jnp.int32, (extra, chunk), 0)
            lane = lax.broadcasted_iota(jnp.int32, (1, chunk), 1)
            window = (key >= own_keys) & (key < own_keys + W)
            for first in firsts:
                line = jnp.zeros((1, chunk), jnp.int32)
                for j in range(chunk // per_row):
                    line = jnp.where(lane // per_row == j, row_at(first // per_row + j), line)
                low = line * (heads * steps) + h * steps
                high = low + lax.rem(lane, steps)
                mask = ((key >= low) & (key <= high)) | window
                s = scores(kx_buf[...], first) * SCALE2
                fold(pl.ds(first, chunk), vt, jnp.where(mask, s, FILL))

        total = l_ref[0:1]
        some = total > 0.0
        safe = jnp.where(some, total, 1.0)
        lse = jnp.where(some, m_ref[...] + jnp.log2(safe), FILL)
        inverse = 1.0 / safe
        per_dest = queries // ctx_count
        lines = max(1, per_dest // 128)
        for b in range(queries // 128):
            sl = slice(b * 128, (b + 1) * 128)
            block = (acc_ref[:, sl] * inverse[:, sl]).T.astype(jnp.bfloat16)
            step = min(128, per_dest)
            for piece in range(128 // step):
                at_row = b * 128 + piece * step
                outs[at_row // per_dest][at, pl.ds(at_row % per_dest, step)] = block[
                    piece * step : (piece + 1) * step
                ]
        for k in range(ctx_count):
            b0 = k * per_dest // 128
            lse_lines = [lse[:, (b0 + i) * 128 : (b0 + i + 1) * 128] for i in range(lines)]
            high = [x.astype(jnp.bfloat16).astype(jnp.float32) for x in lse_lines]
            mid = [(x - y).astype(jnp.bfloat16).astype(jnp.float32) for x, y in zip(lse_lines, high)]
            low = [x - y - z for x, y, z in zip(lse_lines, high, mid)]
            block = jnp.concatenate(
                high + mid + low + [jnp.zeros((TAIL - 3 * lines, HD), jnp.float32)], axis=0
            )
            outs[k][at, pl.ds(per_dest, TAIL)] = block.astype(jnp.bfloat16)


def decode(group, group_count, ctx_count, row_count, keep, order, q, keys, values, own_k, own_v, after):
    rows_total, heads, per_row, _ = q.shape
    local_rows = rows_total // row_count
    queries = local_rows * per_row
    chunk = min(256, queries)
    per_dest = queries // ctx_count
    here = keys.shape[0] // STRETCH
    extra = pl.cdiv(own_k.shape[0] + W, HD) * HD
    n = heads // group_count
    slots = n * here
    any_space = pl.BlockSpec(memory_space=pl.ANY)
    return pl.pallas_call(
        functools.partial(decode_kernel, group, group_count, ctx_count, row_count),
        out_shape=[jax.ShapeDtypeStruct((n, per_dest + TAIL, HD), jnp.bfloat16)] * ctx_count,
        grid_spec=pltpu.PrefetchScalarGridSpec(
            num_scalar_prefetch=2,
            grid=(),
            in_specs=[any_space] * 6,
            out_specs=[pl.BlockSpec(memory_space=pltpu.VMEM)] * ctx_count,
            scratch_shapes=[
                pltpu.VMEM((n, local_rows, per_row, HD), jnp.bfloat16),
                pltpu.VMEM((slots, STRETCH, HD), jnp.bfloat16),
                pltpu.VMEM((slots, STRETCH, HD), jnp.bfloat16),
                pltpu.VMEM((extra, HD), jnp.bfloat16),
                pltpu.VMEM((extra, HD), jnp.bfloat16),
                pltpu.VMEM((1, queries), jnp.float32),
                pltpu.VMEM((8, queries), jnp.float32),
                pltpu.VMEM((HD, queries), jnp.float32),
                pltpu.VMEM((2, 2 * STRETCH, chunk), jnp.float32),
                pltpu.SMEM((n, 2), jnp.int32),
                pltpu.SemaphoreType.DMA((n,)),
                pltpu.SemaphoreType.DMA((slots,)),
                pltpu.SemaphoreType.DMA((slots,)),
                pltpu.SemaphoreType.DMA((4,)),
            ],
        ),
        cost_estimate=pl.CostEstimate(
            flops=n * 8 * queries * STRETCH * HD * 4,
            bytes_accessed=n * 8 * STRETCH * HD * 4,
            transcendentals=n * 8 * queries * STRETCH,
        ),
        name="decode",
    )(keep, order, q, keys, values, own_k, own_v, after)


def window_kernel(ctx_count, score_heads, *refs):
    pieces = refs[:ctx_count]
    k_hbm, after_ref, max_ref, sum_ref, stat_ref, q_buf, k_buf, k_sem = refs[ctx_count:]
    own_index = lax.axis_index("ctx")
    row_index = lax.axis_index("rows")
    is_last = own_index == ctx_count - 1
    here = k_hbm.shape[0] // STRETCH
    span = 2 * STRETCH
    blocks = k_hbm.shape[0] // span
    per_piece = pieces[0].shape[1]
    queries = per_piece * ctx_count
    w_each = W // ctx_count
    for g in range(score_heads):
        cols = pl.ds(pl.multiple_of((row_index * score_heads + g) * HD, HD), HD)
        for b in range(blocks):
            pltpu.make_async_copy(
                k_hbm.at[pl.ds(b * span, span), cols], k_buf.at[g * blocks + b], k_sem.at[g * blocks + b]
            ).start()
    for k, piece in enumerate(pieces):
        source = lax.rem(own_index + (ctx_count - k), ctx_count)
        for g in range(score_heads):
            q_buf[g, source] = piece[row_index * score_heads + g]

    def scores(i):
        g = i // blocks
        q = q_buf[g].reshape(queries, HD)
        return lax.dot_general(k_buf[i], q, NT, preferred_element_type=jnp.float32) * SCALE2

    row = lax.broadcasted_iota(jnp.int32, (W, queries), 0)
    col = lax.broadcasted_iota(jnp.int32, (W, queries), 1)
    w = (col // per_piece) * w_each + lax.rem(col, w_each)
    allowed = (row <= w) | jnp.logical_not(is_last)

    def wait(i):
        pltpu.make_async_copy(k_buf.at[i], k_buf.at[i], k_sem.at[i]).wait()

    total = score_heads * blocks
    wait(0)
    s = scores(0)
    for i in range(total):
        if i + 1 < total:
            wait(i + 1)
            ahead = scores(i + 1)
        g, b = divmod(i, blocks)
        for half in range(2):
            part = s[half * STRETCH : (half + 1) * STRETCH]
            if b == blocks - 1 and half == 1:
                part = jnp.concatenate(
                    [part[: STRETCH - W], jnp.where(allowed, part[STRETCH - W :], FILL)], axis=0
                )
            peak = jnp.max(part, axis=0, keepdims=True)
            max_ref[g, pl.ds(2 * b + half, 1)] = peak
            sum_ref[g, pl.ds(2 * b + half, 1)] = jnp.sum(jnp.exp2(part - peak), axis=0, keepdims=True)
        s = ahead
    lines = []
    for g in range(score_heads):
        top = jnp.max(max_ref[g], axis=0, keepdims=True)
        lines += [top, jnp.sum(sum_ref[g] * jnp.exp2(max_ref[g] - top), axis=0, keepdims=True)]
    lines.append(jnp.zeros((stat_ref.shape[0] - len(lines), queries), jnp.float32))
    stat_ref[...] = jnp.concatenate(lines, axis=0)


def window(ctx_count, score_heads, pieces, keys, after):
    here = keys.shape[0] // STRETCH
    queries = W * GROUP
    stats = jax.ShapeDtypeStruct((score_heads, here, queries), jnp.float32)
    blocks = score_heads * here // 2
    vmem = pl.BlockSpec(memory_space=pltpu.VMEM)
    any_space = pl.BlockSpec(memory_space=pl.ANY)
    return pl.pallas_call(
        functools.partial(window_kernel, ctx_count, score_heads),
        out_shape=[stats, stats, jax.ShapeDtypeStruct((8, queries), jnp.float32)],
        in_specs=[vmem] * ctx_count + [any_space] * 2,
        out_specs=[vmem] * 3,
        scratch_shapes=[
            pltpu.VMEM((score_heads, ctx_count, queries // ctx_count, HD), jnp.bfloat16),
            pltpu.VMEM((blocks, 2 * STRETCH, HD), jnp.bfloat16),
            pltpu.SemaphoreType.DMA((blocks,)),
        ],
        cost_estimate=pl.CostEstimate(
            flops=score_heads * queries * keys.shape[0] * HD * 2,
            bytes_accessed=score_heads * keys.shape[0] * HD * 2,
            transcendentals=score_heads * queries * keys.shape[0],
        ),
        name="window",
    )(*pieces, keys, after)


def combine_kernel(ctx_count, group_count, here, score_heads, keep_ref, *refs):
    score_ref, out_ref = refs[-2:]
    parts = refs[: group_count * ctx_count]
    max_ref, sum_ref = refs[group_count * ctx_count : group_count * ctx_count + 2]
    stats = refs[group_count * ctx_count + 2 : -2]
    heads, per_row = out_ref.shape[1], out_ref.shape[2]
    order = head_order(keep_ref, here)
    n = heads // group_count
    per_dest = parts[0].shape[1] - TAIL
    step = min(128, per_dest)
    lines = max(1, per_dest // 128)
    for group in range(group_count):
        here_parts = parts[group * ctx_count : (group + 1) * ctx_count]
        for at in range(n):
            for b in range(per_dest // step):
                lses = []
                for k, part in enumerate(here_parts):
                    tail = part[at, pl.ds(per_dest, TAIL)].astype(jnp.float32)
                    line = (
                        tail[b : b + 1]
                        + tail[lines + b : lines + b + 1]
                        + tail[2 * lines + b : 2 * lines + b + 1]
                    )
                    off = k * per_dest % 128
                    lses.append(jnp.broadcast_to(line, (128, HD)).T[off : off + step])
                top = functools.reduce(jnp.maximum, lses)
                weights = [jnp.exp2(x - top) for x in lses]
                inverse = 1.0 / functools.reduce(jnp.add, weights)
                total = None
                for part, weight in zip(here_parts, weights):
                    term = part[at, pl.ds(b * step, step)].astype(jnp.float32) * (weight * inverse)
                    total = term if total is None else total + term
                rows = step // per_row
                out_ref[pl.ds(b * rows, rows), order[group * n + at]] = total.reshape(
                    rows, per_row, HD
                ).astype(jnp.bfloat16)
    for g in range(score_heads):
        tops = [x[2 * g : 2 * g + 1] for x in stats]
        peak = functools.reduce(jnp.maximum, tops)
        whole = functools.reduce(
            jnp.add, [x[2 * g + 1 : 2 * g + 2] * jnp.exp2(t - peak) for x, t in zip(stats, tops)]
        )
        shares = sum_ref[g] * (jnp.exp2(max_ref[g] - peak) / whole)
        column = jnp.sum(shares, axis=1, keepdims=True)
        eye = lax.broadcasted_iota(jnp.int32, (here, here), 0) == lax.broadcasted_iota(
            jnp.int32, (here, here), 1
        )
        score_ref[pl.ds(g, 1)] = jnp.sum(jnp.where(eye, column, 0.0), axis=0, keepdims=True)


def local(keys, values, window_q, keep_stretches, dec_q, dec_k, dec_v, row_order):
    ctx_count = lax.axis_size("ctx")
    row_count = lax.axis_size("rows")
    heads = keys.shape[1] // HD
    here = keys.shape[0] // STRETCH
    rows_total, steps = dec_q.shape[:2]
    score_heads = heads // row_count
    group_count = 2
    shifts = range(1, ctx_count)

    def shifted(x, k):
        return lax.ppermute(x, "ctx", [(i, (i + k) % ctx_count) for i in range(ctx_count)])

    w_each = window_q.shape[0]
    tiles = window_q.reshape(w_each, heads * GROUP, HD).transpose(1, 0, 2)
    tiles = tiles.reshape(heads, GROUP * w_each, HD)
    pieces = [tiles] + [shifted(tiles, k) for k in shifts]

    def rows_first(x):
        x = x.reshape(rows_total, steps, -1, HD).transpose(0, 2, 1, 3)
        return x.reshape(-1, HD)

    q = rows_first(dec_q).reshape(rows_total, heads, GROUP * steps, HD)
    own_k, own_v = rows_first(dec_k), rows_first(dec_v)

    operands = []
    after = row_order
    for group in range(group_count):
        parts = decode(
            group,
            group_count,
            ctx_count,
            row_count,
            keep_stretches,
            row_order,
            q,
            keys,
            values,
            own_k,
            own_v,
            after,
        )
        after = parts[0]
        operands += [parts[0]] + [shifted(parts[k], k) for k in shifts]
    peaks, sums, stat = window(ctx_count, score_heads, pieces, keys, after)
    stats = [stat] + [shifted(stat, k) for k in shifts]
    operands += [peaks, sums] + stats

    rows_each = rows_total // (ctx_count * row_count)
    vmem = pl.BlockSpec(memory_space=pltpu.VMEM)
    stretch_scores, decoded = pl.pallas_call(
        functools.partial(combine_kernel, ctx_count, group_count, here, score_heads),
        out_shape=[
            jax.ShapeDtypeStruct((score_heads, here), jnp.float32),
            jax.ShapeDtypeStruct((rows_each, heads, GROUP * steps, HD), jnp.bfloat16),
        ],
        in_specs=[pl.BlockSpec(memory_space=pltpu.SMEM)] + [vmem] * len(operands),
        out_specs=[vmem, vmem],
        name="combine",
    )(keep_stretches, *operands)
    decoded = decoded.reshape(rows_each, heads * GROUP, steps, HD).transpose(0, 2, 1, 3)
    return (stretch_scores, decoded.reshape(rows_each, steps, heads * GROUP * HD))


def solution(mesh):
    placed = (
        P(("groups", "ctx"), "head"),
        P(("groups", "ctx"), "head"),
        P(("groups", "ctx"), "head"),
        P(("groups", "head"), None),
        P("groups", None, "head"),
        P("groups", None, "head"),
        P("groups", None, "head"),
        P("groups"),
    )
    return jax.shard_map(
        local,
        mesh=mesh,
        in_specs=placed,
        out_specs=(
            P(("groups", "head", "rows"), "ctx"),
            P(("groups", "ctx", "rows"), None, "head"),
        ),
        check_vma=False,
    )
```

```python
import functools
import math

import jax
import jax.numpy as jnp
from jax import lax
from jax.experimental import pallas as pl
from jax.experimental.pallas import tpu as pltpu
from jax.sharding import PartitionSpec as P

QH = 64
KVH = 8
HD = 128
STRETCH = 512
W = 32
GROUP = QH // KVH

FILL = -1.0e30
LIMIT = 1.0e30
SCALE2 = HD ** (-0.5) * math.log2(math.e)
NT = (((1,), (1,)), ((), ()))
TAIL = 16
ONES = 16


def head_order(keep_ref, here):
    heads, keep_count = keep_ref.shape
    if heads != 4:
        return [jnp.int32(h) for h in range(heads)]
    full = [keep_ref[h, keep_count // 2] // here for h in range(heads)]

    def clash(a, b, c, d):
        return (full[a] == full[b]).astype(jnp.int32) + (full[c] == full[d]).astype(jnp.int32)

    c1, c2, c3 = clash(0, 1, 2, 3), clash(0, 2, 1, 3), clash(0, 3, 1, 2)
    mate = jnp.where((c1 <= c2) & (c1 <= c3), 1, jnp.where(c2 <= c3, 2, 3))
    return [jnp.int32(0), mate, jnp.where(mate == 1, 2, 1), jnp.where(mate == 3, 2, 3)]


def pick(options, at):
    value = options[-1]
    for i in range(len(options) - 2, -1, -1):
        value = jnp.where(at == i, options[i], value)
    return value


def decode_kernel(
    group,
    group_count,
    ctx_count,
    row_count,
    keep_ref,
    order_ref,
    q_hbm,
    k_hbm,
    v_hbm,
    own_k_hbm,
    own_v_hbm,
    after_ref,
    *rest,
):
    outs = rest[:ctx_count]
    (q_buf, k_buf, v_buf, kx_buf, vx_buf, m_ref, l_ref, acc_ref, s_buf, note, q_sem, k_sem, v_sem, x_sem) = rest[
        ctx_count:
    ]
    keep_count = keep_ref.shape[1]
    here = k_hbm.shape[0] // STRETCH
    own_index = lax.axis_index("ctx")
    row_index = lax.axis_index("rows")
    is_last = own_index == ctx_count - 1
    base = own_index * here
    rows_total, heads, per_row, _ = q_hbm.shape
    rows_each = rows_total // (ctx_count * row_count)
    local_rows = rows_each * ctx_count
    queries = local_rows * per_row
    chunk = min(256, queries)
    firsts = list(range(0, queries, chunk))
    own_keys = own_k_hbm.shape[0]
    steps = own_keys // (rows_total * heads)
    extra = kx_buf.shape[0]
    count_here = heads // group_count
    order = head_order(keep_ref, here)[group * count_here : (group + 1) * count_here]

    def row_at(j):
        k = j // rows_each
        i = lax.rem(j, rows_each)
        dest = lax.rem(own_index + k, ctx_count)
        return order_ref[dest * (row_count * rows_each) + row_index * rows_each + i]

    @pl.loop(0, local_rows)
    def _(j):
        row = row_at(j)
        for at in range(count_here):
            pltpu.make_async_copy(q_hbm.at[row, order[at]], q_buf.at[at, j], q_sem.at[at]).start()

    for at in range(count_here):
        start = jnp.int32(0)
        count = jnp.int32(0)
        for i in range(keep_count):
            local = keep_ref[order[at], i] - base
            start = start + (local < 0).astype(jnp.int32)
            count = count + ((local >= 0) & (local < here)).astype(jnp.int32)
        note[at, 0] = start
        note[at, 1] = count

    def unit_copies(at, h, u):
        local = keep_ref[h, note[at, 0] + u] - base
        rows = pl.ds(pl.multiple_of(local * STRETCH, STRETCH), STRETCH)
        cols = pl.ds(pl.multiple_of(h * HD, HD), HD)
        slot = at * here + u
        return (
            pltpu.make_async_copy(k_hbm.at[rows, cols], k_buf.at[slot], k_sem.at[slot]),
            pltpu.make_async_copy(v_hbm.at[rows, cols], v_buf.at[slot], v_sem.at[slot]),
        )

    def wait_slot(buf, sem, slot):
        pltpu.make_async_copy(buf.at[slot], buf.at[slot], sem.at[slot]).wait()

    for at in range(count_here):

        @pl.loop(0, note[at, 1])
        def _(u):
            for copy in unit_copies(at, order[at], u):
                copy.start()

    def own_copies():
        return (
            pltpu.make_async_copy(own_k_hbm, kx_buf.at[pl.ds(0, own_keys)], x_sem.at[0]),
            pltpu.make_async_copy(own_v_hbm, vx_buf.at[pl.ds(0, own_keys)], x_sem.at[1]),
        )

    def tail_copies(h):
        tail = pl.ds(k_hbm.shape[0] - W, W)
        cols = pl.ds(pl.multiple_of(h * HD, HD), HD)
        return (
            pltpu.make_async_copy(k_hbm.at[tail, cols], kx_buf.at[pl.ds(own_keys, W)], x_sem.at[2]),
            pltpu.make_async_copy(v_hbm.at[tail, cols], vx_buf.at[pl.ds(own_keys, W)], x_sem.at[3]),
        )

    @pl.when(is_last)
    def _():
        spare = extra - own_keys - W
        kx_buf[pl.ds(own_keys + W, spare)] = jnp.zeros((spare, HD), jnp.bfloat16)
        vx_buf[pl.ds(own_keys + W, spare)] = jnp.zeros((spare, HD), jnp.bfloat16)
        for copy in own_copies():
            copy.start()
        for copy in own_copies():
            copy.wait()

    def turned(v):
        return jnp.concatenate([v.T, jnp.ones((ONES, v.shape[0]), jnp.bfloat16)], axis=0)

    def fold(sl, vt, s):
        old = m_ref[:, sl]
        new = jnp.maximum(old, jnp.max(s, axis=0, keepdims=True))
        alpha = jnp.exp2(old - new)
        t = jnp.dot(vt, jnp.exp2(s - new).astype(jnp.bfloat16), preferred_element_type=jnp.float32)
        l_ref[:, sl] = l_ref[:, sl] * alpha + t[HD : HD + 8]
        acc_ref[:, sl] = acc_ref[:, sl] * alpha + t[:HD]
        m_ref[:, sl] = new

    @pl.loop(0, count_here)
    def _(at):
        h = pick(order, at)
        count = note[at, 1]
        pairs = count // 2
        slot0 = at * here

        @pl.when(is_last)
        def _():
            for copy in tail_copies(h):
                copy.start()

        pltpu.make_async_copy(q_buf.at[at], q_buf.at[at], q_sem.at[at]).wait()

        def q_of(first):
            j0 = first // per_row
            return q_buf[at, pl.ds(j0, chunk // per_row)].reshape(chunk, HD)

        def scores(keys, first):
            return lax.dot_general(keys, q_of(first), NT, preferred_element_type=jnp.float32)

        def pair(buf, b):
            return buf[pl.ds(slot0 + 2 * b, 2)].reshape(2 * STRETCH, HD)

        def fast(sl, vt, s):
            p = jnp.exp2(s * SCALE2 - m_ref[:, sl]).astype(jnp.bfloat16)
            t = jnp.dot(vt, p, preferred_element_type=jnp.float32)
            l_ref[:, sl] += t[HD : HD + 8]
            acc_ref[:, sl] += t[:HD]

        l_ref[...] = jnp.zeros(l_ref.shape, jnp.float32)
        acc_ref[...] = jnp.zeros(acc_ref.shape, jnp.float32)

        @pl.when(count == 0)
        def _():
            m_ref[...] = jnp.full(m_ref.shape, FILL, jnp.float32)

        @pl.when(count > 0)
        def _():
            wait_slot(k_buf, k_sem, slot0)
            for first in firsts:
                s = scores(k_buf[slot0, pl.ds(0, 128)], first)
                m_ref[:, pl.ds(first, chunk)] = jnp.max(s, axis=0, keepdims=True) * SCALE2

        @pl.when(pairs > 0)
        def _():
            wait_slot(k_buf, k_sem, slot0 + 1)
            s_buf[0] = scores(pair(k_buf, 0), firsts[0])

            @pl.loop(0, pairs)
            def _(b):
                more = b + 1 < pairs
                wait_slot(v_buf, v_sem, slot0 + 2 * b)
                wait_slot(v_buf, v_sem, slot0 + 2 * b + 1)

                @pl.when(more)
                def _():
                    wait_slot(k_buf, k_sem, slot0 + 2 * b + 2)
                    wait_slot(k_buf, k_sem, slot0 + 2 * b + 3)

                following = jnp.where(more, b + 1, b)
                vt = turned(pair(v_buf, b))
                for i, first in enumerate(firsts):
                    if i + 1 < len(firsts):
                        s_buf[(i + 1) % 2] = scores(pair(k_buf, b), firsts[i + 1])
                    else:
                        s_buf[(i + 1) % 2] = scores(pair(k_buf, following), firsts[0])
                    fast(pl.ds(first, chunk), vt, s_buf[i % 2])

        @pl.when(count > 2 * pairs)
        def _():
            slot = slot0 + 2 * pairs

            @pl.when(pairs > 0)
            def _():
                wait_slot(k_buf, k_sem, slot)

            wait_slot(v_buf, v_sem, slot)
            vt = turned(v_buf[slot])
            s = scores(k_buf[slot], firsts[0])
            for i, first in enumerate(firsts):
                ahead = scores(k_buf[slot], firsts[i + 1]) if i + 1 < len(firsts) else None
                fast(pl.ds(first, chunk), vt, s)
                s = ahead

        bad = jnp.max(jnp.where(l_ref[...] < LIMIT, 0.0, 1.0))

        @pl.when(bad > 0.0)
        def _():
            l_ref[...] = jnp.zeros(l_ref.shape, jnp.float32)
            acc_ref[...] = jnp.zeros(acc_ref.shape, jnp.float32)
            m_ref[...] = jnp.full(m_ref.shape, FILL, jnp.float32)

            @pl.loop(0, count)
            def _(u):
                vt = turned(v_buf[slot0 + u])
                for first in firsts:
                    fold(pl.ds(first, chunk), vt, scores(k_buf[slot0 + u], first) * SCALE2)

        @pl.when(is_last)
        def _():
            for copy in tail_copies(h):
                copy.wait()
            vt = turned(vx_buf[...])
            key = lax.broadcasted_iota(jnp.int32, (extra, chunk), 0)
            lane = lax.broadcasted_iota(jnp.int32, (1, chunk), 1)
            window = (key >= own_keys) & (key < own_keys + W)
            for first in firsts:
                line = jnp.zeros((1, chunk), jnp.int32)
                for j in range(chunk // per_row):
                    line = jnp.where(lane // per_row == j, row_at(first // per_row + j), line)
                low = line * (heads * steps) + h * steps
                high = low + lax.rem(lane, steps)
                mask = ((key >= low) & (key <= high)) | window
                s = scores(kx_buf[...], first) * SCALE2
                fold(pl.ds(first, chunk), vt, jnp.where(mask, s, FILL))

        total = l_ref[0:1]
        some = total > 0.0
        safe = jnp.where(some, total, 1.0)
        lse = jnp.where(some, m_ref[...] + jnp.log2(safe), FILL)
        inverse = 1.0 / safe
        per_dest = queries // ctx_count
        lines = max(1, per_dest // 128)
        for b in range(queries // 128):
            sl = slice(b * 128, (b + 1) * 128)
            block = (acc_ref[:, sl] * inverse[:, sl]).T.astype(jnp.bfloat16)
            step = min(128, per_dest)
            for piece in range(128 // step):
                at_row = b * 128 + piece * step
                outs[at_row // per_dest][at, pl.ds(at_row % per_dest, step)] = block[
                    piece * step : (piece + 1) * step
                ]
        for k in range(ctx_count):
            b0 = k * per_dest // 128
            lse_lines = [lse[:, (b0 + i) * 128 : (b0 + i + 1) * 128] for i in range(lines)]
            high = [x.astype(jnp.bfloat16).astype(jnp.float32) for x in lse_lines]
            mid = [(x - y).astype(jnp.bfloat16).astype(jnp.float32) for x, y in zip(lse_lines, high)]
            low = [x - y - z for x, y, z in zip(lse_lines, high, mid)]
            block = jnp.concatenate(
                high + mid + low + [jnp.zeros((TAIL - 3 * lines, HD), jnp.float32)], axis=0
            )
            outs[k][at, pl.ds(per_dest, TAIL)] = block.astype(jnp.bfloat16)


def decode(group, group_count, ctx_count, row_count, keep, order, q, keys, values, own_k, own_v, after):
    rows_total, heads, per_row, _ = q.shape
    local_rows = rows_total // row_count
    queries = local_rows * per_row
    chunk = min(256, queries)
    per_dest = queries // ctx_count
    here = keys.shape[0] // STRETCH
    extra = pl.cdiv(own_k.shape[0] + W, HD) * HD
    n = heads // group_count
    slots = n * here
    any_space = pl.BlockSpec(memory_space=pl.ANY)
    return pl.pallas_call(
        functools.partial(decode_kernel, group, group_count, ctx_count, row_count),
        out_shape=[jax.ShapeDtypeStruct((n, per_dest + TAIL, HD), jnp.bfloat16)] * ctx_count,
        grid_spec=pltpu.PrefetchScalarGridSpec(
            num_scalar_prefetch=2,
            grid=(),
            in_specs=[any_space] * 6,
            out_specs=[pl.BlockSpec(memory_space=pltpu.VMEM)] * ctx_count,
            scratch_shapes=[
                pltpu.VMEM((n, local_rows, per_row, HD), jnp.bfloat16),
                pltpu.VMEM((slots, STRETCH, HD), jnp.bfloat16),
                pltpu.VMEM((slots, STRETCH, HD), jnp.bfloat16),
                pltpu.VMEM((extra, HD), jnp.bfloat16),
                pltpu.VMEM((extra, HD), jnp.bfloat16),
                pltpu.VMEM((1, queries), jnp.float32),
                pltpu.VMEM((8, queries), jnp.float32),
                pltpu.VMEM((HD, queries), jnp.float32),
                pltpu.VMEM((2, 2 * STRETCH, chunk), jnp.float32),
                pltpu.SMEM((n, 2), jnp.int32),
                pltpu.SemaphoreType.DMA((n,)),
                pltpu.SemaphoreType.DMA((slots,)),
                pltpu.SemaphoreType.DMA((slots,)),
                pltpu.SemaphoreType.DMA((4,)),
            ],
        ),
        cost_estimate=pl.CostEstimate(
            flops=n * 8 * queries * STRETCH * HD * 4,
            bytes_accessed=n * 8 * STRETCH * HD * 4,
            transcendentals=n * 8 * queries * STRETCH,
        ),
        name="decode",
    )(keep, order, q, keys, values, own_k, own_v, after)


def window_kernel(ctx_count, score_heads, *refs):
    pieces = refs[:ctx_count]
    k_hbm, after_ref, sum_ref, stat_ref, q_buf, k_buf, m_ref, s_buf, flag, k_sem = refs[ctx_count:]
    own_index = lax.axis_index("ctx")
    row_index = lax.axis_index("rows")
    is_last = own_index == ctx_count - 1
    per_block = k_buf.shape[1] // STRETCH
    span = k_buf.shape[1]
    blocks = k_hbm.shape[0] // span
    per_piece = pieces[0].shape[1]
    queries = per_piece * ctx_count
    w_each = W // ctx_count
    for g in range(score_heads):
        cols = pl.ds(pl.multiple_of((row_index * score_heads + g) * HD, HD), HD)
        for b in range(blocks):
            pltpu.make_async_copy(
                k_hbm.at[pl.ds(b * span, span), cols], k_buf.at[g * blocks + b], k_sem.at[g * blocks + b]
            ).start()
    for k, piece in enumerate(pieces):
        source = lax.rem(own_index + (ctx_count - k), ctx_count)
        for g in range(score_heads):
            q_buf[g, source] = piece[row_index * score_heads + g]

    def scores(g, keys):
        q = q_buf[g].reshape(queries, HD)
        return lax.dot_general(keys, q, NT, preferred_element_type=jnp.float32)

    row = lax.broadcasted_iota(jnp.int32, (W, queries), 0)
    col = lax.broadcasted_iota(jnp.int32, (W, queries), 1)
    w = (col // per_piece) * w_each + lax.rem(col, w_each)
    allowed = (row <= w) | jnp.logical_not(is_last)

    for g in range(score_heads):
        pltpu.make_async_copy(k_buf.at[g * blocks], k_buf.at[g * blocks], k_sem.at[g * blocks]).wait()
        s = scores(g, k_buf[g * blocks, pl.ds(0, 128)])
        m_ref[pl.ds(g, 1)] = jnp.max(s, axis=0, keepdims=True) * SCALE2
    flag[0] = jnp.int32(1)

    @pl.loop(0, 2)
    def _(attempt):
        @pl.when((attempt == 1) & (flag[0] > 0))
        def _():
            for g in range(score_heads):

                @pl.loop(0, blocks * per_block)
                def _(c):
                    keys = k_buf[g * blocks + c // per_block, pl.ds(lax.rem(c, per_block) * STRETCH, STRETCH)]
                    s = scores(g, keys)
                    tail = jnp.where(allowed | (c + 1 < blocks * per_block), s[STRETCH - W :], FILL)
                    s = jnp.concatenate([s[: STRETCH - W], tail], axis=0)
                    peak = jnp.max(s, axis=0, keepdims=True) * SCALE2
                    m_ref[pl.ds(g, 1)] = jnp.maximum(m_ref[pl.ds(g, 1)], peak)

        @pl.when(flag[0] > 0)
        def _():
            for g in range(score_heads):
                s_buf[0] = scores(g, k_buf[g * blocks, pl.ds(0, 2 * STRETCH)])

                @pl.loop(0, blocks)
                def _(b):
                    more = b + 1 < blocks

                    @pl.when(more & (attempt == 0))
                    def _():
                        at = g * blocks + b + 1
                        pltpu.make_async_copy(k_buf.at[at], k_buf.at[at], k_sem.at[at]).wait()

                    following = g * blocks + jnp.where(more, b + 1, b)
                    m = m_ref[pl.ds(g, 1)]
                    for i in range(per_block // 2):
                        if i + 1 < per_block // 2:
                            keys = k_buf[g * blocks + b, pl.ds((i + 1) * 2 * STRETCH, 2 * STRETCH)]
                        else:
                            keys = k_buf[following, pl.ds(0, 2 * STRETCH)]
                        s_buf[(i + 1) % 2] = scores(g, keys)
                        for half in range(2):
                            s = s_buf[i % 2, pl.ds(half * STRETCH, STRETCH)]
                            if i == per_block // 2 - 1 and half == 1:
                                tail = jnp.where(allowed | more, s[STRETCH - W :], FILL)
                                s = jnp.concatenate([s[: STRETCH - W], tail], axis=0)
                            p = jnp.exp2(s * SCALE2 - m)
                            sum_ref[g, b * per_block + 2 * i + half] = jnp.sum(
                                p.reshape(STRETCH // 8, 8, queries), axis=0
                            )

            worst = jnp.max(jnp.where(sum_ref[...] < LIMIT, 0.0, 1.0))
            flag[0] = (worst > 0.0).astype(jnp.int32)

    lines = []
    for g in range(score_heads):
        total = jnp.sum(jnp.sum(sum_ref[g], axis=0), axis=0, keepdims=True)
        lines += [m_ref[pl.ds(g, 1)], total]
    lines.append(jnp.zeros((stat_ref.shape[0] - len(lines), queries), jnp.float32))
    stat_ref[...] = jnp.concatenate(lines, axis=0)


def window(ctx_count, score_heads, pieces, keys, after):
    here = keys.shape[0] // STRETCH
    queries = W * GROUP
    per_block = math.gcd(here, 8)
    blocks = score_heads * here // per_block
    vmem = pl.BlockSpec(memory_space=pltpu.VMEM)
    any_space = pl.BlockSpec(memory_space=pl.ANY)
    return pl.pallas_call(
        functools.partial(window_kernel, ctx_count, score_heads),
        out_shape=[
            jax.ShapeDtypeStruct((score_heads, here, 8, queries), jnp.float32),
            jax.ShapeDtypeStruct((8, queries), jnp.float32),
        ],
        in_specs=[vmem] * ctx_count + [any_space] * 2,
        out_specs=[vmem] * 2,
        scratch_shapes=[
            pltpu.VMEM((score_heads, ctx_count, queries // ctx_count, HD), jnp.bfloat16),
            pltpu.VMEM((blocks, per_block * STRETCH, HD), jnp.bfloat16),
            pltpu.VMEM((score_heads, queries), jnp.float32),
            pltpu.VMEM((2, 2 * STRETCH, queries), jnp.float32),
            pltpu.SMEM((1,), jnp.int32),
            pltpu.SemaphoreType.DMA((blocks,)),
        ],
        cost_estimate=pl.CostEstimate(
            flops=score_heads * queries * keys.shape[0] * HD * 2,
            bytes_accessed=score_heads * keys.shape[0] * HD * 2,
            transcendentals=score_heads * queries * keys.shape[0],
        ),
        name="window",
    )(*pieces, keys, after)


def combine_kernel(ctx_count, group_count, here, score_heads, keep_ref, *refs):
    score_ref, out_ref = refs[-2:]
    parts = refs[: group_count * ctx_count]
    sum_ref = refs[group_count * ctx_count]
    stats = refs[group_count * ctx_count + 1 : -2]
    heads, per_row = out_ref.shape[1], out_ref.shape[2]
    order = head_order(keep_ref, here)
    n = heads // group_count
    per_dest = parts[0].shape[1] - TAIL
    step = min(128, per_dest)
    lines = max(1, per_dest // 128)
    for group in range(group_count):
        here_parts = parts[group * ctx_count : (group + 1) * ctx_count]
        for at in range(n):
            for b in range(per_dest // step):
                lses = []
                for k, part in enumerate(here_parts):
                    tail = part[at, pl.ds(per_dest, TAIL)].astype(jnp.float32)
                    line = (
                        tail[b : b + 1]
                        + tail[lines + b : lines + b + 1]
                        + tail[2 * lines + b : 2 * lines + b + 1]
                    )
                    off = k * per_dest % 128
                    lses.append(jnp.broadcast_to(line, (128, HD)).T[off : off + step])
                top = functools.reduce(jnp.maximum, lses)
                weights = [jnp.exp2(x - top) for x in lses]
                inverse = 1.0 / functools.reduce(jnp.add, weights)
                total = None
                for part, weight in zip(here_parts, weights):
                    term = part[at, pl.ds(b * step, step)].astype(jnp.float32) * (weight * inverse)
                    total = term if total is None else total + term
                rows = step // per_row
                out_ref[pl.ds(b * rows, rows), order[group * n + at]] = total.reshape(
                    rows, per_row, HD
                ).astype(jnp.bfloat16)
    for g in range(score_heads):
        tops = [x[2 * g : 2 * g + 1] for x in stats]
        peak = functools.reduce(jnp.maximum, tops)
        whole = functools.reduce(
            jnp.add, [x[2 * g + 1 : 2 * g + 2] * jnp.exp2(t - peak) for x, t in zip(stats, tops)]
        )
        shares = jnp.sum(sum_ref[g], axis=1) * (jnp.exp2(tops[0] - peak) / whole)
        column = jnp.sum(shares, axis=1, keepdims=True)
        eye = lax.broadcasted_iota(jnp.int32, (here, here), 0) == lax.broadcasted_iota(
            jnp.int32, (here, here), 1
        )
        score_ref[pl.ds(g, 1)] = jnp.sum(jnp.where(eye, column, 0.0), axis=0, keepdims=True)


def local(keys, values, window_q, keep_stretches, dec_q, dec_k, dec_v, row_order):
    ctx_count = lax.axis_size("ctx")
    row_count = lax.axis_size("rows")
    heads = keys.shape[1] // HD
    here = keys.shape[0] // STRETCH
    rows_total, steps = dec_q.shape[:2]
    score_heads = heads // row_count
    group_count = 2
    shifts = range(1, ctx_count)

    def shifted(x, k):
        return lax.ppermute(x, "ctx", [(i, (i + k) % ctx_count) for i in range(ctx_count)])

    w_each = window_q.shape[0]
    tiles = window_q.reshape(w_each, heads * GROUP, HD).transpose(1, 0, 2)
    tiles = tiles.reshape(heads, GROUP * w_each, HD)

    def rows_first(x):
        x = x.reshape(rows_total, steps, -1, HD).transpose(0, 2, 1, 3)
        return x.reshape(-1, HD)

    q = rows_first(dec_q).reshape(rows_total, heads, GROUP * steps, HD)
    own_k, own_v = rows_first(dec_k), rows_first(dec_v)

    operands = []
    after = row_order
    for group in range(group_count):
        parts = decode(
            group,
            group_count,
            ctx_count,
            row_count,
            keep_stretches,
            row_order,
            q,
            keys,
            values,
            own_k,
            own_v,
            after,
        )
        after = parts[0]
        if group == 0:
            tiles, after = lax.optimization_barrier((tiles, after))
            pieces = [tiles] + [shifted(tiles, k) for k in shifts]
        operands += [parts[0]] + [shifted(parts[k], k) for k in shifts]
    sums, stat = window(ctx_count, score_heads, pieces, keys, after)
    stats = [stat] + [shifted(stat, k) for k in shifts]
    operands += [sums] + stats

    rows_each = rows_total // (ctx_count * row_count)
    vmem = pl.BlockSpec(memory_space=pltpu.VMEM)
    stretch_scores, decoded = pl.pallas_call(
        functools.partial(combine_kernel, ctx_count, group_count, here, score_heads),
        out_shape=[
            jax.ShapeDtypeStruct((score_heads, here), jnp.float32),
            jax.ShapeDtypeStruct((rows_each, heads, GROUP * steps, HD), jnp.bfloat16),
        ],
        in_specs=[pl.BlockSpec(memory_space=pltpu.SMEM)] + [vmem] * len(operands),
        out_specs=[vmem, vmem],
        name="combine",
    )(keep_stretches, *operands)
    decoded = decoded.reshape(rows_each, heads * GROUP, steps, HD).transpose(0, 2, 1, 3)
    return (stretch_scores, decoded.reshape(rows_each, steps, heads * GROUP * HD))


def solution(mesh):
    placed = (
        P(("groups", "ctx"), "head"),
        P(("groups", "ctx"), "head"),
        P(("groups", "ctx"), "head"),
        P(("groups", "head"), None),
        P("groups", None, "head"),
        P("groups", None, "head"),
        P("groups", None, "head"),
        P("groups"),
    )
    return jax.shard_map(
        local,
        mesh=mesh,
        in_specs=placed,
        out_specs=(
            P(("groups", "head", "rows"), "ctx"),
            P(("groups", "ctx", "rows"), None, "head"),
        ),
        check_vma=False,
    )
```

```python
import functools
import math

import jax
import jax.numpy as jnp
from jax import lax
from jax.experimental import pallas as pl
from jax.experimental.pallas import tpu as pltpu
from jax.sharding import PartitionSpec as P

QH = 64
KVH = 8
HD = 128
STRETCH = 512
W = 32
GROUP = QH // KVH

FILL = -1.0e30
LIMIT = 1.0e30
SCALE2 = HD ** (-0.5) * math.log2(math.e)
NT = (((1,), (1,)), ((), ()))
TAIL = 16
ONES = 16


def head_order(keep_ref, here):
    heads, keep_count = keep_ref.shape
    full = [keep_ref[h, keep_count // 2] // here for h in range(heads)]
    last = jnp.int32(0)
    best = jnp.int32(-1)
    for h in range(heads):
        same = sum((full[h] == other).astype(jnp.int32) for other in full)
        last = jnp.where(same > best, h, last)
        best = jnp.maximum(same, best)
    return [h + (last <= h).astype(jnp.int32) for h in range(heads - 1)] + [last]


def terms(lines):
    high = [x.astype(jnp.bfloat16).astype(jnp.float32) for x in lines]
    mid = [(x - y).astype(jnp.bfloat16).astype(jnp.float32) for x, y in zip(lines, high)]
    low = [x - y - z for x, y, z in zip(lines, high, mid)]
    spare = jnp.zeros((TAIL - 3 * len(lines), lines[0].shape[1]), jnp.float32)
    return jnp.concatenate(high + mid + low + [spare], axis=0).astype(jnp.bfloat16)


def line_of(tile, count, at):
    return tile[at : at + 1] + tile[count + at : count + at + 1] + tile[2 * count + at : 2 * count + at + 1]


def pick(options, at):
    value = options[-1]
    for i in range(len(options) - 2, -1, -1):
        value = jnp.where(at == i, options[i], value)
    return value


def decode_kernel(
    head0,
    count_here,
    ctx_count,
    row_count,
    keep_ref,
    order_ref,
    q_hbm,
    k_hbm,
    v_hbm,
    own_k_hbm,
    own_v_hbm,
    tiles_hbm,
    after_ref,
    *rest,
):
    outs = rest[:ctx_count]
    (q_buf, k_buf, v_buf, kx_buf, vx_buf, m_ref, l_ref, acc_ref, s_buf, note, q_sem, k_sem, v_sem, x_sem, t_sem) = (
        rest[ctx_count:]
    )
    keep_count = keep_ref.shape[1]
    here = k_hbm.shape[0] // STRETCH
    own_index = lax.axis_index("ctx")
    row_index = lax.axis_index("rows")
    is_last = own_index == ctx_count - 1
    base = own_index * here
    rows_total, heads, per_row, _ = q_hbm.shape
    rows_each = rows_total // (ctx_count * row_count)
    local_rows = rows_each * ctx_count
    queries = local_rows * per_row
    chunk = min(256, queries)
    firsts = list(range(0, queries, chunk))
    own_keys = own_k_hbm.shape[0]
    steps = own_keys // (rows_total * heads)
    extra = kx_buf.shape[0]
    order = head_order(keep_ref, here)[head0 : head0 + count_here]
    per_dest = queries // ctx_count
    out_rows = per_dest + TAIL

    def row_at(j):
        k = j // rows_each
        i = lax.rem(j, rows_each)
        dest = lax.rem(own_index + k, ctx_count)
        return order_ref[dest * (row_count * rows_each) + row_index * rows_each + i]

    @pl.loop(0, local_rows)
    def _(j):
        row = row_at(j)
        for at in range(count_here):
            pltpu.make_async_copy(q_hbm.at[row, order[at]], q_buf.at[at, j], q_sem.at[at]).start()

    for at in range(count_here):
        start = jnp.int32(0)
        count = jnp.int32(0)
        for i in range(keep_count):
            local = keep_ref[order[at], i] - base
            start = start + (local < 0).astype(jnp.int32)
            count = count + ((local >= 0) & (local < here)).astype(jnp.int32)
        note[at, 0] = start
        note[at, 1] = count

    def unit_copies(at, h, u):
        local = keep_ref[h, note[at, 0] + u] - base
        rows = pl.ds(pl.multiple_of(local * STRETCH, STRETCH), STRETCH)
        cols = pl.ds(pl.multiple_of(h * HD, HD), HD)
        slot = at * here + u
        return (
            pltpu.make_async_copy(k_hbm.at[rows, cols], k_buf.at[slot], k_sem.at[slot]),
            pltpu.make_async_copy(v_hbm.at[rows, cols], v_buf.at[slot], v_sem.at[slot]),
        )

    def wait_slot(buf, sem, slot):
        pltpu.make_async_copy(buf.at[slot], buf.at[slot], sem.at[slot]).wait()

    for at in range(count_here):

        @pl.loop(0, note[at, 1])
        def _(u):
            for copy in unit_copies(at, order[at], u):
                copy.start()

    def tile_copies():
        if head0:
            return []
        space = pl.ds(count_here * out_rows, tiles_hbm.shape[0])
        return [
            pltpu.make_async_copy(tiles_hbm, outs[k].at[space], t_sem.at[k]) for k in range(1, ctx_count)
        ]

    for copy in tile_copies():
        copy.start()

    def own_copies():
        return (
            pltpu.make_async_copy(own_k_hbm, kx_buf.at[pl.ds(0, own_keys)], x_sem.at[0]),
            pltpu.make_async_copy(own_v_hbm, vx_buf.at[pl.ds(0, own_keys)], x_sem.at[1]),
        )

    def tail_copies(h):
        tail = pl.ds(k_hbm.shape[0] - W, W)
        cols = pl.ds(pl.multiple_of(h * HD, HD), HD)
        return (
            pltpu.make_async_copy(k_hbm.at[tail, cols], kx_buf.at[pl.ds(own_keys, W)], x_sem.at[2]),
            pltpu.make_async_copy(v_hbm.at[tail, cols], vx_buf.at[pl.ds(own_keys, W)], x_sem.at[3]),
        )

    @pl.when(is_last)
    def _():
        spare = extra - own_keys - W
        kx_buf[pl.ds(own_keys + W, spare)] = jnp.zeros((spare, HD), jnp.bfloat16)
        vx_buf[pl.ds(own_keys + W, spare)] = jnp.zeros((spare, HD), jnp.bfloat16)
        for copy in own_copies():
            copy.start()
        for copy in own_copies():
            copy.wait()

    def turned(v):
        return jnp.concatenate([v.T, jnp.ones((ONES, v.shape[0]), jnp.bfloat16)], axis=0)

    def fold(sl, vt, s):
        old = m_ref[:, sl]
        new = jnp.maximum(old, jnp.max(s, axis=0, keepdims=True))
        alpha = jnp.exp2(old - new)
        t = jnp.dot(vt, jnp.exp2(s - new).astype(jnp.bfloat16), preferred_element_type=jnp.float32)
        l_ref[:, sl] = l_ref[:, sl] * alpha + t[HD : HD + 8]
        acc_ref[:, sl] = acc_ref[:, sl] * alpha + t[:HD]
        m_ref[:, sl] = new

    @pl.loop(0, count_here)
    def _(at):
        h = pick(order, at)
        count = note[at, 1]
        pairs = count // 2
        slot0 = at * here

        @pl.when(is_last)
        def _():
            for copy in tail_copies(h):
                copy.start()

        pltpu.make_async_copy(q_buf.at[at], q_buf.at[at], q_sem.at[at]).wait()

        def q_of(first):
            j0 = first // per_row
            return q_buf[at, pl.ds(j0, chunk // per_row)].reshape(chunk, HD)

        def scores(keys, first):
            return lax.dot_general(keys, q_of(first), NT, preferred_element_type=jnp.float32)

        def pair(buf, b):
            return buf[pl.ds(slot0 + 2 * b, 2)].reshape(2 * STRETCH, HD)

        def fast(sl, vt, s):
            p = jnp.exp2(s * SCALE2 - m_ref[:, sl]).astype(jnp.bfloat16)
            t = jnp.dot(vt, p, preferred_element_type=jnp.float32)
            l_ref[:, sl] += t[HD : HD + 8]
            acc_ref[:, sl] += t[:HD]

        l_ref[...] = jnp.zeros(l_ref.shape, jnp.float32)
        acc_ref[...] = jnp.zeros(acc_ref.shape, jnp.float32)

        @pl.when(count == 0)
        def _():
            m_ref[...] = jnp.full(m_ref.shape, FILL, jnp.float32)

        @pl.when(count > 0)
        def _():
            wait_slot(k_buf, k_sem, slot0)
            for first in firsts:
                s = scores(k_buf[slot0, pl.ds(0, 128)], first)
                m_ref[:, pl.ds(first, chunk)] = jnp.max(s, axis=0, keepdims=True) * SCALE2

        @pl.when(pairs > 0)
        def _():
            wait_slot(k_buf, k_sem, slot0 + 1)
            s_buf[0] = scores(pair(k_buf, 0), firsts[0])

            @pl.loop(0, pairs)
            def _(b):
                more = b + 1 < pairs
                wait_slot(v_buf, v_sem, slot0 + 2 * b)
                wait_slot(v_buf, v_sem, slot0 + 2 * b + 1)

                @pl.when(more)
                def _():
                    wait_slot(k_buf, k_sem, slot0 + 2 * b + 2)
                    wait_slot(k_buf, k_sem, slot0 + 2 * b + 3)

                following = jnp.where(more, b + 1, b)
                vt = turned(pair(v_buf, b))
                for i, first in enumerate(firsts):
                    if i + 1 < len(firsts):
                        s_buf[(i + 1) % 2] = scores(pair(k_buf, b), firsts[i + 1])
                    else:
                        s_buf[(i + 1) % 2] = scores(pair(k_buf, following), firsts[0])
                    fast(pl.ds(first, chunk), vt, s_buf[i % 2])

        @pl.when(count > 2 * pairs)
        def _():
            slot = slot0 + 2 * pairs

            @pl.when(pairs > 0)
            def _():
                wait_slot(k_buf, k_sem, slot)

            wait_slot(v_buf, v_sem, slot)
            vt = turned(v_buf[slot])
            s = scores(k_buf[slot], firsts[0])
            for i, first in enumerate(firsts):
                ahead = scores(k_buf[slot], firsts[i + 1]) if i + 1 < len(firsts) else None
                fast(pl.ds(first, chunk), vt, s)
                s = ahead

        bad = jnp.max(jnp.where(l_ref[...] < LIMIT, 0.0, 1.0))

        @pl.when(bad > 0.0)
        def _():
            l_ref[...] = jnp.zeros(l_ref.shape, jnp.float32)
            acc_ref[...] = jnp.zeros(acc_ref.shape, jnp.float32)
            m_ref[...] = jnp.full(m_ref.shape, FILL, jnp.float32)

            @pl.loop(0, count)
            def _(u):
                vt = turned(v_buf[slot0 + u])
                for first in firsts:
                    fold(pl.ds(first, chunk), vt, scores(k_buf[slot0 + u], first) * SCALE2)

        @pl.when(is_last)
        def _():
            for copy in tail_copies(h):
                copy.wait()
            vt = turned(vx_buf[...])
            key = lax.broadcasted_iota(jnp.int32, (extra, chunk), 0)
            lane = lax.broadcasted_iota(jnp.int32, (1, chunk), 1)
            window = (key >= own_keys) & (key < own_keys + W)
            for first in firsts:
                line = jnp.zeros((1, chunk), jnp.int32)
                for j in range(chunk // per_row):
                    line = jnp.where(lane // per_row == j, row_at(first // per_row + j), line)
                low = line * (heads * steps) + h * steps
                high = low + lax.rem(lane, steps)
                mask = ((key >= low) & (key <= high)) | window
                s = scores(kx_buf[...], first) * SCALE2
                fold(pl.ds(first, chunk), vt, jnp.where(mask, s, FILL))

        total = l_ref[0:1]
        some = total > 0.0
        safe = jnp.where(some, total, 1.0)
        lse = jnp.where(some, m_ref[...] + jnp.log2(safe), FILL)
        inverse = 1.0 / safe
        lines = max(1, per_dest // 128)
        row0 = pl.multiple_of(at * out_rows, TAIL)
        for b in range(queries // 128):
            sl = slice(b * 128, (b + 1) * 128)
            block = (acc_ref[:, sl] * inverse[:, sl]).T.astype(jnp.bfloat16)
            step = min(128, per_dest)
            for piece in range(128 // step):
                at_row = b * 128 + piece * step
                outs[at_row // per_dest][pl.ds(row0 + at_row % per_dest, step)] = block[
                    piece * step : (piece + 1) * step
                ]
        for k in range(ctx_count):
            b0 = k * per_dest // 128
            lse_lines = [lse[:, (b0 + i) * 128 : (b0 + i + 1) * 128] for i in range(lines)]
            outs[k][pl.ds(row0 + per_dest, TAIL)] = terms(lse_lines)

    for copy in tile_copies():
        copy.wait()


def decode(head0, n, spare, ctx_count, row_count, keep, order, q, keys, values, own_k, own_v, tiles, after):
    rows_total, heads, per_row, _ = q.shape
    local_rows = rows_total // row_count
    queries = local_rows * per_row
    chunk = min(256, queries)
    per_dest = queries // ctx_count
    here = keys.shape[0] // STRETCH
    extra = pl.cdiv(own_k.shape[0] + W, HD) * HD
    slots = n * here
    any_space = pl.BlockSpec(memory_space=pl.ANY)
    return pl.pallas_call(
        functools.partial(decode_kernel, head0, n, ctx_count, row_count),
        out_shape=[jax.ShapeDtypeStruct((n * (per_dest + TAIL) + spare, HD), jnp.bfloat16)] * ctx_count,
        grid_spec=pltpu.PrefetchScalarGridSpec(
            num_scalar_prefetch=2,
            grid=(),
            in_specs=[any_space] * 7,
            out_specs=[pl.BlockSpec(memory_space=pltpu.VMEM)] * ctx_count,
            scratch_shapes=[
                pltpu.VMEM((n, local_rows, per_row, HD), jnp.bfloat16),
                pltpu.VMEM((slots, STRETCH, HD), jnp.bfloat16),
                pltpu.VMEM((slots, STRETCH, HD), jnp.bfloat16),
                pltpu.VMEM((extra, HD), jnp.bfloat16),
                pltpu.VMEM((extra, HD), jnp.bfloat16),
                pltpu.VMEM((1, queries), jnp.float32),
                pltpu.VMEM((8, queries), jnp.float32),
                pltpu.VMEM((HD, queries), jnp.float32),
                pltpu.VMEM((2, 2 * STRETCH, chunk), jnp.float32),
                pltpu.SMEM((n, 2), jnp.int32),
                pltpu.SemaphoreType.DMA((n,)),
                pltpu.SemaphoreType.DMA((slots,)),
                pltpu.SemaphoreType.DMA((slots,)),
                pltpu.SemaphoreType.DMA((4,)),
                pltpu.SemaphoreType.DMA((ctx_count,)),
            ],
        ),
        cost_estimate=pl.CostEstimate(
            flops=n * 8 * queries * STRETCH * HD * 4,
            bytes_accessed=n * 8 * STRETCH * HD * 4,
            transcendentals=n * 8 * queries * STRETCH,
        ),
        name="decode",
    )(keep, order, q, keys, values, own_k, own_v, tiles, after)


def window_kernel(ctx_count, score_heads, *refs):
    pieces = refs[:ctx_count]
    k_hbm = refs[ctx_count]
    outs = refs[2 * ctx_count + 1 : 3 * ctx_count + 1]
    sum_ref, m_ref, q_buf, k_buf, s_buf, stat_buf, flag, q_sem, k_sem, o_sem = refs[3 * ctx_count + 1 :]
    own_index = lax.axis_index("ctx")
    row_index = lax.axis_index("rows")
    is_last = own_index == ctx_count - 1
    per_block = k_buf.shape[1] // STRETCH
    span = k_buf.shape[1]
    blocks = k_hbm.shape[0] // span
    per_piece = q_buf.shape[2]
    queries = per_piece * ctx_count
    w_each = W // ctx_count
    tile_rows = pieces[0].shape[0]

    def piece_copies():
        copies = []
        for k, piece in enumerate(pieces):
            source = lax.rem(own_index + (ctx_count - k), ctx_count)
            for g in range(score_heads):
                row0 = piece.shape[0] - tile_rows + (row_index * score_heads + g) * per_piece
                rows = pl.ds(pl.multiple_of(row0, TAIL), per_piece)
                copies.append(
                    pltpu.make_async_copy(piece.at[rows], q_buf.at[g, source], q_sem.at[k, g])
                )
        return copies

    for copy in piece_copies():
        copy.start()
    for g in range(score_heads):
        cols = pl.ds(pl.multiple_of((row_index * score_heads + g) * HD, HD), HD)
        for b in range(blocks):
            pltpu.make_async_copy(
                k_hbm.at[pl.ds(b * span, span), cols], k_buf.at[g * blocks + b], k_sem.at[g * blocks + b]
            ).start()
    for copy in piece_copies():
        copy.wait()

    def scores(g, keys):
        q = q_buf[g].reshape(queries, HD)
        return lax.dot_general(keys, q, NT, preferred_element_type=jnp.float32)

    row = lax.broadcasted_iota(jnp.int32, (W, queries), 0)
    col = lax.broadcasted_iota(jnp.int32, (W, queries), 1)
    w = (col // per_piece) * w_each + lax.rem(col, w_each)
    allowed = (row <= w) | jnp.logical_not(is_last)

    for g in range(score_heads):
        pltpu.make_async_copy(k_buf.at[g * blocks], k_buf.at[g * blocks], k_sem.at[g * blocks]).wait()
        s = scores(g, k_buf[g * blocks, pl.ds(0, 128)])
        m_ref[pl.ds(g, 1)] = jnp.max(s, axis=0, keepdims=True) * SCALE2
    flag[0] = jnp.int32(1)

    @pl.loop(0, 2)
    def _(attempt):
        @pl.when((attempt == 1) & (flag[0] > 0))
        def _():
            for g in range(score_heads):

                @pl.loop(0, blocks * per_block)
                def _(c):
                    keys = k_buf[g * blocks + c // per_block, pl.ds(lax.rem(c, per_block) * STRETCH, STRETCH)]
                    s = scores(g, keys)
                    tail = jnp.where(allowed | (c + 1 < blocks * per_block), s[STRETCH - W :], FILL)
                    s = jnp.concatenate([s[: STRETCH - W], tail], axis=0)
                    peak = jnp.max(s, axis=0, keepdims=True) * SCALE2
                    m_ref[pl.ds(g, 1)] = jnp.maximum(m_ref[pl.ds(g, 1)], peak)

        @pl.when(flag[0] > 0)
        def _():
            for g in range(score_heads):
                s_buf[0] = scores(g, k_buf[g * blocks, pl.ds(0, 2 * STRETCH)])

                @pl.loop(0, blocks)
                def _(b):
                    more = b + 1 < blocks

                    @pl.when(more & (attempt == 0))
                    def _():
                        at = g * blocks + b + 1
                        pltpu.make_async_copy(k_buf.at[at], k_buf.at[at], k_sem.at[at]).wait()

                    following = g * blocks + jnp.where(more, b + 1, b)
                    m = m_ref[pl.ds(g, 1)]
                    for i in range(per_block // 2):
                        if i + 1 < per_block // 2:
                            keys = k_buf[g * blocks + b, pl.ds((i + 1) * 2 * STRETCH, 2 * STRETCH)]
                        else:
                            keys = k_buf[following, pl.ds(0, 2 * STRETCH)]
                        s_buf[(i + 1) % 2] = scores(g, keys)
                        for half in range(2):
                            s = s_buf[i % 2, pl.ds(half * STRETCH, STRETCH)]
                            if i == per_block // 2 - 1 and half == 1:
                                tail = jnp.where(allowed | more, s[STRETCH - W :], FILL)
                                s = jnp.concatenate([s[: STRETCH - W], tail], axis=0)
                            p = jnp.exp2(s * SCALE2 - m)
                            sum_ref[g, b * per_block + 2 * i + half] = jnp.sum(
                                p.reshape(STRETCH // 8, 8, queries), axis=0
                            )

            worst = jnp.max(jnp.where(sum_ref[...] < LIMIT, 0.0, 1.0))
            flag[0] = (worst > 0.0).astype(jnp.int32)

    lines = []
    for g in range(score_heads):
        total = jnp.sum(jnp.sum(sum_ref[g], axis=0), axis=0, keepdims=True)
        lse = m_ref[pl.ds(g, 1)] + jnp.log2(total)
        lines += [lse[:, at : at + 128] for at in range(0, queries, 128)]
    stat_buf[...] = terms(lines)
    copies = [
        pltpu.make_async_copy(stat_buf, out.at[pl.ds(out.shape[0] - TAIL, TAIL)], o_sem.at[k])
        for k, out in enumerate(outs)
    ]
    for copy in copies:
        copy.start()
    for copy in copies:
        copy.wait()


def window(ctx_count, score_heads, pieces, keys, parts):
    here = keys.shape[0] // STRETCH
    queries = W * GROUP
    per_block = math.gcd(here, 8)
    blocks = score_heads * here // per_block
    vmem = pl.BlockSpec(memory_space=pltpu.VMEM)
    any_space = pl.BlockSpec(memory_space=pl.ANY)
    return pl.pallas_call(
        functools.partial(window_kernel, ctx_count, score_heads),
        out_shape=[jax.ShapeDtypeStruct(part.shape, part.dtype) for part in parts]
        + [
            jax.ShapeDtypeStruct((score_heads, here, 8, queries), jnp.float32),
            jax.ShapeDtypeStruct((score_heads, queries), jnp.float32),
        ],
        in_specs=[any_space] * (2 * ctx_count + 1),
        out_specs=[any_space] * ctx_count + [vmem] * 2,
        scratch_shapes=[
            pltpu.VMEM((score_heads, ctx_count, queries // ctx_count, HD), jnp.bfloat16),
            pltpu.VMEM((blocks, per_block * STRETCH, HD), jnp.bfloat16),
            pltpu.VMEM((2, 2 * STRETCH, queries), jnp.float32),
            pltpu.VMEM((TAIL, HD), jnp.bfloat16),
            pltpu.SMEM((1,), jnp.int32),
            pltpu.SemaphoreType.DMA((ctx_count, score_heads)),
            pltpu.SemaphoreType.DMA((blocks,)),
            pltpu.SemaphoreType.DMA((ctx_count,)),
        ],
        input_output_aliases={ctx_count + 1 + k: k for k in range(ctx_count)},
        cost_estimate=pl.CostEstimate(
            flops=score_heads * queries * keys.shape[0] * HD * 2,
            bytes_accessed=score_heads * keys.shape[0] * HD * 2,
            transcendentals=score_heads * queries * keys.shape[0],
        ),
        name="window",
    )(*pieces, keys, *parts)


def combine_kernel(head0, n, ctx_count, heads, here, score_heads, keep_ref, *refs):
    parts = refs[:ctx_count]
    if head0:
        sum_ref, m_ref, _, score_ref, out_ref, buf, sem = refs[ctx_count:]
    else:
        _, out_ref, buf, sem = refs[ctx_count:]
    per_row = out_ref.shape[2]
    order = head_order(keep_ref, here)
    per_dest = buf.shape[1] * per_row
    step = min(128, per_dest)
    lines = max(1, per_dest // 128)
    copies = []
    for at in range(n):
        row0 = at * (per_dest + TAIL)
        tiles = [part[pl.ds(row0 + per_dest, TAIL)].astype(jnp.float32) for part in parts]
        for b in range(per_dest // step):
            lses = [line_of(tile, lines, b) for tile in tiles]
            if step == 128:
                top = functools.reduce(jnp.maximum, lses)
                weights = [jnp.exp2(x - top) for x in lses]
                inverse = 1.0 / functools.reduce(jnp.add, weights)
                shares = [jnp.broadcast_to(x * inverse, (128, HD)).T for x in weights]
            else:
                turned_lses = [
                    jnp.broadcast_to(x, (128, HD)).T[k * per_dest % 128 : k * per_dest % 128 + step]
                    for k, x in enumerate(lses)
                ]
                top = functools.reduce(jnp.maximum, turned_lses)
                weights = [jnp.exp2(x - top) for x in turned_lses]
                inverse = 1.0 / functools.reduce(jnp.add, weights)
                shares = [x * inverse for x in weights]
            total = None
            for part, share in zip(parts, shares):
                term = part[pl.ds(row0 + b * step, step)].astype(jnp.float32) * share
                total = term if total is None else total + term
            rows = step // per_row
            buf[at, pl.ds(b * rows, rows)] = total.reshape(rows, per_row, HD).astype(jnp.bfloat16)
        copies.append(pltpu.make_async_copy(buf.at[at], out_ref.at[:, order[head0 + at]], sem.at[at]))
        copies[-1].start()
    if head0:
        tiles = [part[pl.ds(part.shape[0] - TAIL, TAIL)].astype(jnp.float32) for part in parts]
        queries = m_ref.shape[1]
        count = queries // 128
        for g in range(score_heads):
            lses = [
                jnp.concatenate(
                    [line_of(tile, score_heads * count, g * count + i) for i in range(count)], axis=1
                )
                for tile in tiles
            ]
            top = functools.reduce(jnp.maximum, lses)
            whole = functools.reduce(jnp.add, [jnp.exp2(x - top) for x in lses])
            shares = jnp.sum(sum_ref[g], axis=1) * (jnp.exp2(m_ref[pl.ds(g, 1)] - top) / whole)
            column = jnp.sum(shares, axis=1, keepdims=True)
            eye = lax.broadcasted_iota(jnp.int32, (here, here), 0) == lax.broadcasted_iota(
                jnp.int32, (here, here), 1
            )
            score_ref[pl.ds(g, 1)] = jnp.sum(jnp.where(eye, column, 0.0), axis=0, keepdims=True)
    for copy in copies:
        copy.wait()


def local(keys, values, window_q, keep_stretches, dec_q, dec_k, dec_v, row_order):
    ctx_count = lax.axis_size("ctx")
    row_count = lax.axis_size("rows")
    heads = keys.shape[1] // HD
    here = keys.shape[0] // STRETCH
    rows_total, steps = dec_q.shape[:2]
    score_heads = heads // row_count
    shifts = range(1, ctx_count)

    def spread(parts):
        return [parts[0]] + [
            lax.ppermute(parts[k], "ctx", [(i, (i + k) % ctx_count) for i in range(ctx_count)])
            for k in shifts
        ]

    w_each = window_q.shape[0]
    tiles = window_q.reshape(w_each, heads * GROUP, HD).transpose(1, 0, 2)
    tiles = tiles.reshape(heads * GROUP * w_each, HD)

    def rows_first(x):
        x = x.reshape(rows_total, steps, -1, HD).transpose(0, 2, 1, 3)
        return x.reshape(-1, HD)

    q = rows_first(dec_q).reshape(rows_total, heads, GROUP * steps, HD)
    own_k, own_v = rows_first(dec_k), rows_first(dec_v)

    def decoded_part(head0, n, spare, after):
        return decode(
            head0,
            n,
            spare,
            ctx_count,
            row_count,
            keep_stretches,
            row_order,
            q,
            keys,
            values,
            own_k,
            own_v,
            tiles,
            after,
        )

    many = heads - 1
    first = decoded_part(0, many, tiles.shape[0], row_order)
    first_parts = spread(first)
    second = decoded_part(many, 1, TAIL, first[0])
    *second, sums, peaks = window(ctx_count, score_heads, [tiles] + first_parts[1:], keys, second)
    second_parts = spread(second)

    rows_each = rows_total // (ctx_count * row_count)
    per_row = GROUP * steps
    vmem = pl.BlockSpec(memory_space=pltpu.VMEM)
    smem = pl.BlockSpec(memory_space=pltpu.SMEM)
    any_space = pl.BlockSpec(memory_space=pl.ANY)
    out_shape = jax.ShapeDtypeStruct((rows_each, heads, per_row, HD), jnp.bfloat16)

    def scratch(n):
        return [pltpu.VMEM((n, rows_each, per_row, HD), jnp.bfloat16), pltpu.SemaphoreType.DMA((n,))]

    begun = pl.pallas_call(
        functools.partial(combine_kernel, 0, many, ctx_count, heads, here, score_heads),
        out_shape=out_shape,
        in_specs=[smem] + [vmem] * ctx_count + [any_space],
        out_specs=any_space,
        scratch_shapes=scratch(many),
        cost_estimate=pl.CostEstimate(flops=10**6, bytes_accessed=10**7, transcendentals=0),
        name="combine_many",
    )(keep_stretches, *first_parts, peaks)
    stretch_scores, decoded = pl.pallas_call(
        functools.partial(combine_kernel, many, 1, ctx_count, heads, here, score_heads),
        out_shape=[jax.ShapeDtypeStruct((score_heads, here), jnp.float32), out_shape],
        in_specs=[smem] + [vmem] * (ctx_count + 2) + [any_space],
        out_specs=[vmem, any_space],
        scratch_shapes=scratch(1),
        input_output_aliases={ctx_count + 3: 1},
        name="combine_one",
    )(keep_stretches, *second_parts, sums, peaks, begun)
    decoded = decoded.reshape(rows_each, heads * GROUP, steps, HD).transpose(0, 2, 1, 3)
    return (stretch_scores, decoded.reshape(rows_each, steps, heads * GROUP * HD))


def solution(mesh):
    placed = (
        P(("groups", "ctx"), "head"),
        P(("groups", "ctx"), "head"),
        P(("groups", "ctx"), "head"),
        P(("groups", "head"), None),
        P("groups", None, "head"),
        P("groups", None, "head"),
        P("groups", None, "head"),
        P("groups"),
    )
    return jax.shard_map(
        local,
        mesh=mesh,
        in_specs=placed,
        out_specs=(
            P(("groups", "head", "rows"), "ctx"),
            P(("groups", "ctx", "rows"), None, "head"),
        ),
        check_vma=False,
    )
```

```python
import functools
import math

import jax
import jax.numpy as jnp
from jax import lax
from jax.experimental import pallas as pl
from jax.experimental.pallas import tpu as pltpu
from jax.sharding import PartitionSpec as P

QH = 64
KVH = 8
HD = 128
STRETCH = 512
W = 32
GROUP = QH // KVH

FILL = -1.0e30
LIMIT = 1.0e30
SCALE2 = HD ** (-0.5) * math.log2(math.e)
NT = (((1,), (1,)), ((), ()))
TAIL = 16
ONES = 16


def head_order(keep_ref, here):
    heads, keep_count = keep_ref.shape
    full = [keep_ref[h, keep_count // 2] // here for h in range(heads)]
    last = jnp.int32(0)
    best = jnp.int32(-1)
    for h in range(heads):
        same = sum((full[h] == other).astype(jnp.int32) for other in full)
        last = jnp.where(same > best, h, last)
        best = jnp.maximum(same, best)
    return [h + (last <= h).astype(jnp.int32) for h in range(heads - 1)] + [last]


def terms(lines):
    high = [x.astype(jnp.bfloat16).astype(jnp.float32) for x in lines]
    mid = [(x - y).astype(jnp.bfloat16).astype(jnp.float32) for x, y in zip(lines, high)]
    low = [x - y - z for x, y, z in zip(lines, high, mid)]
    spare = jnp.zeros((TAIL - 3 * len(lines), lines[0].shape[1]), jnp.float32)
    return jnp.concatenate(high + mid + low + [spare], axis=0).astype(jnp.bfloat16)


def line_of(tile, count, at):
    return tile[at : at + 1] + tile[count + at : count + at + 1] + tile[2 * count + at : 2 * count + at + 1]


def partner(own_index, k, ctx_count):
    assert ctx_count & (ctx_count - 1) == 0
    return own_index ^ k


def pick(options, at):
    value = options[-1]
    for i in range(len(options) - 2, -1, -1):
        value = jnp.where(at == i, options[i], value)
    return value


def window_part(pieces, k_hbm, sum_ref, scratch):
    m_ref, q_buf, k_buf, s_buf, flag, q_sem, k_sem = scratch
    ctx_count = len(pieces)
    score_heads = q_buf.shape[0]
    own_index = lax.axis_index("ctx")
    row_index = lax.axis_index("rows")
    is_last = own_index == ctx_count - 1
    per_block = k_buf.shape[1] // STRETCH
    span = k_buf.shape[1]
    blocks = k_hbm.shape[0] // span
    per_piece = q_buf.shape[2]
    queries = per_piece * ctx_count
    w_each = W // ctx_count

    def piece_copies():
        copies = []
        for k, piece in enumerate(pieces):
            source = partner(own_index, k, ctx_count) if k else own_index
            for g in range(score_heads):
                row0 = (row_index * score_heads + g) * per_piece
                rows = pl.ds(pl.multiple_of(row0, TAIL), per_piece)
                copies.append(
                    pltpu.make_async_copy(piece.at[rows], q_buf.at[g, source], q_sem.at[k, g])
                )
        return copies

    for copy in piece_copies():
        copy.start()
    for g in range(score_heads):
        cols = pl.ds(pl.multiple_of((row_index * score_heads + g) * HD, HD), HD)
        for b in range(blocks):
            pltpu.make_async_copy(
                k_hbm.at[pl.ds(b * span, span), cols], k_buf.at[g * blocks + b], k_sem.at[g * blocks + b]
            ).start()
    def run():
        for copy in piece_copies():
            copy.wait()

        def scores(g, keys):
            q = q_buf[g].reshape(queries, HD)
            return lax.dot_general(keys, q, NT, preferred_element_type=jnp.float32)

        row = lax.broadcasted_iota(jnp.int32, (W, queries), 0)
        col = lax.broadcasted_iota(jnp.int32, (W, queries), 1)
        w = (col // per_piece) * w_each + lax.rem(col, w_each)
        allowed = (row <= w) | jnp.logical_not(is_last)

        for g in range(score_heads):
            pltpu.make_async_copy(k_buf.at[g * blocks], k_buf.at[g * blocks], k_sem.at[g * blocks]).wait()
            s = scores(g, k_buf[g * blocks, pl.ds(0, 128)])
            m_ref[pl.ds(g, 1)] = jnp.max(s, axis=0, keepdims=True) * SCALE2
        flag[0] = jnp.int32(1)

        @pl.loop(0, 2)
        def _(attempt):
            @pl.when((attempt == 1) & (flag[0] > 0))
            def _():
                for g in range(score_heads):

                    @pl.loop(0, blocks * per_block)
                    def _(c):
                        keys = k_buf[g * blocks + c // per_block, pl.ds(lax.rem(c, per_block) * STRETCH, STRETCH)]
                        s = scores(g, keys)
                        tail = jnp.where(allowed | (c + 1 < blocks * per_block), s[STRETCH - W :], FILL)
                        s = jnp.concatenate([s[: STRETCH - W], tail], axis=0)
                        peak = jnp.max(s, axis=0, keepdims=True) * SCALE2
                        m_ref[pl.ds(g, 1)] = jnp.maximum(m_ref[pl.ds(g, 1)], peak)

            @pl.when(flag[0] > 0)
            def _():
                for g in range(score_heads):
                    s_buf[0] = scores(g, k_buf[g * blocks, pl.ds(0, 2 * STRETCH)])

                    @pl.loop(0, blocks)
                    def _(b):
                        more = b + 1 < blocks

                        @pl.when(more & (attempt == 0))
                        def _():
                            at = g * blocks + b + 1
                            pltpu.make_async_copy(k_buf.at[at], k_buf.at[at], k_sem.at[at]).wait()

                        following = g * blocks + jnp.where(more, b + 1, b)
                        m = m_ref[pl.ds(g, 1)]
                        for i in range(per_block // 2):
                            if i + 1 < per_block // 2:
                                keys = k_buf[g * blocks + b, pl.ds((i + 1) * 2 * STRETCH, 2 * STRETCH)]
                            else:
                                keys = k_buf[following, pl.ds(0, 2 * STRETCH)]
                            s_buf[(i + 1) % 2] = scores(g, keys)
                            for half in range(2):
                                s = s_buf[i % 2, pl.ds(half * STRETCH, STRETCH)]
                                if i == per_block // 2 - 1 and half == 1:
                                    tail = jnp.where(allowed | more, s[STRETCH - W :], FILL)
                                    s = jnp.concatenate([s[: STRETCH - W], tail], axis=0)
                                p = jnp.exp2(s * SCALE2 - m)
                                sum_ref[g, b * per_block + 2 * i + half] = jnp.sum(
                                    p.reshape(STRETCH // 8, 8, queries), axis=0
                                )

                worst = jnp.max(jnp.where(sum_ref[...] < LIMIT, 0.0, 1.0))
                flag[0] = (worst > 0.0).astype(jnp.int32)

        lines = []
        for g in range(score_heads):
            total = jnp.sum(jnp.sum(sum_ref[g], axis=0), axis=0, keepdims=True)
            lse = m_ref[pl.ds(g, 1)] + jnp.log2(total)
            lines += [lse[:, at : at + 128] for at in range(0, queries, 128)]
        return lines

    return run


def decode_kernel(
    head0,
    count_here,
    ctx_count,
    row_count,
    keep_ref,
    order_ref,
    q_hbm,
    k_hbm,
    v_hbm,
    own_k_hbm,
    own_v_hbm,
    after_ref,
    *rest,
):
    run_window = None
    if head0:
        pieces, rest = rest[:ctx_count], rest[ctx_count:]
        run_window = window_part(pieces, k_hbm, rest[ctx_count], rest[-7:])
        rest = rest[:ctx_count] + rest[ctx_count + 1 : -7]
    outs = rest[:ctx_count]
    (q_buf, k_buf, v_buf, kx_buf, vx_buf, m_ref, l_ref, acc_ref, s_buf, note, q_sem, k_sem, v_sem, x_sem) = rest[
        ctx_count:
    ]
    keep_count = keep_ref.shape[1]
    here = k_hbm.shape[0] // STRETCH
    own_index = lax.axis_index("ctx")
    row_index = lax.axis_index("rows")
    is_last = own_index == ctx_count - 1
    base = own_index * here
    rows_total, heads, per_row, _ = q_hbm.shape
    rows_each = rows_total // (ctx_count * row_count)
    local_rows = rows_each * ctx_count
    queries = local_rows * per_row
    chunk = min(256, queries)
    firsts = list(range(0, queries, chunk))
    own_keys = own_k_hbm.shape[0]
    steps = own_keys // (rows_total * heads)
    extra = kx_buf.shape[0]
    order = head_order(keep_ref, here)[head0 : head0 + count_here]
    per_dest = queries // ctx_count
    out_rows = per_dest + TAIL

    def row_at(j):
        k = j // rows_each
        i = lax.rem(j, rows_each)
        dest = partner(own_index, k, ctx_count)
        return order_ref[dest * (row_count * rows_each) + row_index * rows_each + i]

    @pl.loop(0, local_rows)
    def _(j):
        row = row_at(j)
        for at in range(count_here):
            pltpu.make_async_copy(q_hbm.at[row, order[at]], q_buf.at[at, j], q_sem.at[at]).start()

    for at in range(count_here):
        start = jnp.int32(0)
        count = jnp.int32(0)
        for i in range(keep_count):
            local = keep_ref[order[at], i] - base
            start = start + (local < 0).astype(jnp.int32)
            count = count + ((local >= 0) & (local < here)).astype(jnp.int32)
        note[at, 0] = start
        note[at, 1] = count

    def unit_copies(at, h, u):
        local = keep_ref[h, note[at, 0] + u] - base
        rows = pl.ds(pl.multiple_of(local * STRETCH, STRETCH), STRETCH)
        cols = pl.ds(pl.multiple_of(h * HD, HD), HD)
        slot = at * here + u
        return (
            pltpu.make_async_copy(k_hbm.at[rows, cols], k_buf.at[slot], k_sem.at[slot]),
            pltpu.make_async_copy(v_hbm.at[rows, cols], v_buf.at[slot], v_sem.at[slot]),
        )

    def wait_slot(buf, sem, slot):
        pltpu.make_async_copy(buf.at[slot], buf.at[slot], sem.at[slot]).wait()

    for at in range(count_here):

        @pl.loop(0, note[at, 1])
        def _(u):
            for copy in unit_copies(at, order[at], u):
                copy.start()

    def own_copies():
        return (
            pltpu.make_async_copy(own_k_hbm, kx_buf.at[pl.ds(0, own_keys)], x_sem.at[0]),
            pltpu.make_async_copy(own_v_hbm, vx_buf.at[pl.ds(0, own_keys)], x_sem.at[1]),
        )

    def tail_copies(h):
        tail = pl.ds(k_hbm.shape[0] - W, W)
        cols = pl.ds(pl.multiple_of(h * HD, HD), HD)
        return (
            pltpu.make_async_copy(k_hbm.at[tail, cols], kx_buf.at[pl.ds(own_keys, W)], x_sem.at[2]),
            pltpu.make_async_copy(v_hbm.at[tail, cols], vx_buf.at[pl.ds(own_keys, W)], x_sem.at[3]),
        )

    @pl.when(is_last)
    def _():
        spare = extra - own_keys - W
        kx_buf[pl.ds(own_keys + W, spare)] = jnp.zeros((spare, HD), jnp.bfloat16)
        vx_buf[pl.ds(own_keys + W, spare)] = jnp.zeros((spare, HD), jnp.bfloat16)
        for copy in own_copies():
            copy.start()
        for copy in own_copies():
            copy.wait()

    def turned(v):
        return jnp.concatenate([v.T, jnp.ones((ONES, v.shape[0]), jnp.bfloat16)], axis=0)

    def fold(sl, vt, s):
        old = m_ref[:, sl]
        new = jnp.maximum(old, jnp.max(s, axis=0, keepdims=True))
        alpha = jnp.exp2(old - new)
        t = jnp.dot(vt, jnp.exp2(s - new).astype(jnp.bfloat16), preferred_element_type=jnp.float32)
        l_ref[:, sl] = l_ref[:, sl] * alpha + t[HD : HD + 8]
        acc_ref[:, sl] = acc_ref[:, sl] * alpha + t[:HD]
        m_ref[:, sl] = new

    if run_window is not None:
        tile = terms(run_window())
        for out in outs:
            out[pl.ds(count_here * out_rows, TAIL)] = tile

    @pl.loop(0, count_here)
    def _(at):
        h = pick(order, at)
        count = note[at, 1]
        pairs = count // 2
        slot0 = at * here

        @pl.when(is_last)
        def _():
            for copy in tail_copies(h):
                copy.start()

        pltpu.make_async_copy(q_buf.at[at], q_buf.at[at], q_sem.at[at]).wait()

        def q_of(first):
            j0 = first // per_row
            return q_buf[at, pl.ds(j0, chunk // per_row)].reshape(chunk, HD)

        def scores(keys, first):
            return lax.dot_general(keys, q_of(first), NT, preferred_element_type=jnp.float32)

        def pair(buf, b):
            return buf[pl.ds(slot0 + 2 * b, 2)].reshape(2 * STRETCH, HD)

        def fast(sl, vt, s):
            p = jnp.exp2(s * SCALE2 - m_ref[:, sl]).astype(jnp.bfloat16)
            t = jnp.dot(vt, p, preferred_element_type=jnp.float32)
            l_ref[:, sl] += t[HD : HD + 8]
            acc_ref[:, sl] += t[:HD]

        l_ref[...] = jnp.zeros(l_ref.shape, jnp.float32)
        acc_ref[...] = jnp.zeros(acc_ref.shape, jnp.float32)

        @pl.when(count == 0)
        def _():
            m_ref[...] = jnp.full(m_ref.shape, FILL, jnp.float32)

        @pl.when(count > 0)
        def _():
            wait_slot(k_buf, k_sem, slot0)
            for first in firsts:
                s = scores(k_buf[slot0, pl.ds(0, 128)], first)
                m_ref[:, pl.ds(first, chunk)] = jnp.max(s, axis=0, keepdims=True) * SCALE2

        @pl.when(pairs > 0)
        def _():
            wait_slot(k_buf, k_sem, slot0 + 1)
            s_buf[0] = scores(pair(k_buf, 0), firsts[0])

            @pl.loop(0, pairs)
            def _(b):
                more = b + 1 < pairs
                wait_slot(v_buf, v_sem, slot0 + 2 * b)
                wait_slot(v_buf, v_sem, slot0 + 2 * b + 1)

                @pl.when(more)
                def _():
                    wait_slot(k_buf, k_sem, slot0 + 2 * b + 2)
                    wait_slot(k_buf, k_sem, slot0 + 2 * b + 3)

                following = jnp.where(more, b + 1, b)
                vt = turned(pair(v_buf, b))
                for i, first in enumerate(firsts):
                    if i + 1 < len(firsts):
                        s_buf[(i + 1) % 2] = scores(pair(k_buf, b), firsts[i + 1])
                    else:
                        s_buf[(i + 1) % 2] = scores(pair(k_buf, following), firsts[0])
                    fast(pl.ds(first, chunk), vt, s_buf[i % 2])

        @pl.when(count > 2 * pairs)
        def _():
            slot = slot0 + 2 * pairs

            @pl.when(pairs > 0)
            def _():
                wait_slot(k_buf, k_sem, slot)

            wait_slot(v_buf, v_sem, slot)
            vt = turned(v_buf[slot])
            s = scores(k_buf[slot], firsts[0])
            for i, first in enumerate(firsts):
                ahead = scores(k_buf[slot], firsts[i + 1]) if i + 1 < len(firsts) else None
                fast(pl.ds(first, chunk), vt, s)
                s = ahead

        bad = jnp.max(jnp.where(l_ref[...] < LIMIT, 0.0, 1.0))

        @pl.when(bad > 0.0)
        def _():
            l_ref[...] = jnp.zeros(l_ref.shape, jnp.float32)
            acc_ref[...] = jnp.zeros(acc_ref.shape, jnp.float32)
            m_ref[...] = jnp.full(m_ref.shape, FILL, jnp.float32)

            @pl.loop(0, count)
            def _(u):
                vt = turned(v_buf[slot0 + u])
                for first in firsts:
                    fold(pl.ds(first, chunk), vt, scores(k_buf[slot0 + u], first) * SCALE2)

        @pl.when(is_last)
        def _():
            for copy in tail_copies(h):
                copy.wait()
            vt = turned(vx_buf[...])
            key = lax.broadcasted_iota(jnp.int32, (extra, chunk), 0)
            lane = lax.broadcasted_iota(jnp.int32, (1, chunk), 1)
            window = (key >= own_keys) & (key < own_keys + W)
            for first in firsts:
                line = jnp.zeros((1, chunk), jnp.int32)
                for j in range(chunk // per_row):
                    line = jnp.where(lane // per_row == j, row_at(first // per_row + j), line)
                low = line * (heads * steps) + h * steps
                high = low + lax.rem(lane, steps)
                mask = ((key >= low) & (key <= high)) | window
                s = scores(kx_buf[...], first) * SCALE2
                fold(pl.ds(first, chunk), vt, jnp.where(mask, s, FILL))

        total = l_ref[0:1]
        some = total > 0.0
        safe = jnp.where(some, total, 1.0)
        lse = jnp.where(some, m_ref[...] + jnp.log2(safe), FILL)
        inverse = 1.0 / safe
        lines = max(1, per_dest // 128)
        row0 = pl.multiple_of(at * out_rows, TAIL)
        for b in range(queries // 128):
            sl = slice(b * 128, (b + 1) * 128)
            block = (acc_ref[:, sl] * inverse[:, sl]).T.astype(jnp.bfloat16)
            step = min(128, per_dest)
            for piece in range(128 // step):
                at_row = b * 128 + piece * step
                outs[at_row // per_dest][pl.ds(row0 + at_row % per_dest, step)] = block[
                    piece * step : (piece + 1) * step
                ]
        for k in range(ctx_count):
            b0 = k * per_dest // 128
            lse_lines = [lse[:, (b0 + i) * 128 : (b0 + i + 1) * 128] for i in range(lines)]
            outs[k][pl.ds(row0 + per_dest, TAIL)] = terms(lse_lines)


def decode(head0, n, ctx_count, row_count, keep, order, q, keys, values, own_k, own_v, after, pieces):
    rows_total, heads, per_row, _ = q.shape
    local_rows = rows_total // row_count
    queries = local_rows * per_row
    chunk = min(256, queries)
    per_dest = queries // ctx_count
    here = keys.shape[0] // STRETCH
    extra = pl.cdiv(own_k.shape[0] + W, HD) * HD
    slots = n * here
    any_space = pl.BlockSpec(memory_space=pl.ANY)
    vmem = pl.BlockSpec(memory_space=pltpu.VMEM)
    score_heads = heads // row_count
    window_queries = W * GROUP
    window_outs, window_scratch = [], []
    if pieces:
        per_block = math.gcd(here, 8)
        blocks = score_heads * here // per_block
        window_outs = [jax.ShapeDtypeStruct((score_heads, here, 8, window_queries), jnp.float32)]
        window_scratch = [
            pltpu.VMEM((score_heads, window_queries), jnp.float32),
            pltpu.VMEM((score_heads, ctx_count, window_queries // ctx_count, HD), jnp.bfloat16),
            pltpu.VMEM((blocks, per_block * STRETCH, HD), jnp.bfloat16),
            pltpu.VMEM((2, 2 * STRETCH, window_queries), jnp.float32),
            pltpu.SMEM((1,), jnp.int32),
            pltpu.SemaphoreType.DMA((ctx_count, score_heads)),
            pltpu.SemaphoreType.DMA((blocks,)),
        ]
    spare = TAIL if pieces else 0
    return pl.pallas_call(
        functools.partial(decode_kernel, head0, n, ctx_count, row_count),
        out_shape=[jax.ShapeDtypeStruct((n * (per_dest + TAIL) + spare, HD), jnp.bfloat16)] * ctx_count
        + window_outs,
        grid_spec=pltpu.PrefetchScalarGridSpec(
            num_scalar_prefetch=2,
            grid=(),
            in_specs=[any_space] * (6 + len(pieces)),
            out_specs=[vmem] * (ctx_count + len(window_outs)),
            scratch_shapes=[
                pltpu.VMEM((n, local_rows, per_row, HD), jnp.bfloat16),
                pltpu.VMEM((slots, STRETCH, HD), jnp.bfloat16),
                pltpu.VMEM((slots, STRETCH, HD), jnp.bfloat16),
                pltpu.VMEM((extra, HD), jnp.bfloat16),
                pltpu.VMEM((extra, HD), jnp.bfloat16),
                pltpu.VMEM((1, queries), jnp.float32),
                pltpu.VMEM((8, queries), jnp.float32),
                pltpu.VMEM((HD, queries), jnp.float32),
                pltpu.VMEM((2, 2 * STRETCH, chunk), jnp.float32),
                pltpu.SMEM((n, 2), jnp.int32),
                pltpu.SemaphoreType.DMA((n,)),
                pltpu.SemaphoreType.DMA((slots,)),
                pltpu.SemaphoreType.DMA((slots,)),
                pltpu.SemaphoreType.DMA((4,)),
            ]
            + window_scratch,
        ),
        cost_estimate=pl.CostEstimate(
            flops=n * 8 * queries * STRETCH * HD * 4,
            bytes_accessed=n * 8 * STRETCH * HD * 4,
            transcendentals=n * 8 * queries * STRETCH,
        ),
        name="decode",
    )(keep, order, q, keys, values, own_k, own_v, after, *pieces)


def combine_kernel(head0, n, ctx_count, heads, here, score_heads, keep_ref, *refs):
    parts = refs[:ctx_count]
    if head0:
        share_ref, _, score_ref, out_ref, buf, sem = refs[ctx_count:]
    else:
        sum_ref, share_ref, out_ref, buf, sem = refs[ctx_count:]
    per_row = out_ref.shape[2]
    order = head_order(keep_ref, here)
    per_dest = buf.shape[1] * per_row
    step = min(128, per_dest)
    lines = max(1, per_dest // 128)
    copies = []
    for at in range(n):
        row0 = at * (per_dest + TAIL)
        tiles = [part[pl.ds(row0 + per_dest, TAIL)].astype(jnp.float32) for part in parts]
        for b in range(per_dest // step):
            lses = [line_of(tile, lines, b) for tile in tiles]
            if step == 128:
                top = functools.reduce(jnp.maximum, lses)
                weights = [jnp.exp2(x - top) for x in lses]
                inverse = 1.0 / functools.reduce(jnp.add, weights)
                shares = [jnp.broadcast_to(x * inverse, (128, HD)).T for x in weights]
            else:
                turned_lses = [
                    jnp.broadcast_to(x, (128, HD)).T[k * per_dest % 128 : k * per_dest % 128 + step]
                    for k, x in enumerate(lses)
                ]
                top = functools.reduce(jnp.maximum, turned_lses)
                weights = [jnp.exp2(x - top) for x in turned_lses]
                inverse = 1.0 / functools.reduce(jnp.add, weights)
                shares = [x * inverse for x in weights]
            total = None
            for part, share in zip(parts, shares):
                term = part[pl.ds(row0 + b * step, step)].astype(jnp.float32) * share
                total = term if total is None else total + term
            rows = step // per_row
            buf[at, pl.ds(b * rows, rows)] = total.reshape(rows, per_row, HD).astype(jnp.bfloat16)
        copies.append(pltpu.make_async_copy(buf.at[at], out_ref.at[:, order[head0 + at]], sem.at[at]))
        copies[-1].start()
    if head0:
        tiles = [part[pl.ds(part.shape[0] - TAIL, TAIL)].astype(jnp.float32) for part in parts]
        queries = share_ref.shape[2]
        count = queries // 128
        for g in range(score_heads):
            lses = [
                jnp.concatenate(
                    [line_of(tile, score_heads * count, g * count + i) for i in range(count)], axis=1
                )
                for tile in tiles
            ]
            top = functools.reduce(jnp.maximum, lses)
            whole = functools.reduce(jnp.add, [jnp.exp2(x - top) for x in lses])
            shares = share_ref[g] * (jnp.exp2(lses[0] - top) / whole)
            column = jnp.sum(shares, axis=1, keepdims=True)
            eye = lax.broadcasted_iota(jnp.int32, (here, here), 0) == lax.broadcasted_iota(
                jnp.int32, (here, here), 1
            )
            score_ref[pl.ds(g, 1)] = jnp.sum(jnp.where(eye, column, 0.0), axis=0, keepdims=True)
    else:
        for g in range(score_heads):
            sums = jnp.sum(sum_ref[g], axis=1)
            share_ref[g] = sums / jnp.sum(sums, axis=0, keepdims=True)
    for copy in copies:
        copy.wait()


def local(keys, values, window_q, keep_stretches, dec_q, dec_k, dec_v, row_order):
    ctx_count = lax.axis_size("ctx")
    row_count = lax.axis_size("rows")
    heads = keys.shape[1] // HD
    here = keys.shape[0] // STRETCH
    rows_total, steps = dec_q.shape[:2]
    score_heads = heads // row_count
    shifts = range(1, ctx_count)

    def shifted(x, k):
        pairs = [(i, int(partner(i, k, ctx_count))) for i in range(ctx_count)]
        return lax.ppermute(x, "ctx", pairs)

    def spread(parts):
        return [parts[0]] + [shifted(parts[k], k) for k in range(1, ctx_count)]

    w_each = window_q.shape[0]
    tiles = window_q.reshape(w_each, heads * GROUP, HD).transpose(1, 0, 2)
    tiles = tiles.reshape(heads * GROUP * w_each, HD)
    pieces = spread([tiles] * ctx_count)

    def rows_first(x):
        x = x.reshape(rows_total, steps, -1, HD).transpose(0, 2, 1, 3)
        return x.reshape(-1, HD)

    q = rows_first(dec_q).reshape(rows_total, heads, GROUP * steps, HD)
    own_k, own_v = rows_first(dec_k), rows_first(dec_v)

    def decoded_part(head0, n, after, pieces):
        return decode(
            head0,
            n,
            ctx_count,
            row_count,
            keep_stretches,
            row_order,
            q,
            keys,
            values,
            own_k,
            own_v,
            after,
            pieces,
        )

    many = heads - 1
    first_parts = spread(decoded_part(0, many, row_order, []))
    *second, sums = decoded_part(many, 1, first_parts[0], pieces)
    second_parts = spread(second)

    rows_each = rows_total // (ctx_count * row_count)
    per_row = GROUP * steps
    vmem = pl.BlockSpec(memory_space=pltpu.VMEM)
    smem = pl.BlockSpec(memory_space=pltpu.SMEM)
    any_space = pl.BlockSpec(memory_space=pl.ANY)
    out_shape = jax.ShapeDtypeStruct((rows_each, heads, per_row, HD), jnp.bfloat16)

    def scratch(n):
        return [pltpu.VMEM((n, rows_each, per_row, HD), jnp.bfloat16), pltpu.SemaphoreType.DMA((n,))]

    shares, begun = pl.pallas_call(
        functools.partial(combine_kernel, 0, many, ctx_count, heads, here, score_heads),
        out_shape=[jax.ShapeDtypeStruct((score_heads, here, W * GROUP), jnp.float32), out_shape],
        in_specs=[smem] + [vmem] * (ctx_count + 1),
        out_specs=[vmem, any_space],
        scratch_shapes=scratch(many),
        cost_estimate=pl.CostEstimate(flops=10**6, bytes_accessed=10**7, transcendentals=0),
        name="combine_many",
    )(keep_stretches, *first_parts, sums)
    stretch_scores, decoded = pl.pallas_call(
        functools.partial(combine_kernel, many, 1, ctx_count, heads, here, score_heads),
        out_shape=[jax.ShapeDtypeStruct((score_heads, here), jnp.float32), out_shape],
        in_specs=[smem] + [vmem] * (ctx_count + 1) + [any_space],
        out_specs=[vmem, any_space],
        scratch_shapes=scratch(1),
        input_output_aliases={ctx_count + 2: 1},
        name="combine_one",
    )(keep_stretches, *second_parts, shares, begun)
    decoded = decoded.reshape(rows_each, heads * GROUP, steps, HD).transpose(0, 2, 1, 3)
    return (stretch_scores, decoded.reshape(rows_each, steps, heads * GROUP * HD))


def solution(mesh):
    placed = (
        P(("groups", "ctx"), "head"),
        P(("groups", "ctx"), "head"),
        P(("groups", "ctx"), "head"),
        P(("groups", "head"), None),
        P("groups", None, "head"),
        P("groups", None, "head"),
        P("groups", None, "head"),
        P("groups"),
    )
    return jax.shard_map(
        local,
        mesh=mesh,
        in_specs=placed,
        out_specs=(
            P(("groups", "head", "rows"), "ctx"),
            P(("groups", "ctx", "rows"), None, "head"),
        ),
        check_vma=False,
    )
```

```python
import functools
import math

import jax
import jax.numpy as jnp
from jax import lax
from jax.experimental import pallas as pl
from jax.experimental.pallas import tpu as pltpu
from jax.sharding import PartitionSpec as P

QH = 64
KVH = 8
HD = 128
STRETCH = 512
W = 32
GROUP = QH // KVH

FILL = -1.0e30
LIMIT = 1.0e30
SCALE2 = HD ** (-0.5) * math.log2(math.e)
NT = (((1,), (1,)), ((), ()))
TAIL = 16
ONES = 16


def head_order(keep_ref, here):
    heads, keep_count = keep_ref.shape
    full = [keep_ref[h, keep_count // 2] // here for h in range(heads)]
    last = jnp.int32(0)
    best = jnp.int32(-1)
    for h in range(heads):
        same = sum((full[h] == other).astype(jnp.int32) for other in full)
        last = jnp.where(same > best, h, last)
        best = jnp.maximum(same, best)
    return [h + (last <= h).astype(jnp.int32) for h in range(heads - 1)] + [last]


def terms(lines):
    high = [x.astype(jnp.bfloat16).astype(jnp.float32) for x in lines]
    mid = [(x - y).astype(jnp.bfloat16).astype(jnp.float32) for x, y in zip(lines, high)]
    low = [x - y - z for x, y, z in zip(lines, high, mid)]
    spare = jnp.zeros((TAIL - 3 * len(lines), lines[0].shape[1]), jnp.float32)
    return jnp.concatenate(high + mid + low + [spare], axis=0).astype(jnp.bfloat16)


def line_of(tile, count, at):
    return tile[at : at + 1] + tile[count + at : count + at + 1] + tile[2 * count + at : 2 * count + at + 1]


def partner(own_index, k, ctx_count):
    assert ctx_count & (ctx_count - 1) == 0
    return own_index ^ k


def pick(options, at):
    value = options[-1]
    for i in range(len(options) - 2, -1, -1):
        value = jnp.where(at == i, options[i], value)
    return value


def window_part(pieces, k_hbm, sum_ref, scratch):
    m_ref, q_buf, k_buf, s_buf, flag, q_sem, k_sem = scratch
    ctx_count = len(pieces)
    score_heads = q_buf.shape[0]
    own_index = lax.axis_index("ctx")
    row_index = lax.axis_index("rows")
    is_last = own_index == ctx_count - 1
    per_block = k_buf.shape[1] // STRETCH
    span = k_buf.shape[1]
    blocks = k_hbm.shape[0] // span
    per_piece = q_buf.shape[2]
    queries = per_piece * ctx_count
    w_each = W // ctx_count

    def piece_copies():
        copies = []
        for k, piece in enumerate(pieces):
            source = partner(own_index, k, ctx_count) if k else own_index
            for g in range(score_heads):
                row0 = (row_index * score_heads + g) * per_piece
                rows = pl.ds(pl.multiple_of(row0, TAIL), per_piece)
                copies.append(
                    pltpu.make_async_copy(piece.at[rows], q_buf.at[g, source], q_sem.at[k, g])
                )
        return copies

    for copy in piece_copies():
        copy.start()
    for g in range(score_heads):
        cols = pl.ds(pl.multiple_of((row_index * score_heads + g) * HD, HD), HD)
        for b in range(blocks):
            pltpu.make_async_copy(
                k_hbm.at[pl.ds(b * span, span), cols], k_buf.at[g * blocks + b], k_sem.at[g * blocks + b]
            ).start()
    def run():
        for copy in piece_copies():
            copy.wait()

        def scores(g, keys):
            q = q_buf[g].reshape(queries, HD)
            return lax.dot_general(keys, q, NT, preferred_element_type=jnp.float32)

        row = lax.broadcasted_iota(jnp.int32, (W, queries), 0)
        col = lax.broadcasted_iota(jnp.int32, (W, queries), 1)
        w = (col // per_piece) * w_each + lax.rem(col, w_each)
        allowed = (row <= w) | jnp.logical_not(is_last)

        for g in range(score_heads):
            pltpu.make_async_copy(k_buf.at[g * blocks], k_buf.at[g * blocks], k_sem.at[g * blocks]).wait()
            s = scores(g, k_buf[g * blocks, pl.ds(0, 128)])
            m_ref[pl.ds(g, 1)] = jnp.max(s, axis=0, keepdims=True) * SCALE2
        flag[0] = jnp.int32(1)

        @pl.loop(0, 2)
        def _(attempt):
            @pl.when((attempt == 1) & (flag[0] > 0))
            def _():
                for g in range(score_heads):

                    @pl.loop(0, blocks * per_block)
                    def _(c):
                        keys = k_buf[g * blocks + c // per_block, pl.ds(lax.rem(c, per_block) * STRETCH, STRETCH)]
                        s = scores(g, keys)
                        tail = jnp.where(allowed | (c + 1 < blocks * per_block), s[STRETCH - W :], FILL)
                        s = jnp.concatenate([s[: STRETCH - W], tail], axis=0)
                        peak = jnp.max(s, axis=0, keepdims=True) * SCALE2
                        m_ref[pl.ds(g, 1)] = jnp.maximum(m_ref[pl.ds(g, 1)], peak)

            @pl.when(flag[0] > 0)
            def _():
                for g in range(score_heads):
                    s_buf[0] = scores(g, k_buf[g * blocks, pl.ds(0, 2 * STRETCH)])

                    @pl.loop(0, blocks)
                    def _(b):
                        more = b + 1 < blocks

                        @pl.when(more & (attempt == 0))
                        def _():
                            at = g * blocks + b + 1
                            pltpu.make_async_copy(k_buf.at[at], k_buf.at[at], k_sem.at[at]).wait()

                        following = g * blocks + jnp.where(more, b + 1, b)
                        m = m_ref[pl.ds(g, 1)]
                        for i in range(per_block // 2):
                            if i + 1 < per_block // 2:
                                keys = k_buf[g * blocks + b, pl.ds((i + 1) * 2 * STRETCH, 2 * STRETCH)]
                            else:
                                keys = k_buf[following, pl.ds(0, 2 * STRETCH)]
                            s_buf[(i + 1) % 2] = scores(g, keys)
                            for half in range(2):
                                s = s_buf[i % 2, pl.ds(half * STRETCH, STRETCH)]
                                if i == per_block // 2 - 1 and half == 1:
                                    tail = jnp.where(allowed | more, s[STRETCH - W :], FILL)
                                    s = jnp.concatenate([s[: STRETCH - W], tail], axis=0)
                                p = jnp.exp2(s * SCALE2 - m)
                                sum_ref[g, b * per_block + 2 * i + half] = jnp.sum(
                                    p.reshape(STRETCH // 8, 8, queries), axis=0
                                )

                worst = jnp.max(jnp.where(sum_ref[...] < LIMIT, 0.0, 1.0))
                flag[0] = (worst > 0.0).astype(jnp.int32)

        lines = []
        for g in range(score_heads):
            total = jnp.sum(jnp.sum(sum_ref[g], axis=0), axis=0, keepdims=True)
            lse = m_ref[pl.ds(g, 1)] + jnp.log2(total)
            lines += [lse[:, at : at + 128] for at in range(0, queries, 128)]
        return lines

    return run


def decode_kernel(
    head0,
    count_here,
    ctx_count,
    row_count,
    keep_ref,
    order_ref,
    q_hbm,
    k_hbm,
    v_hbm,
    own_k_hbm,
    own_v_hbm,
    after_ref,
    *rest,
):
    run_window = None
    if head0:
        pieces, rest = rest[:ctx_count], rest[ctx_count:]
        run_window = window_part(pieces, k_hbm, rest[ctx_count], rest[-7:])
        rest = rest[:ctx_count] + rest[ctx_count + 1 : -7]
    outs = rest[:ctx_count]
    (q_buf, k_buf, v_buf, kx_buf, vx_buf, m_ref, l_ref, acc_ref, s_buf, note, q_sem, k_sem, v_sem, x_sem) = rest[
        ctx_count:
    ]
    keep_count = keep_ref.shape[1]
    here = k_hbm.shape[0] // STRETCH
    own_index = lax.axis_index("ctx")
    row_index = lax.axis_index("rows")
    is_last = own_index == ctx_count - 1
    base = own_index * here
    rows_total, heads, per_row, _ = q_hbm.shape
    rows_each = rows_total // (ctx_count * row_count)
    local_rows = rows_each * ctx_count
    queries = local_rows * per_row
    chunk = min(256, queries)
    firsts = list(range(0, queries, chunk))
    own_keys = own_k_hbm.shape[0]
    steps = own_keys // (rows_total * heads)
    extra = kx_buf.shape[0]
    order = head_order(keep_ref, here)[head0 : head0 + count_here]
    per_dest = queries // ctx_count
    out_rows = per_dest + TAIL

    def row_at(j):
        k = j // rows_each
        i = lax.rem(j, rows_each)
        dest = partner(own_index, k, ctx_count)
        return order_ref[dest * (row_count * rows_each) + row_index * rows_each + i]

    all_heads = q_buf.shape[0] == heads

    @pl.loop(0, local_rows)
    def _(j):
        row = row_at(j)
        if all_heads:
            pltpu.make_async_copy(q_hbm.at[row], q_buf.at[:, j], q_sem.at[0]).start()
        else:
            pltpu.make_async_copy(q_hbm.at[row, order[0]], q_buf.at[0, j], q_sem.at[0]).start()

    for at in range(count_here):
        start = jnp.int32(0)
        count = jnp.int32(0)
        for i in range(keep_count):
            local = keep_ref[order[at], i] - base
            start = start + (local < 0).astype(jnp.int32)
            count = count + ((local >= 0) & (local < here)).astype(jnp.int32)
        note[at, 0] = start
        note[at, 1] = count

    def unit_copies(at, h, u):
        local = keep_ref[h, note[at, 0] + u] - base
        rows = pl.ds(pl.multiple_of(local * STRETCH, STRETCH), STRETCH)
        cols = pl.ds(pl.multiple_of(h * HD, HD), HD)
        slot = at * here + u
        return (
            pltpu.make_async_copy(k_hbm.at[rows, cols], k_buf.at[slot], k_sem.at[slot]),
            pltpu.make_async_copy(v_hbm.at[rows, cols], v_buf.at[slot], v_sem.at[slot]),
        )

    def wait_slot(buf, sem, slot):
        pltpu.make_async_copy(buf.at[slot], buf.at[slot], sem.at[slot]).wait()

    for at in range(count_here):

        @pl.loop(0, note[at, 1])
        def _(u):
            for copy in unit_copies(at, order[at], u):
                copy.start()

    def own_copies():
        return (
            pltpu.make_async_copy(own_k_hbm, kx_buf.at[pl.ds(0, own_keys)], x_sem.at[0]),
            pltpu.make_async_copy(own_v_hbm, vx_buf.at[pl.ds(0, own_keys)], x_sem.at[1]),
        )

    def tail_copies(h):
        tail = pl.ds(k_hbm.shape[0] - W, W)
        cols = pl.ds(pl.multiple_of(h * HD, HD), HD)
        return (
            pltpu.make_async_copy(k_hbm.at[tail, cols], kx_buf.at[pl.ds(own_keys, W)], x_sem.at[2]),
            pltpu.make_async_copy(v_hbm.at[tail, cols], vx_buf.at[pl.ds(own_keys, W)], x_sem.at[3]),
        )

    @pl.when(is_last)
    def _():
        spare = extra - own_keys - W
        kx_buf[pl.ds(own_keys + W, spare)] = jnp.zeros((spare, HD), jnp.bfloat16)
        vx_buf[pl.ds(own_keys + W, spare)] = jnp.zeros((spare, HD), jnp.bfloat16)
        for copy in own_copies():
            copy.start()
        for copy in own_copies():
            copy.wait()

    def turned(v):
        return jnp.concatenate([v.T, jnp.ones((ONES, v.shape[0]), jnp.bfloat16)], axis=0)

    def fold(sl, vt, s):
        old = m_ref[:, sl]
        new = jnp.maximum(old, jnp.max(s, axis=0, keepdims=True))
        alpha = jnp.exp2(old - new)
        t = jnp.dot(vt, jnp.exp2(s - new).astype(jnp.bfloat16), preferred_element_type=jnp.float32)
        l_ref[:, sl] = l_ref[:, sl] * alpha + t[HD : HD + 8]
        acc_ref[:, sl] = acc_ref[:, sl] * alpha + t[:HD]
        m_ref[:, sl] = new

    def attend(at):
        h = pick(order, at)
        count = note[at, 1]
        pairs = count // 2
        slot0 = at * here

        @pl.when(is_last)
        def _():
            for copy in tail_copies(h):
                copy.start()

        slab = h if all_heads else 0

        def q_of(first):
            j0 = first // per_row
            return q_buf[slab, pl.ds(j0, chunk // per_row)].reshape(chunk, HD)

        def scores(keys, first):
            return lax.dot_general(keys, q_of(first), NT, preferred_element_type=jnp.float32)

        def pair(buf, b):
            return buf[pl.ds(slot0 + 2 * b, 2)].reshape(2 * STRETCH, HD)

        def fast(sl, vt, s):
            p = jnp.exp2(s * SCALE2 - m_ref[:, sl]).astype(jnp.bfloat16)
            t = jnp.dot(vt, p, preferred_element_type=jnp.float32)
            l_ref[:, sl] += t[HD : HD + 8]
            acc_ref[:, sl] += t[:HD]

        l_ref[...] = jnp.zeros(l_ref.shape, jnp.float32)
        acc_ref[...] = jnp.zeros(acc_ref.shape, jnp.float32)

        @pl.when(count == 0)
        def _():
            m_ref[...] = jnp.full(m_ref.shape, FILL, jnp.float32)

        @pl.when(count > 0)
        def _():
            wait_slot(k_buf, k_sem, slot0)
            for first in firsts:
                s = scores(k_buf[slot0, pl.ds(0, 128)], first)
                m_ref[:, pl.ds(first, chunk)] = jnp.max(s, axis=0, keepdims=True) * SCALE2

        @pl.when(pairs > 0)
        def _():
            wait_slot(k_buf, k_sem, slot0 + 1)
            s_buf[0] = scores(pair(k_buf, 0), firsts[0])

            @pl.loop(0, pairs)
            def _(b):
                more = b + 1 < pairs
                wait_slot(v_buf, v_sem, slot0 + 2 * b)
                wait_slot(v_buf, v_sem, slot0 + 2 * b + 1)

                @pl.when(more)
                def _():
                    wait_slot(k_buf, k_sem, slot0 + 2 * b + 2)
                    wait_slot(k_buf, k_sem, slot0 + 2 * b + 3)

                following = jnp.where(more, b + 1, b)
                vt = turned(pair(v_buf, b))
                for i, first in enumerate(firsts):
                    if i + 1 < len(firsts):
                        s_buf[(i + 1) % 2] = scores(pair(k_buf, b), firsts[i + 1])
                    else:
                        s_buf[(i + 1) % 2] = scores(pair(k_buf, following), firsts[0])
                    fast(pl.ds(first, chunk), vt, s_buf[i % 2])

        @pl.when(count > 2 * pairs)
        def _():
            slot = slot0 + 2 * pairs

            @pl.when(pairs > 0)
            def _():
                wait_slot(k_buf, k_sem, slot)

            wait_slot(v_buf, v_sem, slot)
            vt = turned(v_buf[slot])
            s = scores(k_buf[slot], firsts[0])
            for i, first in enumerate(firsts):
                ahead = scores(k_buf[slot], firsts[i + 1]) if i + 1 < len(firsts) else None
                fast(pl.ds(first, chunk), vt, s)
                s = ahead

        bad = jnp.max(jnp.where(l_ref[...] < LIMIT, 0.0, 1.0))

        @pl.when(bad > 0.0)
        def _():
            l_ref[...] = jnp.zeros(l_ref.shape, jnp.float32)
            acc_ref[...] = jnp.zeros(acc_ref.shape, jnp.float32)
            m_ref[...] = jnp.full(m_ref.shape, FILL, jnp.float32)

            @pl.loop(0, count)
            def _(u):
                vt = turned(v_buf[slot0 + u])
                for first in firsts:
                    fold(pl.ds(first, chunk), vt, scores(k_buf[slot0 + u], first) * SCALE2)

        @pl.when(is_last)
        def _():
            for copy in tail_copies(h):
                copy.wait()
            vt = turned(vx_buf[...])
            key = lax.broadcasted_iota(jnp.int32, (extra, chunk), 0)
            lane = lax.broadcasted_iota(jnp.int32, (1, chunk), 1)
            window = (key >= own_keys) & (key < own_keys + W)
            for first in firsts:
                line = jnp.zeros((1, chunk), jnp.int32)
                for j in range(chunk // per_row):
                    line = jnp.where(lane // per_row == j, row_at(first // per_row + j), line)
                low = line * (heads * steps) + h * steps
                high = low + lax.rem(lane, steps)
                mask = ((key >= low) & (key <= high)) | window
                s = scores(kx_buf[...], first) * SCALE2
                fold(pl.ds(first, chunk), vt, jnp.where(mask, s, FILL))

        total = l_ref[0:1]
        some = total > 0.0
        safe = jnp.where(some, total, 1.0)
        lse = jnp.where(some, m_ref[...] + jnp.log2(safe), FILL)
        inverse = 1.0 / safe
        lines = max(1, per_dest // 128)
        row0 = pl.multiple_of(at * out_rows, TAIL)
        for b in range(queries // 128):
            sl = slice(b * 128, (b + 1) * 128)
            block = (acc_ref[:, sl] * inverse[:, sl]).T.astype(jnp.bfloat16)
            step = min(128, per_dest)
            for piece in range(128 // step):
                at_row = b * 128 + piece * step
                outs[at_row // per_dest][pl.ds(row0 + at_row % per_dest, step)] = block[
                    piece * step : (piece + 1) * step
                ]
        for k in range(ctx_count):
            b0 = k * per_dest // 128
            lse_lines = [lse[:, (b0 + i) * 128 : (b0 + i + 1) * 128] for i in range(lines)]
            outs[k][pl.ds(row0 + per_dest, TAIL)] = terms(lse_lines)

    if run_window is not None:
        tile = terms(run_window())
        for out in outs:
            out[pl.ds(count_here * out_rows, TAIL)] = tile

    pltpu.make_async_copy(q_buf, q_buf, q_sem.at[0]).wait()

    def empty(at):
        for out in outs:
            row0 = pl.multiple_of(at * out_rows, TAIL)
            out[pl.ds(row0, per_dest)] = jnp.zeros((per_dest, HD), jnp.bfloat16)
            out[pl.ds(row0 + per_dest, TAIL)] = terms(
                [jnp.full((1, HD), FILL, jnp.float32)] * max(1, per_dest // 128)
            )

    @pl.loop(0, count_here)
    def _(at):
        active = (note[at, 1] > 0) | is_last
        pl.when(active)(functools.partial(attend, at))
        pl.when(jnp.logical_not(active))(functools.partial(empty, at))


def decode(head0, n, ctx_count, row_count, keep, order, q, keys, values, own_k, own_v, after, pieces):
    rows_total, heads, per_row, _ = q.shape
    local_rows = rows_total // row_count
    queries = local_rows * per_row
    chunk = min(256, queries)
    per_dest = queries // ctx_count
    here = keys.shape[0] // STRETCH
    extra = pl.cdiv(own_k.shape[0] + W, HD) * HD
    slots = n * here
    any_space = pl.BlockSpec(memory_space=pl.ANY)
    vmem = pl.BlockSpec(memory_space=pltpu.VMEM)
    score_heads = heads // row_count
    window_queries = W * GROUP
    window_outs, window_scratch = [], []
    if pieces:
        per_block = math.gcd(here, 8)
        blocks = score_heads * here // per_block
        window_outs = [jax.ShapeDtypeStruct((score_heads, here, 8, window_queries), jnp.float32)]
        window_scratch = [
            pltpu.VMEM((score_heads, window_queries), jnp.float32),
            pltpu.VMEM((score_heads, ctx_count, window_queries // ctx_count, HD), jnp.bfloat16),
            pltpu.VMEM((blocks, per_block * STRETCH, HD), jnp.bfloat16),
            pltpu.VMEM((2, 2 * STRETCH, window_queries), jnp.float32),
            pltpu.SMEM((1,), jnp.int32),
            pltpu.SemaphoreType.DMA((ctx_count, score_heads)),
            pltpu.SemaphoreType.DMA((blocks,)),
        ]
    spare = TAIL if pieces else 0
    return pl.pallas_call(
        functools.partial(decode_kernel, head0, n, ctx_count, row_count),
        out_shape=[jax.ShapeDtypeStruct((n * (per_dest + TAIL) + spare, HD), jnp.bfloat16)] * ctx_count
        + window_outs,
        grid_spec=pltpu.PrefetchScalarGridSpec(
            num_scalar_prefetch=2,
            grid=(),
            in_specs=[any_space] * (6 + len(pieces)),
            out_specs=[vmem] * (ctx_count + len(window_outs)),
            scratch_shapes=[
                pltpu.VMEM((1 if n == 1 else heads, local_rows, per_row, HD), jnp.bfloat16),
                pltpu.VMEM((slots, STRETCH, HD), jnp.bfloat16),
                pltpu.VMEM((slots, STRETCH, HD), jnp.bfloat16),
                pltpu.VMEM((extra, HD), jnp.bfloat16),
                pltpu.VMEM((extra, HD), jnp.bfloat16),
                pltpu.VMEM((1, queries), jnp.float32),
                pltpu.VMEM((8, queries), jnp.float32),
                pltpu.VMEM((HD, queries), jnp.float32),
                pltpu.VMEM((2, 2 * STRETCH, chunk), jnp.float32),
                pltpu.SMEM((n, 2), jnp.int32),
                pltpu.SemaphoreType.DMA((1,)),
                pltpu.SemaphoreType.DMA((slots,)),
                pltpu.SemaphoreType.DMA((slots,)),
                pltpu.SemaphoreType.DMA((4,)),
            ]
            + window_scratch,
        ),
        cost_estimate=pl.CostEstimate(
            flops=n * 8 * queries * STRETCH * HD * 4,
            bytes_accessed=n * 8 * STRETCH * HD * 4,
            transcendentals=n * 8 * queries * STRETCH,
        ),
        name="decode",
    )(keep, order, q, keys, values, own_k, own_v, after, *pieces)


def combine_kernel(head0, n, ctx_count, heads, here, score_heads, keep_ref, *refs):
    parts = refs[:ctx_count]
    if head0:
        share_ref, _, score_ref, out_ref, buf, sem = refs[ctx_count:]
    else:
        sum_ref, share_ref, out_ref, buf, sem = refs[ctx_count:]
    per_row = out_ref.shape[2]
    order = head_order(keep_ref, here)
    per_dest = buf.shape[1] * per_row
    step = min(128, per_dest)
    lines = max(1, per_dest // 128)
    copies = []
    for at in range(n):
        row0 = at * (per_dest + TAIL)
        tiles = [part[pl.ds(row0 + per_dest, TAIL)].astype(jnp.float32) for part in parts]
        for b in range(per_dest // step):
            lses = [line_of(tile, lines, b) for tile in tiles]
            if step == 128:
                top = functools.reduce(jnp.maximum, lses)
                weights = [jnp.exp2(x - top) for x in lses]
                inverse = 1.0 / functools.reduce(jnp.add, weights)
                shares = [jnp.broadcast_to(x * inverse, (128, HD)).T for x in weights]
            else:
                turned_lses = [
                    jnp.broadcast_to(x, (128, HD)).T[k * per_dest % 128 : k * per_dest % 128 + step]
                    for k, x in enumerate(lses)
                ]
                top = functools.reduce(jnp.maximum, turned_lses)
                weights = [jnp.exp2(x - top) for x in turned_lses]
                inverse = 1.0 / functools.reduce(jnp.add, weights)
                shares = [x * inverse for x in weights]
            total = None
            for part, share in zip(parts, shares):
                term = part[pl.ds(row0 + b * step, step)].astype(jnp.float32) * share
                total = term if total is None else total + term
            rows = step // per_row
            buf[at, pl.ds(b * rows, rows)] = total.reshape(rows, per_row, HD).astype(jnp.bfloat16)
        copies.append(pltpu.make_async_copy(buf.at[at], out_ref.at[:, order[head0 + at]], sem.at[at]))
        copies[-1].start()
    if head0:
        tiles = [part[pl.ds(part.shape[0] - TAIL, TAIL)].astype(jnp.float32) for part in parts]
        queries = share_ref.shape[2]
        count = queries // 128
        for g in range(score_heads):
            lses = [
                jnp.concatenate(
                    [line_of(tile, score_heads * count, g * count + i) for i in range(count)], axis=1
                )
                for tile in tiles
            ]
            top = functools.reduce(jnp.maximum, lses)
            whole = functools.reduce(jnp.add, [jnp.exp2(x - top) for x in lses])
            shares = share_ref[g] * (jnp.exp2(lses[0] - top) / whole)
            column = jnp.sum(shares, axis=1, keepdims=True)
            eye = lax.broadcasted_iota(jnp.int32, (here, here), 0) == lax.broadcasted_iota(
                jnp.int32, (here, here), 1
            )
            score_ref[pl.ds(g, 1)] = jnp.sum(jnp.where(eye, column, 0.0), axis=0, keepdims=True)
    else:
        for g in range(score_heads):
            sums = jnp.sum(sum_ref[g], axis=1)
            share_ref[g] = sums / jnp.sum(sums, axis=0, keepdims=True)
    for copy in copies:
        copy.wait()


def local(keys, values, window_q, keep_stretches, dec_q, dec_k, dec_v, row_order):
    ctx_count = lax.axis_size("ctx")
    row_count = lax.axis_size("rows")
    heads = keys.shape[1] // HD
    here = keys.shape[0] // STRETCH
    rows_total, steps = dec_q.shape[:2]
    score_heads = heads // row_count
    shifts = range(1, ctx_count)

    def shifted(x, k):
        pairs = [(i, int(partner(i, k, ctx_count))) for i in range(ctx_count)]
        return lax.ppermute(x, "ctx", pairs)

    def spread(parts):
        return [parts[0]] + [shifted(parts[k], k) for k in range(1, ctx_count)]

    w_each = window_q.shape[0]
    tiles = window_q.reshape(w_each, heads * GROUP, HD).transpose(1, 0, 2)
    tiles = tiles.reshape(heads * GROUP * w_each, HD)
    pieces = spread([tiles] * ctx_count)

    def rows_first(x):
        x = x.reshape(rows_total, steps, -1, HD).transpose(0, 2, 1, 3)
        return x.reshape(-1, HD)

    q = rows_first(dec_q).reshape(rows_total, heads, GROUP * steps, HD)
    own_k, own_v = rows_first(dec_k), rows_first(dec_v)

    def decoded_part(head0, n, after, pieces):
        return decode(
            head0,
            n,
            ctx_count,
            row_count,
            keep_stretches,
            row_order,
            q,
            keys,
            values,
            own_k,
            own_v,
            after,
            pieces,
        )

    many = heads - 1
    first_parts = spread(decoded_part(0, many, row_order, []))
    *second, sums = decoded_part(many, 1, first_parts[0], pieces)
    second_parts = spread(second)

    rows_each = rows_total // (ctx_count * row_count)
    per_row = GROUP * steps
    vmem = pl.BlockSpec(memory_space=pltpu.VMEM)
    smem = pl.BlockSpec(memory_space=pltpu.SMEM)
    any_space = pl.BlockSpec(memory_space=pl.ANY)
    out_shape = jax.ShapeDtypeStruct((rows_each, heads, per_row, HD), jnp.bfloat16)

    def scratch(n):
        return [pltpu.VMEM((n, rows_each, per_row, HD), jnp.bfloat16), pltpu.SemaphoreType.DMA((n,))]

    shares, begun = pl.pallas_call(
        functools.partial(combine_kernel, 0, many, ctx_count, heads, here, score_heads),
        out_shape=[jax.ShapeDtypeStruct((score_heads, here, W * GROUP), jnp.float32), out_shape],
        in_specs=[smem] + [vmem] * (ctx_count + 1),
        out_specs=[vmem, any_space],
        scratch_shapes=scratch(many),
        cost_estimate=pl.CostEstimate(flops=10**6, bytes_accessed=10**7, transcendentals=0),
        compiler_params=pltpu.CompilerParams(vmem_limit_bytes=8 * 2**20),
        name="combine_many",
    )(keep_stretches, *first_parts, sums)
    stretch_scores, decoded = pl.pallas_call(
        functools.partial(combine_kernel, many, 1, ctx_count, heads, here, score_heads),
        out_shape=[jax.ShapeDtypeStruct((score_heads, here), jnp.float32), out_shape],
        in_specs=[smem] + [vmem] * (ctx_count + 1) + [any_space],
        out_specs=[vmem, any_space],
        scratch_shapes=scratch(1),
        input_output_aliases={ctx_count + 2: 1},
        compiler_params=pltpu.CompilerParams(vmem_limit_bytes=8 * 2**20),
        name="combine_one",
    )(keep_stretches, *second_parts, shares, begun)
    decoded = decoded.reshape(rows_each, heads * GROUP, steps, HD).transpose(0, 2, 1, 3)
    return (stretch_scores, decoded.reshape(rows_each, steps, heads * GROUP * HD))


def solution(mesh):
    placed = (
        P(("groups", "ctx"), "head"),
        P(("groups", "ctx"), "head"),
        P(("groups", "ctx"), "head"),
        P(("groups", "head"), None),
        P("groups", None, "head"),
        P("groups", None, "head"),
        P("groups", None, "head"),
        P("groups"),
    )
    return jax.shard_map(
        local,
        mesh=mesh,
        in_specs=placed,
        out_specs=(
            P(("groups", "head", "rows"), "ctx"),
            P(("groups", "ctx", "rows"), None, "head"),
        ),
        check_vma=False,
    )
```

```python
import functools
import math

import jax
import jax.numpy as jnp
from jax import lax
from jax.experimental import pallas as pl
from jax.experimental.pallas import tpu as pltpu
from jax.sharding import PartitionSpec as P

QH = 64
KVH = 8
HD = 128
STRETCH = 512
W = 32
GROUP = QH // KVH

FILL = -1.0e30
LIMIT = 1.0e30
SCALE2 = HD ** (-0.5) * math.log2(math.e)
NT = (((1,), (1,)), ((), ()))
TAIL = 16
ONES = 16


def head_order(keep_ref, here):
    heads, keep_count = keep_ref.shape
    full = [keep_ref[h, keep_count // 2] // here for h in range(heads)]
    last = jnp.int32(0)
    best = jnp.int32(-1)
    for h in range(heads):
        same = sum((full[h] == other).astype(jnp.int32) for other in full)
        last = jnp.where(same > best, h, last)
        best = jnp.maximum(same, best)
    return [h + (last <= h).astype(jnp.int32) for h in range(heads - 1)] + [last]


def terms(lines):
    high = [x.astype(jnp.bfloat16).astype(jnp.float32) for x in lines]
    mid = [(x - y).astype(jnp.bfloat16).astype(jnp.float32) for x, y in zip(lines, high)]
    low = [x - y - z for x, y, z in zip(lines, high, mid)]
    spare = jnp.zeros((TAIL - 3 * len(lines), lines[0].shape[1]), jnp.float32)
    return jnp.concatenate(high + mid + low + [spare], axis=0).astype(jnp.bfloat16)


def line_of(tile, count, at):
    return tile[at : at + 1] + tile[count + at : count + at + 1] + tile[2 * count + at : 2 * count + at + 1]


def partner(own_index, k, ctx_count):
    assert ctx_count & (ctx_count - 1) == 0
    return own_index ^ k


def pick(options, at):
    value = options[-1]
    for i in range(len(options) - 2, -1, -1):
        value = jnp.where(at == i, options[i], value)
    return value


def window_part(pieces, k_hbm, sum_ref, scratch):
    m_ref, q_buf, k_buf, s_buf, flag, q_sem, k_sem = scratch
    ctx_count = len(pieces)
    score_heads = q_buf.shape[0]
    own_index = lax.axis_index("ctx")
    row_index = lax.axis_index("rows")
    is_last = own_index == ctx_count - 1
    per_block = k_buf.shape[1] // STRETCH
    span = k_buf.shape[1]
    blocks = k_hbm.shape[0] // span
    per_piece = q_buf.shape[2]
    queries = per_piece * ctx_count
    w_each = W // ctx_count

    def piece_copies():
        copies = []
        for k, piece in enumerate(pieces):
            source = partner(own_index, k, ctx_count) if k else own_index
            for g in range(score_heads):
                row0 = (row_index * score_heads + g) * per_piece
                rows = pl.ds(pl.multiple_of(row0, TAIL), per_piece)
                copies.append(
                    pltpu.make_async_copy(piece.at[rows], q_buf.at[g, source], q_sem.at[k, g])
                )
        return copies

    for copy in piece_copies():
        copy.start()
    for g in range(score_heads):
        cols = pl.ds(pl.multiple_of((row_index * score_heads + g) * HD, HD), HD)
        for b in range(blocks):
            pltpu.make_async_copy(
                k_hbm.at[pl.ds(b * span, span), cols], k_buf.at[g * blocks + b], k_sem.at[g * blocks + b]
            ).start()
    def run():
        for copy in piece_copies():
            copy.wait()

        def scores(g, keys):
            q = q_buf[g].reshape(queries, HD)
            return lax.dot_general(keys, q, NT, preferred_element_type=jnp.float32)

        row = lax.broadcasted_iota(jnp.int32, (W, queries), 0)
        col = lax.broadcasted_iota(jnp.int32, (W, queries), 1)
        w = (col // per_piece) * w_each + lax.rem(col, w_each)
        allowed = (row <= w) | jnp.logical_not(is_last)

        for g in range(score_heads):
            pltpu.make_async_copy(k_buf.at[g * blocks], k_buf.at[g * blocks], k_sem.at[g * blocks]).wait()
            s = scores(g, k_buf[g * blocks, pl.ds(0, 128)])
            m_ref[pl.ds(g, 1)] = jnp.max(s, axis=0, keepdims=True) * SCALE2
        flag[0] = jnp.int32(1)

        @pl.loop(0, 2)
        def _(attempt):
            @pl.when((attempt == 1) & (flag[0] > 0))
            def _():
                for g in range(score_heads):

                    @pl.loop(0, blocks * per_block)
                    def _(c):
                        keys = k_buf[g * blocks + c // per_block, pl.ds(lax.rem(c, per_block) * STRETCH, STRETCH)]
                        s = scores(g, keys)
                        tail = jnp.where(allowed | (c + 1 < blocks * per_block), s[STRETCH - W :], FILL)
                        s = jnp.concatenate([s[: STRETCH - W], tail], axis=0)
                        peak = jnp.max(s, axis=0, keepdims=True) * SCALE2
                        m_ref[pl.ds(g, 1)] = jnp.maximum(m_ref[pl.ds(g, 1)], peak)

            @pl.when(flag[0] > 0)
            def _():
                for g in range(score_heads):
                    s_buf[0] = scores(g, k_buf[g * blocks, pl.ds(0, 2 * STRETCH)])

                    @pl.loop(0, blocks)
                    def _(b):
                        more = b + 1 < blocks

                        @pl.when(more & (attempt == 0))
                        def _():
                            at = g * blocks + b + 1
                            pltpu.make_async_copy(k_buf.at[at], k_buf.at[at], k_sem.at[at]).wait()

                        following = g * blocks + jnp.where(more, b + 1, b)
                        m = m_ref[pl.ds(g, 1)]
                        for i in range(per_block // 2):
                            if i + 1 < per_block // 2:
                                keys = k_buf[g * blocks + b, pl.ds((i + 1) * 2 * STRETCH, 2 * STRETCH)]
                            else:
                                keys = k_buf[following, pl.ds(0, 2 * STRETCH)]
                            s_buf[(i + 1) % 2] = scores(g, keys)
                            for half in range(2):
                                s = s_buf[i % 2, pl.ds(half * STRETCH, STRETCH)]
                                if i == per_block // 2 - 1 and half == 1:
                                    tail = jnp.where(allowed | more, s[STRETCH - W :], FILL)
                                    s = jnp.concatenate([s[: STRETCH - W], tail], axis=0)
                                p = jnp.exp2(s * SCALE2 - m)
                                sum_ref[g, b * per_block + 2 * i + half] = jnp.sum(
                                    p.reshape(STRETCH // 8, 8, queries), axis=0
                                )

                worst = jnp.max(jnp.where(sum_ref[...] < LIMIT, 0.0, 1.0))
                flag[0] = (worst > 0.0).astype(jnp.int32)

        lines = []
        for g in range(score_heads):
            total = jnp.sum(jnp.sum(sum_ref[g], axis=0), axis=0, keepdims=True)
            lse = m_ref[pl.ds(g, 1)] + jnp.log2(total)
            lines += [lse[:, at : at + 128] for at in range(0, queries, 128)]
        return lines

    return run


def decode_kernel(
    head0,
    count_here,
    ctx_count,
    row_count,
    keep_ref,
    order_ref,
    q_hbm,
    k_hbm,
    v_hbm,
    own_k_hbm,
    own_v_hbm,
    after_ref,
    *rest,
):
    run_window = None
    if head0:
        pieces, rest = rest[:ctx_count], rest[ctx_count:]
        run_window = window_part(pieces, k_hbm, rest[ctx_count], rest[-7:])
        rest = rest[:ctx_count] + rest[ctx_count + 1 : -7]
    outs = rest[:ctx_count]
    (q_buf, k_buf, v_buf, kx_buf, vx_buf, m_ref, l_ref, acc_ref, s_buf, note, q_sem, k_sem, v_sem, x_sem) = rest[
        ctx_count:
    ]
    keep_count = keep_ref.shape[1]
    here = k_hbm.shape[0] // STRETCH
    own_index = lax.axis_index("ctx")
    row_index = lax.axis_index("rows")
    is_last = own_index == ctx_count - 1
    base = own_index * here
    rows_total, heads, per_row, _ = q_hbm.shape
    rows_each = rows_total // (ctx_count * row_count)
    local_rows = rows_each * ctx_count
    queries = local_rows * per_row
    chunk = min(256, queries)
    firsts = list(range(0, queries, chunk))
    own_keys = own_k_hbm.shape[0]
    steps = own_keys // (rows_total * heads)
    extra = kx_buf.shape[0]
    order = head_order(keep_ref, here)[head0 : head0 + count_here]
    per_dest = queries // ctx_count
    out_rows = per_dest + TAIL

    def row_at(j):
        k = j // rows_each
        i = lax.rem(j, rows_each)
        dest = partner(own_index, k, ctx_count)
        return order_ref[dest * (row_count * rows_each) + row_index * rows_each + i]

    all_heads = q_buf.shape[0] == heads

    @pl.loop(0, local_rows)
    def _(j):
        row = row_at(j)
        if all_heads:
            pltpu.make_async_copy(q_hbm.at[row], q_buf.at[:, j], q_sem.at[0]).start()
        else:
            pltpu.make_async_copy(q_hbm.at[row, order[0]], q_buf.at[0, j], q_sem.at[0]).start()

    for at in range(count_here):
        start = jnp.int32(0)
        count = jnp.int32(0)
        for i in range(keep_count):
            local = keep_ref[order[at], i] - base
            start = start + (local < 0).astype(jnp.int32)
            count = count + ((local >= 0) & (local < here)).astype(jnp.int32)
        note[at, 0] = start
        note[at, 1] = count

    def unit_copies(at, h, u):
        local = keep_ref[h, note[at, 0] + u] - base
        rows = pl.ds(pl.multiple_of(local * STRETCH, STRETCH), STRETCH)
        cols = pl.ds(pl.multiple_of(h * HD, HD), HD)
        slot = at * here + u
        return (
            pltpu.make_async_copy(k_hbm.at[rows, cols], k_buf.at[slot], k_sem.at[slot]),
            pltpu.make_async_copy(v_hbm.at[rows, cols], v_buf.at[slot], v_sem.at[slot]),
        )

    def wait_slot(buf, sem, slot):
        pltpu.make_async_copy(buf.at[slot], buf.at[slot], sem.at[slot]).wait()

    for at in range(count_here):

        @pl.loop(0, note[at, 1])
        def _(u):
            for copy in unit_copies(at, order[at], u):
                copy.start()

    def own_copies():
        return (
            pltpu.make_async_copy(own_k_hbm, kx_buf.at[pl.ds(0, own_keys)], x_sem.at[0]),
            pltpu.make_async_copy(own_v_hbm, vx_buf.at[pl.ds(0, own_keys)], x_sem.at[1]),
        )

    def tail_copies(h):
        tail = pl.ds(k_hbm.shape[0] - W, W)
        cols = pl.ds(pl.multiple_of(h * HD, HD), HD)
        return (
            pltpu.make_async_copy(k_hbm.at[tail, cols], kx_buf.at[pl.ds(own_keys, W)], x_sem.at[2]),
            pltpu.make_async_copy(v_hbm.at[tail, cols], vx_buf.at[pl.ds(own_keys, W)], x_sem.at[3]),
        )

    @pl.when(is_last)
    def _():
        spare = extra - own_keys - W
        kx_buf[pl.ds(own_keys + W, spare)] = jnp.zeros((spare, HD), jnp.bfloat16)
        vx_buf[pl.ds(own_keys + W, spare)] = jnp.zeros((spare, HD), jnp.bfloat16)
        for copy in own_copies():
            copy.start()
        for copy in own_copies():
            copy.wait()

    def turned(v):
        return jnp.concatenate([v.T, jnp.ones((ONES, v.shape[0]), jnp.bfloat16)], axis=0)

    def fold(sl, vt, s):
        old = m_ref[:, sl]
        new = jnp.maximum(old, jnp.max(s, axis=0, keepdims=True))
        alpha = jnp.exp2(old - new)
        t = jnp.dot(vt, jnp.exp2(s - new).astype(jnp.bfloat16), preferred_element_type=jnp.float32)
        l_ref[:, sl] = l_ref[:, sl] * alpha + t[HD : HD + 8]
        acc_ref[:, sl] = acc_ref[:, sl] * alpha + t[:HD]
        m_ref[:, sl] = new

    def attend(at):
        h = pick(order, at)
        count = note[at, 1]
        pairs = count // 2
        slot0 = at * here

        @pl.when(is_last)
        def _():
            for copy in tail_copies(h):
                copy.start()

        slab = h if all_heads else 0

        def q_of(first):
            j0 = first // per_row
            return q_buf[slab, pl.ds(j0, chunk // per_row)].reshape(chunk, HD)

        def scores(keys, first):
            return lax.dot_general(keys, q_of(first), NT, preferred_element_type=jnp.float32)

        def pair(buf, b):
            return buf[pl.ds(slot0 + 2 * b, 2)].reshape(2 * STRETCH, HD)

        def fast(sl, vt, s):
            p = jnp.exp2(s * SCALE2 - m_ref[:, sl]).astype(jnp.bfloat16)
            t = jnp.dot(vt, p, preferred_element_type=jnp.float32)
            l_ref[:, sl] += t[HD : HD + 8]
            acc_ref[:, sl] += t[:HD]

        l_ref[...] = jnp.zeros(l_ref.shape, jnp.float32)
        acc_ref[...] = jnp.zeros(acc_ref.shape, jnp.float32)

        @pl.when(count == 0)
        def _():
            m_ref[...] = jnp.full(m_ref.shape, FILL, jnp.float32)

        @pl.when(count > 0)
        def _():
            wait_slot(k_buf, k_sem, slot0)
            for first in firsts:
                s = scores(k_buf[slot0, pl.ds(0, 128)], first)
                m_ref[:, pl.ds(first, chunk)] = jnp.max(s, axis=0, keepdims=True) * SCALE2

        @pl.when(pairs > 0)
        def _():
            wait_slot(k_buf, k_sem, slot0 + 1)
            s_buf[0] = scores(pair(k_buf, 0), firsts[0])

            @pl.loop(0, pairs)
            def _(b):
                more = b + 1 < pairs
                wait_slot(v_buf, v_sem, slot0 + 2 * b)
                wait_slot(v_buf, v_sem, slot0 + 2 * b + 1)

                @pl.when(more)
                def _():
                    wait_slot(k_buf, k_sem, slot0 + 2 * b + 2)
                    wait_slot(k_buf, k_sem, slot0 + 2 * b + 3)

                following = jnp.where(more, b + 1, b)
                vt = turned(pair(v_buf, b))
                for i, first in enumerate(firsts):
                    if i + 1 < len(firsts):
                        s_buf[(i + 1) % 2] = scores(pair(k_buf, b), firsts[i + 1])
                    else:
                        s_buf[(i + 1) % 2] = scores(pair(k_buf, following), firsts[0])
                    fast(pl.ds(first, chunk), vt, s_buf[i % 2])

        @pl.when(count > 2 * pairs)
        def _():
            slot = slot0 + 2 * pairs

            @pl.when(pairs > 0)
            def _():
                wait_slot(k_buf, k_sem, slot)

            wait_slot(v_buf, v_sem, slot)
            vt = turned(v_buf[slot])
            s = scores(k_buf[slot], firsts[0])
            for i, first in enumerate(firsts):
                ahead = scores(k_buf[slot], firsts[i + 1]) if i + 1 < len(firsts) else None
                fast(pl.ds(first, chunk), vt, s)
                s = ahead

        bad = jnp.max(jnp.where(l_ref[...] < LIMIT, 0.0, 1.0))

        @pl.when(bad > 0.0)
        def _():
            l_ref[...] = jnp.zeros(l_ref.shape, jnp.float32)
            acc_ref[...] = jnp.zeros(acc_ref.shape, jnp.float32)
            m_ref[...] = jnp.full(m_ref.shape, FILL, jnp.float32)

            @pl.loop(0, count)
            def _(u):
                vt = turned(v_buf[slot0 + u])
                for first in firsts:
                    fold(pl.ds(first, chunk), vt, scores(k_buf[slot0 + u], first) * SCALE2)

        @pl.when(is_last)
        def _():
            for copy in tail_copies(h):
                copy.wait()
            vt = turned(vx_buf[...])
            key = lax.broadcasted_iota(jnp.int32, (extra, chunk), 0)
            lane = lax.broadcasted_iota(jnp.int32, (1, chunk), 1)
            window = (key >= own_keys) & (key < own_keys + W)
            for first in firsts:
                line = jnp.zeros((1, chunk), jnp.int32)
                for j in range(chunk // per_row):
                    line = jnp.where(lane // per_row == j, row_at(first // per_row + j), line)
                low = line * (heads * steps) + h * steps
                high = low + lax.rem(lane, steps)
                mask = ((key >= low) & (key <= high)) | window
                s = scores(kx_buf[...], first) * SCALE2
                fold(pl.ds(first, chunk), vt, jnp.where(mask, s, FILL))

        total = l_ref[0:1]
        some = total > 0.0
        safe = jnp.where(some, total, 1.0)
        lse = jnp.where(some, m_ref[...] + jnp.log2(safe), FILL)
        inverse = 1.0 / safe
        lines = max(1, per_dest // 128)
        row0 = pl.multiple_of(at * out_rows, TAIL)
        for b in range(queries // 128):
            sl = slice(b * 128, (b + 1) * 128)
            block = (acc_ref[:, sl] * inverse[:, sl]).T.astype(jnp.bfloat16)
            step = min(128, per_dest)
            for piece in range(128 // step):
                at_row = b * 128 + piece * step
                outs[at_row // per_dest][pl.ds(row0 + at_row % per_dest, step)] = block[
                    piece * step : (piece + 1) * step
                ]
        for k in range(ctx_count):
            b0 = k * per_dest // 128
            lse_lines = [lse[:, (b0 + i) * 128 : (b0 + i + 1) * 128] for i in range(lines)]
            outs[k][pl.ds(row0 + per_dest, TAIL)] = terms(lse_lines)

    if run_window is not None:
        tile = terms(run_window())
        for out in outs:
            out[pl.ds(count_here * out_rows, TAIL)] = tile

    pltpu.make_async_copy(q_buf, q_buf, q_sem.at[0]).wait()

    def empty(at):
        for out in outs:
            row0 = pl.multiple_of(at * out_rows, TAIL)
            out[pl.ds(row0, per_dest)] = jnp.zeros((per_dest, HD), jnp.bfloat16)
            out[pl.ds(row0 + per_dest, TAIL)] = terms(
                [jnp.full((1, HD), FILL, jnp.float32)] * max(1, per_dest // 128)
            )

    @pl.loop(0, count_here)
    def _(at):
        active = (note[at, 1] > 0) | is_last
        pl.when(active)(functools.partial(attend, at))
        pl.when(jnp.logical_not(active))(functools.partial(empty, at))


def decode(head0, n, ctx_count, row_count, keep, order, q, keys, values, own_k, own_v, after, pieces):
    rows_total, heads, per_row, _ = q.shape
    local_rows = rows_total // row_count
    queries = local_rows * per_row
    chunk = min(256, queries)
    per_dest = queries // ctx_count
    here = keys.shape[0] // STRETCH
    extra = pl.cdiv(own_k.shape[0] + W, HD) * HD
    slots = n * here
    any_space = pl.BlockSpec(memory_space=pl.ANY)
    vmem = pl.BlockSpec(memory_space=pltpu.VMEM)
    score_heads = heads // row_count
    window_queries = W * GROUP
    window_outs, window_scratch = [], []
    if pieces:
        per_block = math.gcd(here, 8)
        blocks = score_heads * here // per_block
        window_outs = [jax.ShapeDtypeStruct((score_heads, here, 8, window_queries), jnp.float32)]
        window_scratch = [
            pltpu.VMEM((score_heads, window_queries), jnp.float32),
            pltpu.VMEM((score_heads, ctx_count, window_queries // ctx_count, HD), jnp.bfloat16),
            pltpu.VMEM((blocks, per_block * STRETCH, HD), jnp.bfloat16),
            pltpu.VMEM((2, 2 * STRETCH, window_queries), jnp.float32),
            pltpu.SMEM((1,), jnp.int32),
            pltpu.SemaphoreType.DMA((ctx_count, score_heads)),
            pltpu.SemaphoreType.DMA((blocks,)),
        ]
    spare = TAIL if pieces else 0
    return pl.pallas_call(
        functools.partial(decode_kernel, head0, n, ctx_count, row_count),
        out_shape=[jax.ShapeDtypeStruct((n * (per_dest + TAIL) + spare, HD), jnp.bfloat16)] * ctx_count
        + window_outs,
        grid_spec=pltpu.PrefetchScalarGridSpec(
            num_scalar_prefetch=2,
            grid=(),
            in_specs=[any_space] * (6 + len(pieces)),
            out_specs=[vmem] * (ctx_count + len(window_outs)),
            scratch_shapes=[
                pltpu.VMEM((1 if n == 1 else heads, local_rows, per_row, HD), jnp.bfloat16),
                pltpu.VMEM((slots, STRETCH, HD), jnp.bfloat16),
                pltpu.VMEM((slots, STRETCH, HD), jnp.bfloat16),
                pltpu.VMEM((extra, HD), jnp.bfloat16),
                pltpu.VMEM((extra, HD), jnp.bfloat16),
                pltpu.VMEM((1, queries), jnp.float32),
                pltpu.VMEM((8, queries), jnp.float32),
                pltpu.VMEM((HD, queries), jnp.float32),
                pltpu.VMEM((2, 2 * STRETCH, chunk), jnp.float32),
                pltpu.SMEM((n, 2), jnp.int32),
                pltpu.SemaphoreType.DMA((1,)),
                pltpu.SemaphoreType.DMA((slots,)),
                pltpu.SemaphoreType.DMA((slots,)),
                pltpu.SemaphoreType.DMA((4,)),
            ]
            + window_scratch,
        ),
        cost_estimate=pl.CostEstimate(
            flops=n * 8 * queries * STRETCH * HD * 4,
            bytes_accessed=n * 8 * STRETCH * HD * 4,
            transcendentals=n * 8 * queries * STRETCH,
        ),
        name="decode",
    )(keep, order, q, keys, values, own_k, own_v, after, *pieces)


def combine_kernel(head0, n, ctx_count, heads, here, score_heads, keep_ref, *refs):
    parts = refs[:ctx_count]
    if head0:
        share_ref, _, score_ref, out_ref, buf, sem = refs[ctx_count:]
    else:
        sum_ref, own_ref, share_ref, kept_ref, out_ref, buf, sem = refs[ctx_count:]
    per_row = out_ref.shape[2]
    order = head_order(keep_ref, here)
    per_dest = buf.shape[1] * per_row
    step = min(128, per_dest)
    lines = max(1, per_dest // 128)
    copies = []
    for at in range(n):
        row0 = at * (per_dest + TAIL)
        tiles = [part[pl.ds(row0 + per_dest, TAIL)].astype(jnp.float32) for part in parts]
        for b in range(per_dest // step):
            lses = [line_of(tile, lines, b) for tile in tiles]
            if step == 128:
                top = functools.reduce(jnp.maximum, lses)
                weights = [jnp.exp2(x - top) for x in lses]
                inverse = 1.0 / functools.reduce(jnp.add, weights)
                shares = [jnp.broadcast_to(x * inverse, (128, HD)).T for x in weights]
            else:
                turned_lses = [
                    jnp.broadcast_to(x, (128, HD)).T[k * per_dest % 128 : k * per_dest % 128 + step]
                    for k, x in enumerate(lses)
                ]
                top = functools.reduce(jnp.maximum, turned_lses)
                weights = [jnp.exp2(x - top) for x in turned_lses]
                inverse = 1.0 / functools.reduce(jnp.add, weights)
                shares = [x * inverse for x in weights]
            total = None
            for part, share in zip(parts, shares):
                term = part[pl.ds(row0 + b * step, step)].astype(jnp.float32) * share
                total = term if total is None else total + term
            rows = step // per_row
            buf[at, pl.ds(b * rows, rows)] = total.reshape(rows, per_row, HD).astype(jnp.bfloat16)
        copies.append(pltpu.make_async_copy(buf.at[at], out_ref.at[:, order[head0 + at]], sem.at[at]))
        copies[-1].start()
    if head0:
        tiles = [part[pl.ds(part.shape[0] - TAIL, TAIL)].astype(jnp.float32) for part in parts]
        queries = share_ref.shape[2]
        count = queries // 128
        for g in range(score_heads):
            lses = [
                jnp.concatenate(
                    [line_of(tile, score_heads * count, g * count + i) for i in range(count)], axis=1
                )
                for tile in tiles
            ]
            top = functools.reduce(jnp.maximum, lses)
            whole = functools.reduce(jnp.add, [jnp.exp2(x - top) for x in lses])
            shares = share_ref[g] * (jnp.exp2(lses[0] - top) / whole)
            column = jnp.sum(shares, axis=1, keepdims=True)
            eye = lax.broadcasted_iota(jnp.int32, (here, here), 0) == lax.broadcasted_iota(
                jnp.int32, (here, here), 1
            )
            score_ref[pl.ds(g, 1)] = jnp.sum(jnp.where(eye, column, 0.0), axis=0, keepdims=True)
    else:
        kept_ref[...] = own_ref[...]
        for g in range(score_heads):
            sums = jnp.sum(sum_ref[g], axis=1)
            share_ref[g] = sums / jnp.sum(sums, axis=0, keepdims=True)
    for copy in copies:
        copy.wait()


def local(keys, values, window_q, keep_stretches, dec_q, dec_k, dec_v, row_order):
    ctx_count = lax.axis_size("ctx")
    row_count = lax.axis_size("rows")
    heads = keys.shape[1] // HD
    here = keys.shape[0] // STRETCH
    rows_total, steps = dec_q.shape[:2]
    score_heads = heads // row_count
    shifts = range(1, ctx_count)

    def shifted(x, k):
        pairs = [(i, int(partner(i, k, ctx_count))) for i in range(ctx_count)]
        return lax.ppermute(x, "ctx", pairs)

    def spread(parts):
        return [parts[0]] + [shifted(parts[k], k) for k in range(1, ctx_count)]

    w_each = window_q.shape[0]
    tiles = window_q.reshape(w_each, heads * GROUP, HD).transpose(1, 0, 2)
    tiles = tiles.reshape(heads * GROUP * w_each, HD)
    pieces = spread([tiles] * ctx_count)

    def rows_first(x):
        x = x.reshape(rows_total, steps, -1, HD).transpose(0, 2, 1, 3)
        return x.reshape(-1, HD)

    q = rows_first(dec_q).reshape(rows_total, heads, GROUP * steps, HD)
    own_k, own_v = rows_first(dec_k), rows_first(dec_v)

    def decoded_part(head0, n, after, pieces):
        return decode(
            head0,
            n,
            ctx_count,
            row_count,
            keep_stretches,
            row_order,
            q,
            keys,
            values,
            own_k,
            own_v,
            after,
            pieces,
        )

    many = heads - 1
    first, pieces = lax.optimization_barrier((decoded_part(0, many, row_order, []), pieces))
    first_parts = spread(first)
    *second, sums = decoded_part(many, 1, first_parts[0], pieces)
    second_parts = spread(second)

    rows_each = rows_total // (ctx_count * row_count)
    per_row = GROUP * steps
    vmem = pl.BlockSpec(memory_space=pltpu.VMEM)
    smem = pl.BlockSpec(memory_space=pltpu.SMEM)
    any_space = pl.BlockSpec(memory_space=pl.ANY)
    out_shape = jax.ShapeDtypeStruct((rows_each, heads, per_row, HD), jnp.bfloat16)

    def scratch(n):
        return [pltpu.VMEM((n, rows_each, per_row, HD), jnp.bfloat16), pltpu.SemaphoreType.DMA((n,))]

    shares, kept, begun = pl.pallas_call(
        functools.partial(combine_kernel, 0, many, ctx_count, heads, here, score_heads),
        out_shape=[
            jax.ShapeDtypeStruct((score_heads, here, W * GROUP), jnp.float32),
            jax.ShapeDtypeStruct(second[0].shape, second[0].dtype),
            out_shape,
        ],
        in_specs=[smem] + [vmem] * (ctx_count + 2),
        out_specs=[vmem, vmem, any_space],
        scratch_shapes=scratch(many),
        cost_estimate=pl.CostEstimate(flops=10**6, bytes_accessed=10**7, transcendentals=0),
        compiler_params=pltpu.CompilerParams(vmem_limit_bytes=8 * 2**20),
        name="combine_many",
    )(keep_stretches, *first_parts, sums, second_parts[0])
    stretch_scores, decoded = pl.pallas_call(
        functools.partial(combine_kernel, many, 1, ctx_count, heads, here, score_heads),
        out_shape=[jax.ShapeDtypeStruct((score_heads, here), jnp.float32), out_shape],
        in_specs=[smem] + [vmem] * (ctx_count + 1) + [any_space],
        out_specs=[vmem, any_space],
        scratch_shapes=scratch(1),
        input_output_aliases={ctx_count + 2: 1},
        compiler_params=pltpu.CompilerParams(vmem_limit_bytes=8 * 2**20),
        name="combine_one",
    )(keep_stretches, kept, *second_parts[1:], shares, begun)
    decoded = decoded.reshape(rows_each, heads * GROUP, steps, HD).transpose(0, 2, 1, 3)
    return (stretch_scores, decoded.reshape(rows_each, steps, heads * GROUP * HD))


def solution(mesh):
    placed = (
        P(("groups", "ctx"), "head"),
        P(("groups", "ctx"), "head"),
        P(("groups", "ctx"), "head"),
        P(("groups", "head"), None),
        P("groups", None, "head"),
        P("groups", None, "head"),
        P("groups", None, "head"),
        P("groups"),
    )
    return jax.shard_map(
        local,
        mesh=mesh,
        in_specs=placed,
        out_specs=(
            P(("groups", "head", "rows"), "ctx"),
            P(("groups", "ctx", "rows"), None, "head"),
        ),
        check_vma=False,
    )
```

```python
import functools
import math

import jax
import jax.numpy as jnp
from jax import lax
from jax.experimental import pallas as pl
from jax.experimental.pallas import tpu as pltpu
from jax.sharding import PartitionSpec as P

QH = 64
KVH = 8
HD = 128
STRETCH = 512
W = 32
GROUP = QH // KVH

FILL = -1.0e30
LIMIT = 1.0e30
SCALE2 = HD ** (-0.5) * math.log2(math.e)
NT = (((1,), (1,)), ((), ()))
TAIL = 16
BLOCK = 4
ONES = 16


def head_order(keep_ref, here):
    heads, keep_count = keep_ref.shape
    full = [keep_ref[h, keep_count // 2] // here for h in range(heads)]
    last = jnp.int32(0)
    best = jnp.int32(-1)
    for h in range(heads):
        same = sum((full[h] == other).astype(jnp.int32) for other in full)
        last = jnp.where(same > best, h, last)
        best = jnp.maximum(same, best)
    return [h + (last <= h).astype(jnp.int32) for h in range(heads - 1)] + [last]


def terms(lines):
    high = [x.astype(jnp.bfloat16).astype(jnp.float32) for x in lines]
    mid = [(x - y).astype(jnp.bfloat16).astype(jnp.float32) for x, y in zip(lines, high)]
    low = [x - y - z for x, y, z in zip(lines, high, mid)]
    spare = jnp.zeros((TAIL - 3 * len(lines), lines[0].shape[1]), jnp.float32)
    return jnp.concatenate(high + mid + low + [spare], axis=0).astype(jnp.bfloat16)


def line_of(tile, count, at):
    return tile[at : at + 1] + tile[count + at : count + at + 1] + tile[2 * count + at : 2 * count + at + 1]


def partner(own_index, k, ctx_count):
    assert ctx_count & (ctx_count - 1) == 0
    return own_index ^ k


def pick(options, at):
    value = options[-1]
    for i in range(len(options) - 2, -1, -1):
        value = jnp.where(at == i, options[i], value)
    return value


def window_part(pieces, k_hbm, sum_ref, scratch):
    m_ref, q_buf, k_buf, s_buf, flag, q_sem, k_sem = scratch
    ctx_count = len(pieces)
    score_heads = q_buf.shape[0]
    own_index = lax.axis_index("ctx")
    row_index = lax.axis_index("rows")
    is_last = own_index == ctx_count - 1
    per_block = k_buf.shape[1] // STRETCH
    span = k_buf.shape[1]
    blocks = k_hbm.shape[0] // span
    per_piece = q_buf.shape[2]
    queries = per_piece * ctx_count
    w_each = W // ctx_count

    def piece_copies():
        copies = []
        for k, piece in enumerate(pieces):
            source = partner(own_index, k, ctx_count) if k else own_index
            for g in range(score_heads):
                row0 = (row_index * score_heads + g) * per_piece
                rows = pl.ds(pl.multiple_of(row0, TAIL), per_piece)
                copies.append(
                    pltpu.make_async_copy(piece.at[rows], q_buf.at[g, source], q_sem.at[k, g])
                )
        return copies

    for copy in piece_copies():
        copy.start()
    for g in range(score_heads):
        cols = pl.ds(pl.multiple_of((row_index * score_heads + g) * HD, HD), HD)
        for b in range(blocks):
            pltpu.make_async_copy(
                k_hbm.at[pl.ds(b * span, span), cols], k_buf.at[g * blocks + b], k_sem.at[g * blocks + b]
            ).start()
    def run():
        for copy in piece_copies():
            copy.wait()

        def scores(g, keys):
            q = q_buf[g].reshape(queries, HD)
            return lax.dot_general(keys, q, NT, preferred_element_type=jnp.float32)

        row = lax.broadcasted_iota(jnp.int32, (W, queries), 0)
        col = lax.broadcasted_iota(jnp.int32, (W, queries), 1)
        w = (col // per_piece) * w_each + lax.rem(col, w_each)
        allowed = (row <= w) | jnp.logical_not(is_last)

        for g in range(score_heads):
            pltpu.make_async_copy(k_buf.at[g * blocks], k_buf.at[g * blocks], k_sem.at[g * blocks]).wait()
            s = scores(g, k_buf[g * blocks, pl.ds(0, 128)])
            m_ref[pl.ds(g, 1)] = jnp.max(s, axis=0, keepdims=True) * SCALE2
        flag[0] = jnp.int32(1)

        @pl.loop(0, 2)
        def _(attempt):
            @pl.when((attempt == 1) & (flag[0] > 0))
            def _():
                for g in range(score_heads):

                    @pl.loop(0, blocks * per_block)
                    def _(c):
                        keys = k_buf[g * blocks + c // per_block, pl.ds(lax.rem(c, per_block) * STRETCH, STRETCH)]
                        s = scores(g, keys)
                        tail = jnp.where(allowed | (c + 1 < blocks * per_block), s[STRETCH - W :], FILL)
                        s = jnp.concatenate([s[: STRETCH - W], tail], axis=0)
                        peak = jnp.max(s, axis=0, keepdims=True) * SCALE2
                        m_ref[pl.ds(g, 1)] = jnp.maximum(m_ref[pl.ds(g, 1)], peak)

            @pl.when(flag[0] > 0)
            def _():
                for g in range(score_heads):
                    s_buf[0] = scores(g, k_buf[g * blocks, pl.ds(0, 2 * STRETCH)])

                    @pl.loop(0, blocks)
                    def _(b):
                        more = b + 1 < blocks

                        @pl.when(more & (attempt == 0))
                        def _():
                            at = g * blocks + b + 1
                            pltpu.make_async_copy(k_buf.at[at], k_buf.at[at], k_sem.at[at]).wait()

                        following = g * blocks + jnp.where(more, b + 1, b)
                        m = m_ref[pl.ds(g, 1)]
                        for i in range(per_block // 2):
                            if i + 1 < per_block // 2:
                                keys = k_buf[g * blocks + b, pl.ds((i + 1) * 2 * STRETCH, 2 * STRETCH)]
                            else:
                                keys = k_buf[following, pl.ds(0, 2 * STRETCH)]
                            s_buf[(i + 1) % 2] = scores(g, keys)
                            for half in range(2):
                                s = s_buf[i % 2, pl.ds(half * STRETCH, STRETCH)]
                                if i == per_block // 2 - 1 and half == 1:
                                    tail = jnp.where(allowed | more, s[STRETCH - W :], FILL)
                                    s = jnp.concatenate([s[: STRETCH - W], tail], axis=0)
                                p = jnp.exp2(s * SCALE2 - m)
                                sum_ref[g, b * per_block + 2 * i + half] = jnp.sum(
                                    p.reshape(STRETCH // 8, 8, queries), axis=0
                                )

                worst = jnp.max(jnp.where(sum_ref[...] < LIMIT, 0.0, 1.0))
                flag[0] = (worst > 0.0).astype(jnp.int32)

        lines = []
        for g in range(score_heads):
            total = jnp.sum(jnp.sum(sum_ref[g], axis=0), axis=0, keepdims=True)
            lse = m_ref[pl.ds(g, 1)] + jnp.log2(total)
            lines += [lse[:, at : at + 128] for at in range(0, queries, 128)]
        return lines

    return run


def decode_kernel(
    head0,
    count_here,
    ctx_count,
    row_count,
    keep_ref,
    order_ref,
    q_hbm,
    k_hbm,
    v_hbm,
    own_k_hbm,
    own_v_hbm,
    after_ref,
    *rest,
):
    run_window = None
    if head0:
        pieces, rest = rest[:ctx_count], rest[ctx_count:]
        run_window = window_part(pieces, k_hbm, rest[ctx_count], rest[-7:])
        rest = rest[:ctx_count] + rest[ctx_count + 1 : -7]
    outs = rest[:ctx_count]
    (q_buf, k_buf, v_buf, kx_buf, vx_buf, m_ref, l_ref, acc_ref, s_buf, note, q_sem, k_sem, v_sem, x_sem) = rest[
        ctx_count:
    ]
    keep_count = keep_ref.shape[1]
    here = k_hbm.shape[0] // STRETCH
    own_index = lax.axis_index("ctx")
    row_index = lax.axis_index("rows")
    is_last = own_index == ctx_count - 1
    base = own_index * here
    rows_total, heads, per_row, _ = q_hbm.shape
    rows_each = rows_total // (ctx_count * row_count)
    local_rows = rows_each * ctx_count
    queries = local_rows * per_row
    chunk = min(256, queries)
    firsts = list(range(0, queries, chunk))
    own_keys = own_k_hbm.shape[0]
    steps = own_keys // (rows_total * heads)
    extra = kx_buf.shape[0]
    order = head_order(keep_ref, here)[head0 : head0 + count_here]
    per_dest = queries // ctx_count
    out_rows = per_dest + TAIL

    def row_at(j):
        k = j // rows_each
        i = lax.rem(j, rows_each)
        dest = partner(own_index, k, ctx_count)
        return order_ref[dest * (row_count * rows_each) + row_index * rows_each + i]

    all_heads = q_buf.shape[0] == heads

    @pl.loop(0, local_rows)
    def _(j):
        row = row_at(j)
        if all_heads:
            pltpu.make_async_copy(q_hbm.at[row], q_buf.at[:, j], q_sem.at[0]).start()
        else:
            pltpu.make_async_copy(q_hbm.at[row, order[0]], q_buf.at[0, j], q_sem.at[0]).start()

    for at in range(count_here):
        start = jnp.int32(0)
        count = jnp.int32(0)
        for i in range(keep_count):
            local = keep_ref[order[at], i] - base
            start = start + (local < 0).astype(jnp.int32)
            count = count + ((local >= 0) & (local < here)).astype(jnp.int32)
        note[at, 0] = start
        note[at, 1] = count

    def unit_copies(at, h, u):
        local = keep_ref[h, note[at, 0] + u] - base
        rows = pl.ds(pl.multiple_of(local * STRETCH, STRETCH), STRETCH)
        cols = pl.ds(pl.multiple_of(h * HD, HD), HD)
        slot = at * here + u
        return (
            pltpu.make_async_copy(k_hbm.at[rows, cols], k_buf.at[slot], k_sem.at[slot]),
            pltpu.make_async_copy(v_hbm.at[rows, cols], v_buf.at[slot], v_sem.at[slot]),
        )

    def wait_slot(buf, sem, slot):
        pltpu.make_async_copy(buf.at[slot], buf.at[slot], sem.at[slot]).wait()

    for at in range(count_here):

        @pl.loop(0, note[at, 1])
        def _(u):
            for copy in unit_copies(at, order[at], u):
                copy.start()

    def own_copies():
        return (
            pltpu.make_async_copy(own_k_hbm, kx_buf.at[pl.ds(0, own_keys)], x_sem.at[0]),
            pltpu.make_async_copy(own_v_hbm, vx_buf.at[pl.ds(0, own_keys)], x_sem.at[1]),
        )

    def tail_copies(h):
        tail = pl.ds(k_hbm.shape[0] - W, W)
        cols = pl.ds(pl.multiple_of(h * HD, HD), HD)
        return (
            pltpu.make_async_copy(k_hbm.at[tail, cols], kx_buf.at[pl.ds(own_keys, W)], x_sem.at[2]),
            pltpu.make_async_copy(v_hbm.at[tail, cols], vx_buf.at[pl.ds(own_keys, W)], x_sem.at[3]),
        )

    @pl.when(is_last)
    def _():
        spare = extra - own_keys - W
        kx_buf[pl.ds(own_keys + W, spare)] = jnp.zeros((spare, HD), jnp.bfloat16)
        vx_buf[pl.ds(own_keys + W, spare)] = jnp.zeros((spare, HD), jnp.bfloat16)
        for copy in own_copies():
            copy.start()
        for copy in own_copies():
            copy.wait()

    def turned(v):
        return jnp.concatenate([v.T, jnp.ones((ONES, v.shape[0]), jnp.bfloat16)], axis=0)

    def fold(sl, vt, s):
        old = m_ref[:, sl]
        new = jnp.maximum(old, jnp.max(s, axis=0, keepdims=True))
        alpha = jnp.exp2(old - new)
        t = jnp.dot(vt, jnp.exp2(s - new).astype(jnp.bfloat16), preferred_element_type=jnp.float32)
        l_ref[:, sl] = l_ref[:, sl] * alpha + t[HD : HD + 8]
        acc_ref[:, sl] = acc_ref[:, sl] * alpha + t[:HD]
        m_ref[:, sl] = new

    def attend(at):
        h = pick(order, at)
        count = note[at, 1]
        blocks = count // BLOCK
        slot0 = at * here

        @pl.when(is_last)
        def _():
            for copy in tail_copies(h):
                copy.start()

        slab = h if all_heads else 0

        def q_of(first):
            j0 = first // per_row
            return q_buf[slab, pl.ds(j0, chunk // per_row)].reshape(chunk, HD)

        def scores(keys, first):
            return lax.dot_general(keys, q_of(first), NT, preferred_element_type=jnp.float32)

        def block(buf, at_unit, size):
            return buf[pl.ds(slot0 + at_unit, size)].reshape(size * STRETCH, HD)

        def fast(sl, vt, s):
            p = jnp.exp2(s * SCALE2 - m_ref[:, sl]).astype(jnp.bfloat16)
            t = jnp.dot(vt, p, preferred_element_type=jnp.float32)
            l_ref[:, sl] += t[HD : HD + 8]
            acc_ref[:, sl] += t[:HD]

        l_ref[...] = jnp.zeros(l_ref.shape, jnp.float32)
        acc_ref[...] = jnp.zeros(acc_ref.shape, jnp.float32)

        @pl.when(count == 0)
        def _():
            m_ref[...] = jnp.full(m_ref.shape, FILL, jnp.float32)

        @pl.when(count > 0)
        def _():
            wait_slot(k_buf, k_sem, slot0)
            for first in firsts:
                s = scores(k_buf[slot0, pl.ds(0, 128)], first)
                m_ref[:, pl.ds(first, chunk)] = jnp.max(s, axis=0, keepdims=True) * SCALE2

        def span(size):
            return pl.ds(0, size * STRETCH)

        @pl.when(blocks > 0)
        def _():
            for i in range(1, BLOCK):
                wait_slot(k_buf, k_sem, slot0 + i)
            s_buf[0] = scores(block(k_buf, 0, BLOCK), firsts[0])

            @pl.loop(0, blocks)
            def _(b):
                more = b + 1 < blocks
                for i in range(BLOCK):
                    wait_slot(v_buf, v_sem, slot0 + BLOCK * b + i)

                @pl.when(more)
                def _():
                    for i in range(BLOCK):
                        wait_slot(k_buf, k_sem, slot0 + BLOCK * (b + 1) + i)

                following = jnp.where(more, b + 1, b)
                vt = turned(block(v_buf, BLOCK * b, BLOCK))
                for i, first in enumerate(firsts):
                    if i + 1 < len(firsts):
                        s_buf[(i + 1) % 2] = scores(block(k_buf, BLOCK * b, BLOCK), firsts[i + 1])
                    else:
                        s_buf[(i + 1) % 2] = scores(block(k_buf, BLOCK * following, BLOCK), firsts[0])
                    fast(pl.ds(first, chunk), vt, s_buf[i % 2])

        size = BLOCK // 2
        done = BLOCK * blocks
        while size:

            def single(size=size, done=done):
                for i in range(size):
                    if i:
                        wait_slot(k_buf, k_sem, slot0 + done + i)
                    else:
                        pl.when(done > 0)(lambda: wait_slot(k_buf, k_sem, slot0 + done))
                    wait_slot(v_buf, v_sem, slot0 + done + i)
                vt = turned(block(v_buf, done, size))
                s_buf[0, span(size)] = scores(block(k_buf, done, size), firsts[0])
                for i, first in enumerate(firsts):
                    if i + 1 < len(firsts):
                        s_buf[(i + 1) % 2, span(size)] = scores(block(k_buf, done, size), firsts[i + 1])
                    fast(pl.ds(first, chunk), vt, s_buf[i % 2, span(size)])

            left = count - done >= size
            pl.when(left)(single)
            done = done + jnp.where(left, size, 0)
            size //= 2

        bad = jnp.max(jnp.where(l_ref[...] < LIMIT, 0.0, 1.0))

        @pl.when(bad > 0.0)
        def _():
            l_ref[...] = jnp.zeros(l_ref.shape, jnp.float32)
            acc_ref[...] = jnp.zeros(acc_ref.shape, jnp.float32)
            m_ref[...] = jnp.full(m_ref.shape, FILL, jnp.float32)

            @pl.loop(0, count)
            def _(u):
                vt = turned(v_buf[slot0 + u])
                for first in firsts:
                    fold(pl.ds(first, chunk), vt, scores(k_buf[slot0 + u], first) * SCALE2)

        @pl.when(is_last)
        def _():
            for copy in tail_copies(h):
                copy.wait()
            vt = turned(vx_buf[...])
            key = lax.broadcasted_iota(jnp.int32, (extra, chunk), 0)
            lane = lax.broadcasted_iota(jnp.int32, (1, chunk), 1)
            window = (key >= own_keys) & (key < own_keys + W)
            for first in firsts:
                line = jnp.zeros((1, chunk), jnp.int32)
                for j in range(chunk // per_row):
                    line = jnp.where(lane // per_row == j, row_at(first // per_row + j), line)
                low = line * (heads * steps) + h * steps
                high = low + lax.rem(lane, steps)
                mask = ((key >= low) & (key <= high)) | window
                s = scores(kx_buf[...], first) * SCALE2
                fold(pl.ds(first, chunk), vt, jnp.where(mask, s, FILL))

        total = l_ref[0:1]
        some = total > 0.0
        safe = jnp.where(some, total, 1.0)
        lse = jnp.where(some, m_ref[...] + jnp.log2(safe), FILL)
        inverse = 1.0 / safe
        lines = max(1, per_dest // 128)
        row0 = pl.multiple_of(at * out_rows, TAIL)
        for b in range(queries // 128):
            sl = slice(b * 128, (b + 1) * 128)
            block = (acc_ref[:, sl] * inverse[:, sl]).T.astype(jnp.bfloat16)
            step = min(128, per_dest)
            for piece in range(128 // step):
                at_row = b * 128 + piece * step
                outs[at_row // per_dest][pl.ds(row0 + at_row % per_dest, step)] = block[
                    piece * step : (piece + 1) * step
                ]
        for k in range(ctx_count):
            b0 = k * per_dest // 128
            lse_lines = [lse[:, (b0 + i) * 128 : (b0 + i + 1) * 128] for i in range(lines)]
            outs[k][pl.ds(row0 + per_dest, TAIL)] = terms(lse_lines)

    if run_window is not None:
        tile = terms(run_window())
        for out in outs:
            out[pl.ds(count_here * out_rows, TAIL)] = tile

    pltpu.make_async_copy(q_buf, q_buf, q_sem.at[0]).wait()

    def empty(at):
        for out in outs:
            row0 = pl.multiple_of(at * out_rows, TAIL)
            out[pl.ds(row0, per_dest)] = jnp.zeros((per_dest, HD), jnp.bfloat16)
            out[pl.ds(row0 + per_dest, TAIL)] = terms(
                [jnp.full((1, HD), FILL, jnp.float32)] * max(1, per_dest // 128)
            )

    @pl.loop(0, count_here)
    def _(at):
        active = (note[at, 1] > 0) | is_last
        pl.when(active)(functools.partial(attend, at))
        pl.when(jnp.logical_not(active))(functools.partial(empty, at))


def decode(head0, n, ctx_count, row_count, keep, order, q, keys, values, own_k, own_v, after, pieces):
    rows_total, heads, per_row, _ = q.shape
    local_rows = rows_total // row_count
    queries = local_rows * per_row
    chunk = min(256, queries)
    per_dest = queries // ctx_count
    here = keys.shape[0] // STRETCH
    extra = pl.cdiv(own_k.shape[0] + W, HD) * HD
    slots = n * here
    any_space = pl.BlockSpec(memory_space=pl.ANY)
    vmem = pl.BlockSpec(memory_space=pltpu.VMEM)
    score_heads = heads // row_count
    window_queries = W * GROUP
    window_outs, window_scratch = [], []
    if pieces:
        per_block = math.gcd(here, 8)
        blocks = score_heads * here // per_block
        window_outs = [jax.ShapeDtypeStruct((score_heads, here, 8, window_queries), jnp.float32)]
        window_scratch = [
            pltpu.VMEM((score_heads, window_queries), jnp.float32),
            pltpu.VMEM((score_heads, ctx_count, window_queries // ctx_count, HD), jnp.bfloat16),
            pltpu.VMEM((blocks, per_block * STRETCH, HD), jnp.bfloat16),
            pltpu.VMEM((2, 2 * STRETCH, window_queries), jnp.float32),
            pltpu.SMEM((1,), jnp.int32),
            pltpu.SemaphoreType.DMA((ctx_count, score_heads)),
            pltpu.SemaphoreType.DMA((blocks,)),
        ]
    spare = TAIL if pieces else 0
    return pl.pallas_call(
        functools.partial(decode_kernel, head0, n, ctx_count, row_count),
        out_shape=[jax.ShapeDtypeStruct((n * (per_dest + TAIL) + spare, HD), jnp.bfloat16)] * ctx_count
        + window_outs,
        grid_spec=pltpu.PrefetchScalarGridSpec(
            num_scalar_prefetch=2,
            grid=(),
            in_specs=[any_space] * (6 + len(pieces)),
            out_specs=[vmem] * (ctx_count + len(window_outs)),
            scratch_shapes=[
                pltpu.VMEM((1 if n == 1 else heads, local_rows, per_row, HD), jnp.bfloat16),
                pltpu.VMEM((slots, STRETCH, HD), jnp.bfloat16),
                pltpu.VMEM((slots, STRETCH, HD), jnp.bfloat16),
                pltpu.VMEM((extra, HD), jnp.bfloat16),
                pltpu.VMEM((extra, HD), jnp.bfloat16),
                pltpu.VMEM((1, queries), jnp.float32),
                pltpu.VMEM((8, queries), jnp.float32),
                pltpu.VMEM((HD, queries), jnp.float32),
                pltpu.VMEM((2, BLOCK * STRETCH, chunk), jnp.float32),
                pltpu.SMEM((n, 2), jnp.int32),
                pltpu.SemaphoreType.DMA((1,)),
                pltpu.SemaphoreType.DMA((slots,)),
                pltpu.SemaphoreType.DMA((slots,)),
                pltpu.SemaphoreType.DMA((4,)),
            ]
            + window_scratch,
        ),
        cost_estimate=pl.CostEstimate(
            flops=n * 8 * queries * STRETCH * HD * 4,
            bytes_accessed=n * 8 * STRETCH * HD * 4,
            transcendentals=n * 8 * queries * STRETCH,
        ),
        name="decode",
    )(keep, order, q, keys, values, own_k, own_v, after, *pieces)


def combine_kernel(head0, n, ctx_count, heads, here, score_heads, keep_ref, *refs):
    parts = refs[:ctx_count]
    if head0:
        share_ref, _, score_ref, out_ref, buf, sem = refs[ctx_count:]
    else:
        sum_ref, own_ref, share_ref, kept_ref, out_ref, buf, sem = refs[ctx_count:]
    per_row = out_ref.shape[2]
    order = head_order(keep_ref, here)
    per_dest = buf.shape[1] * per_row
    step = min(128, per_dest)
    lines = max(1, per_dest // 128)
    copies = []
    for at in range(n):
        row0 = at * (per_dest + TAIL)
        tiles = [part[pl.ds(row0 + per_dest, TAIL)].astype(jnp.float32) for part in parts]
        for b in range(per_dest // step):
            lses = [line_of(tile, lines, b) for tile in tiles]
            if step == 128:
                top = functools.reduce(jnp.maximum, lses)
                weights = [jnp.exp2(x - top) for x in lses]
                inverse = 1.0 / functools.reduce(jnp.add, weights)
                shares = [jnp.broadcast_to(x * inverse, (128, HD)).T for x in weights]
            else:
                turned_lses = [
                    jnp.broadcast_to(x, (128, HD)).T[k * per_dest % 128 : k * per_dest % 128 + step]
                    for k, x in enumerate(lses)
                ]
                top = functools.reduce(jnp.maximum, turned_lses)
                weights = [jnp.exp2(x - top) for x in turned_lses]
                inverse = 1.0 / functools.reduce(jnp.add, weights)
                shares = [x * inverse for x in weights]
            total = None
            for part, share in zip(parts, shares):
                term = part[pl.ds(row0 + b * step, step)].astype(jnp.float32) * share
                total = term if total is None else total + term
            rows = step // per_row
            buf[at, pl.ds(b * rows, rows)] = total.reshape(rows, per_row, HD).astype(jnp.bfloat16)
        copies.append(pltpu.make_async_copy(buf.at[at], out_ref.at[:, order[head0 + at]], sem.at[at]))
        copies[-1].start()
    if head0:
        tiles = [part[pl.ds(part.shape[0] - TAIL, TAIL)].astype(jnp.float32) for part in parts]
        queries = share_ref.shape[2]
        count = queries // 128
        for g in range(score_heads):
            lses = [
                jnp.concatenate(
                    [line_of(tile, score_heads * count, g * count + i) for i in range(count)], axis=1
                )
                for tile in tiles
            ]
            top = functools.reduce(jnp.maximum, lses)
            whole = functools.reduce(jnp.add, [jnp.exp2(x - top) for x in lses])
            shares = share_ref[g] * (jnp.exp2(lses[0] - top) / whole)
            column = jnp.sum(shares, axis=1, keepdims=True)
            eye = lax.broadcasted_iota(jnp.int32, (here, here), 0) == lax.broadcasted_iota(
                jnp.int32, (here, here), 1
            )
            score_ref[pl.ds(g, 1)] = jnp.sum(jnp.where(eye, column, 0.0), axis=0, keepdims=True)
    else:
        kept_ref[...] = own_ref[...]
        for g in range(score_heads):
            sums = jnp.sum(sum_ref[g], axis=1)
            share_ref[g] = sums / jnp.sum(sums, axis=0, keepdims=True)
    for copy in copies:
        copy.wait()


def local(keys, values, window_q, keep_stretches, dec_q, dec_k, dec_v, row_order):
    ctx_count = lax.axis_size("ctx")
    row_count = lax.axis_size("rows")
    heads = keys.shape[1] // HD
    here = keys.shape[0] // STRETCH
    rows_total, steps = dec_q.shape[:2]
    score_heads = heads // row_count
    shifts = range(1, ctx_count)

    def shifted(x, k):
        pairs = [(i, int(partner(i, k, ctx_count))) for i in range(ctx_count)]
        return lax.ppermute(x, "ctx", pairs)

    def spread(parts):
        return [parts[0]] + [shifted(parts[k], k) for k in range(1, ctx_count)]

    w_each = window_q.shape[0]
    tiles = window_q.reshape(w_each, heads * GROUP, HD).transpose(1, 0, 2)
    tiles = tiles.reshape(heads * GROUP * w_each, HD)
    pieces = spread([tiles] * ctx_count)

    def rows_first(x):
        x = x.reshape(rows_total, steps, -1, HD).transpose(0, 2, 1, 3)
        return x.reshape(-1, HD)

    q = rows_first(dec_q).reshape(rows_total, heads, GROUP * steps, HD)
    own_k, own_v = rows_first(dec_k), rows_first(dec_v)

    def decoded_part(head0, n, after, pieces):
        return decode(
            head0,
            n,
            ctx_count,
            row_count,
            keep_stretches,
            row_order,
            q,
            keys,
            values,
            own_k,
            own_v,
            after,
            pieces,
        )

    many = heads - 1
    first, pieces = lax.optimization_barrier((decoded_part(0, many, row_order, []), pieces))
    first_parts = spread(first)
    *second, sums = decoded_part(many, 1, first_parts[0], pieces)
    second_parts = spread(second)

    rows_each = rows_total // (ctx_count * row_count)
    per_row = GROUP * steps
    vmem = pl.BlockSpec(memory_space=pltpu.VMEM)
    smem = pl.BlockSpec(memory_space=pltpu.SMEM)
    any_space = pl.BlockSpec(memory_space=pl.ANY)
    out_shape = jax.ShapeDtypeStruct((rows_each, heads, per_row, HD), jnp.bfloat16)

    def scratch(n):
        return [pltpu.VMEM((n, rows_each, per_row, HD), jnp.bfloat16), pltpu.SemaphoreType.DMA((n,))]

    shares, kept, begun = pl.pallas_call(
        functools.partial(combine_kernel, 0, many, ctx_count, heads, here, score_heads),
        out_shape=[
            jax.ShapeDtypeStruct((score_heads, here, W * GROUP), jnp.float32),
            jax.ShapeDtypeStruct(second[0].shape, second[0].dtype),
            out_shape,
        ],
        in_specs=[smem] + [vmem] * (ctx_count + 2),
        out_specs=[vmem, vmem, any_space],
        scratch_shapes=scratch(many),
        cost_estimate=pl.CostEstimate(flops=10**6, bytes_accessed=10**7, transcendentals=0),
        compiler_params=pltpu.CompilerParams(vmem_limit_bytes=8 * 2**20),
        name="combine_many",
    )(keep_stretches, *first_parts, sums, second_parts[0])
    stretch_scores, decoded = pl.pallas_call(
        functools.partial(combine_kernel, many, 1, ctx_count, heads, here, score_heads),
        out_shape=[jax.ShapeDtypeStruct((score_heads, here), jnp.float32), out_shape],
        in_specs=[smem] + [vmem] * (ctx_count + 1) + [any_space],
        out_specs=[vmem, any_space],
        scratch_shapes=scratch(1),
        input_output_aliases={ctx_count + 2: 1},
        compiler_params=pltpu.CompilerParams(vmem_limit_bytes=8 * 2**20),
        name="combine_one",
    )(keep_stretches, kept, *second_parts[1:], shares, begun)
    decoded = decoded.reshape(rows_each, heads * GROUP, steps, HD).transpose(0, 2, 1, 3)
    return (stretch_scores, decoded.reshape(rows_each, steps, heads * GROUP * HD))


def solution(mesh):
    placed = (
        P(("groups", "ctx"), "head"),
        P(("groups", "ctx"), "head"),
        P(("groups", "ctx"), "head"),
        P(("groups", "head"), None),
        P("groups", None, "head"),
        P("groups", None, "head"),
        P("groups", None, "head"),
        P("groups"),
    )
    return jax.shard_map(
        local,
        mesh=mesh,
        in_specs=placed,
        out_specs=(
            P(("groups", "head", "rows"), "ctx"),
            P(("groups", "ctx", "rows"), None, "head"),
        ),
        check_vma=False,
    )
```
